32 devices in a mesh: gz: 2 (over x), gy: 4 (over y, core), gx: 4 (over z).
Axes of the slice: x: 2, y: 2, z: 4, core: 2. Of those that a mesh axis runs over, the one named last changes fastest.
Arguments:
- pressure: float32 [8, 512, 512], P('gz', 'gy', 'gx'), may hold values from -6 to 6
- light: float32 [4, 3], replicated, may hold values from -4 to 4
- palette: float32 [3, 2], replicated, may hold values from -4 to 4
- rate: float32 [4], replicated, may hold values from 0.0625 to 0.375
- shear: int32 [4, 8, 2], replicated, may hold values from 0 to 8
- offset: int32 [4, 2, 2], replicated, may hold values from 0 to 31
- order: int32 [4, 2], replicated, may hold values from 0 to 1, each once within a row
Outputs:
- picture: float32 [4, 4, 2, 256, 512], P(None, None, 'gz', 'gy', 'gx')
The draws below stay inside these ranges and needn't reach their ends.
Inputs may be any that keep to these rules, and one draw needn't show every extreme that they name: `order`: each row is a permutation of 0 to 1.
All inputs are finite; a program needn't handle non-finite values.
Results may differ from the reference program's by a relative error of at most 0.00005.
Values sent between devices are 32-bit elements; how exact they have to be, the bound alone decides.
A program may use at most 64 MiB of HBM per device.

```python
import math
import jax
import jax.numpy as jnp
from jax import lax

BZ = 4
VIEWS = 4
SHEAR = 8
REACH = 32
NBRICK = 2
NZ = 8
NY = 512
NX = 512
ROWS = 64
N_GY = 4


def draw_shear(key, part):
    drawn = jax.random.randint(jax.random.fold_in(key, 11), (VIEWS, NZ, 2), 0, SHEAR + 1)
    picked = jax.random.randint(jax.random.fold_in(key, 12), (VIEWS,), 0, NZ)
    marked = (jnp.arange(NZ, dtype=jnp.int32)[None, :] == picked[:, None])[:, :, None]
    return jnp.where(marked, SHEAR, drawn).astype(jnp.int32)


def draw_offset(key, part):
    drawn = jax.random.randint(jax.random.fold_in(key, 21), (VIEWS, NBRICK, 2), 0, REACH)
    picked = jax.random.randint(jax.random.fold_in(key, 22), (VIEWS,), 0, NBRICK)
    marked = (jnp.arange(NBRICK, dtype=jnp.int32)[None, :] == picked[:, None])[:, :, None]
    return jnp.where(marked, REACH - 1, drawn).astype(jnp.int32)


def block_levels(own_key, shape, split, low, high):
    def one(axis_at, shards_of):
        steps = jax.random.uniform(jax.random.fold_in(jax.random.fold_in(own_key, 6), axis_at), (shards_of,), jnp.float32, low / len(split), high / len(split))
        return jnp.repeat(jnp.exp(steps), shape[axis_at] // shards_of).reshape((-1,) + (1,) * (len(shape) - axis_at - 1))

    factor_of = one(*split[0])
    for cut in split[1:]:
        factor_of = factor_of * one(*cut)
    return factor_of


def bell_draw(stream_key, extent, spread, limit, split=(), kind=jnp.bfloat16):
    gain = block_levels(stream_key, extent, split, -0.22, 0.18) if split else 1.0
    result = jax.random.normal(stream_key, extent, jnp.float32) * spread * gain
    return jnp.minimum(jnp.maximum(result, -limit), limit).astype(kind)


def setup_inputs(seed: int = 0) -> dict:
    seeds = jax.random.split(jax.random.key(seed), 8)
    pressure = bell_draw(seeds[0], (NZ, NY, NX), 1.0, 6.0, ((0, 2), (1, 4), (2, 4)), jnp.float32)
    light = bell_draw(seeds[1], (VIEWS, 3), 1.0, 4.0, (), jnp.float32)
    palette = bell_draw(seeds[2], (3, 2), 1.0, 4.0, (), jnp.float32)
    rate = jnp.clip(jnp.exp(jax.random.uniform(seeds[3], (VIEWS,), jnp.float32, math.log(0.0625), math.log(0.375))), 0.0625, 0.375)
    shear = draw_shear(jax.random.fold_in(seeds[7], 71), 0)
    offset = draw_offset(jax.random.fold_in(seeds[7], 71), 0)
    order = jax.vmap(lambda own: jax.random.permutation(own, NBRICK))(jax.random.split(seeds[6], VIEWS)).reshape((VIEWS, NBRICK)).astype(jnp.int32)
    return dict(pressure=pressure, light=light, palette=palette, rate=rate, shear=shear, offset=offset, order=order)


def surface_terms(slab):
    inner = slab[1:-1, 1:-1, 1:-1]
    grad_depth = 0.5 * (slab[2:, 1:-1, 1:-1] - slab[:-2, 1:-1, 1:-1])
    grad_rows = 0.5 * (slab[1:-1, 2:, 1:-1] - slab[1:-1, :-2, 1:-1])
    grad_cols = 0.5 * (slab[1:-1, 1:-1, 2:] - slab[1:-1, 1:-1, :-2])
    factor = lax.rsqrt(grad_depth * grad_depth + grad_rows * grad_rows + grad_cols * grad_cols + 1.0)
    return (inner, (grad_depth * factor, grad_rows * factor, grad_cols * factor))

def render_layers(inner, normals, shifts, light, palette, rate, rows, cols):
    lengths = jnp.sqrt(lax.optimization_barrier(jnp.sum(light * light, axis=1, keepdims=True)) + 1.0)
    towards = light / lengths
    offsets = palette[:, 0][:, None, None]
    slopes = palette[:, 1][:, None, None]
    layers = []
    for view in range(light.shape[0]):

        def advance(carry, items):
            color, depth = carry
            value_slab, normal_depth, normal_rows, normal_cols, moved = items
            start = (SHEAR - moved[0], SHEAR - moved[1])
            value = lax.dynamic_slice(value_slab, start, (rows, cols))
            dot = lax.dynamic_slice(normal_depth, start, (rows, cols)) * towards[view, 0] + lax.dynamic_slice(normal_rows, start, (rows, cols)) * towards[view, 1] + lax.dynamic_slice(normal_cols, start, (rows, cols)) * towards[view, 2]
            shade = 0.25 + 0.75 * dot * dot
            density = rate[view] * (1.0 + jnp.tanh(value))
            alpha = 1.0 - jnp.exp(-density)
            weight = alpha * jnp.exp(-depth)
            hues = jax.nn.sigmoid(offsets + slopes * value[None]) * shade[None]
            return ((color + hues * weight[None], depth + density), None)
        start_carry = (jnp.zeros((3, rows, cols), jnp.float32), jnp.zeros((rows, cols), jnp.float32))
        (color, depth), _ = lax.scan(advance, start_carry, (inner, normals[0], normals[1], normals[2], shifts[view]))
        layers.append(jnp.concatenate([color, depth[None]], axis=0))
    return jnp.stack(layers)

def precedence(order):
    bricks = order.shape[1]
    onehot = (order[:, :, None] == jnp.arange(bricks, dtype=jnp.int32)[None, None, :]).astype(jnp.float32)
    ranks = lax.optimization_barrier(jnp.sum(onehot * jnp.arange(bricks, dtype=jnp.float32)[None, :, None], axis=1))
    return (ranks[:, None, :] < ranks[:, :, None]).astype(jnp.float32)

def place(layer, moved):
    padded = jnp.pad(layer, ((0, 0), (REACH, 0), (REACH, 0)))
    zero = jnp.zeros((), jnp.int32)
    return lax.dynamic_slice(padded, (zero, REACH - moved[0], REACH - moved[1]), layer.shape)

def reference(pressure, light, palette, rate, shear, offset, order):
    margin = SHEAR + 1
    rows = pressure.shape[1]
    cols = pressure.shape[2]
    padded = jnp.pad(pressure, ((1, 1), (margin, margin), (margin, margin)))

    def one_brick(brick):
        zero = jnp.zeros((), jnp.int32)
        slab = lax.dynamic_slice(padded, (brick * BZ, zero, zero), (BZ + 2, rows + 2 * margin, cols + 2 * margin))
        inner, normals = surface_terms(slab)
        shifts = lax.dynamic_slice(shear, (zero, brick * BZ, zero), (VIEWS, BZ, 2))
        layers = render_layers(inner, normals, shifts, light, palette, rate, rows, cols)
        moved = lax.dynamic_index_in_dim(offset, brick, 1, keepdims=False)
        return jnp.stack([place(layers[view], moved[view]) for view in range(VIEWS)])
    stacked = lax.map(one_brick, jnp.arange(NBRICK, dtype=jnp.int32))
    ranking = precedence(order)
    depths = stacked[:, :, 3]
    cover = jnp.einsum('vbc,cvyx->bvyx', ranking, depths, precision=lax.Precision.HIGHEST)
    colors = lax.optimization_barrier(jnp.sum(stacked[:, :, :3] * jnp.exp(-cover)[:, :, None], axis=0))
    opacity = 1.0 - jnp.exp(-lax.optimization_barrier(jnp.sum(depths, axis=0)))
    image = jnp.concatenate([colors, opacity[:, None]], axis=1)
    image = image.reshape(VIEWS, 4, N_GY, NBRICK, ROWS, NX)
    image = jnp.transpose(image, (0, 1, 3, 2, 4, 5))
    return image.reshape(VIEWS, 4, NBRICK, N_GY * ROWS, NX)
```

```python
import functools
import math

import jax
import jax.numpy as jnp
from jax import lax
from jax.experimental import pallas as pl
from jax.experimental.pallas import tpu as pltpu
from jax.sharding import PartitionSpec as P

VIEWS = 4
SHEAR = 8
REACH = 32
HALO = SHEAR + REACH
SUB = 8
LANES = 128
MESH = pl.DeviceIdType.MESH


def padded(cells, sides, width):
    for axis, dim in sides:
        count = lax.axis_size(axis)
        ends = count - 1
        head = lax.slice_in_dim(cells, 0, width, axis=dim)
        tail = lax.slice_in_dim(cells, cells.shape[dim] - width, cells.shape[dim], axis=dim)
        cells = jnp.concatenate(
            [
                lax.ppermute(tail, axis, [(i, (i + 1) % count) for i in range(ends)]),
                cells,
                lax.ppermute(head, axis, [((i + 1) % count, i) for i in range(ends)]),
            ],
            axis=dim,
        )
    return cells


def shifted(value, axis, steps):
    count = lax.axis_size(axis)
    first, last = (max(0, -steps), min(count, count - steps))
    return lax.ppermute(value, axis, [(source, source + steps) for source in range(first, last)])


def surface_terms(slab):
    inner = slab[1:-1, 1:-1, 1:-1]
    grad_depth = 0.5 * (slab[2:, 1:-1, 1:-1] - slab[:-2, 1:-1, 1:-1])
    grad_rows = 0.5 * (slab[1:-1, 2:, 1:-1] - slab[1:-1, :-2, 1:-1])
    grad_cols = 0.5 * (slab[1:-1, 1:-1, 2:] - slab[1:-1, 1:-1, :-2])
    factor = lax.rsqrt(
        grad_depth * grad_depth + grad_rows * grad_rows + grad_cols * grad_cols + 1.0
    )
    return (inner, (grad_depth * factor, grad_rows * factor, grad_cols * factor))


def render_layers(inner, normals, shifts, light, palette, rate, rows, cols):
    lengths = jnp.sqrt(jnp.sum(light * light, axis=1, keepdims=True) + 1.0)
    towards = light / lengths
    offsets = palette[:, 0][:, None, None]
    slopes = palette[:, 1][:, None, None]
    layers = []
    for view in range(light.shape[0]):

        def advance(carry, items):
            color, depth = carry
            value_slab, normal_depth, normal_rows, normal_cols, moved = items
            start = (SHEAR - moved[0], SHEAR - moved[1])
            value = lax.dynamic_slice(value_slab, start, (rows, cols))
            dot = (
                lax.dynamic_slice(normal_depth, start, (rows, cols)) * towards[view, 0]
                + lax.dynamic_slice(normal_rows, start, (rows, cols)) * towards[view, 1]
                + lax.dynamic_slice(normal_cols, start, (rows, cols)) * towards[view, 2]
            )
            shade = 0.25 + 0.75 * dot * dot
            density = rate[view] * (1.0 + jnp.tanh(value))
            alpha = 1.0 - jnp.exp(-density)
            weight = alpha * jnp.exp(-depth)
            hues = jax.nn.sigmoid(offsets + slopes * value[None]) * shade[None]
            return ((color + hues * weight[None], depth + density), None)

        start_carry = (
            jnp.zeros((3, rows, cols), jnp.float32),
            jnp.zeros((rows, cols), jnp.float32),
        )
        (color, depth), _ = lax.scan(
            advance, start_carry, (inner, normals[0], normals[1], normals[2], shifts[view])
        )
        layers.append(jnp.concatenate([color, depth[None]], axis=0))
    return jnp.stack(layers)


def precedence(order):
    bricks = order.shape[1]
    onehot = (order[:, :, None] == jnp.arange(bricks, dtype=jnp.int32)[None, None, :]).astype(
        jnp.float32
    )
    ranks = jnp.sum(onehot * jnp.arange(bricks, dtype=jnp.float32)[None, :, None], axis=1)
    return (ranks[:, None, :] < ranks[:, :, None]).astype(jnp.float32)


def many_bricks(pressure, light, palette, rate, shear, offset, order):
    depth_cells, rows, cols = pressure.shape
    brick = lax.axis_index("gz")
    zero = jnp.zeros((), jnp.int32)
    widened = padded(pressure, (("gy", 1), ("gx", 2)), SHEAR + 1)
    slab = padded(widened, (("gz", 0),), 1)
    inner, normals = surface_terms(slab)
    shifts = lax.dynamic_slice(shear, (zero, brick * depth_cells, zero), (VIEWS, depth_cells, 2))
    layers = render_layers(inner, normals, shifts, light, palette, rate, rows, cols)
    moved = lax.dynamic_index_in_dim(offset, brick, 1, keepdims=False)
    blank = jnp.zeros((4, rows + REACH, cols + REACH), jnp.float32)
    canvas = jnp.stack(
        [
            lax.dynamic_update_slice(blank, layers[view], (zero, moved[view, 0], moved[view, 1]))
            for view in range(VIEWS)
        ]
    )
    own_tile = canvas[:, :, :rows, :cols]
    from_above = shifted(canvas[:, :, rows:, :cols], "gy", 1)
    from_left = shifted(canvas[:, :, :rows, cols:], "gx", 1)
    from_diagonal = shifted(canvas[:, :, rows:, cols:], ("gy", "gx"), lax.axis_size("gx") + 1)
    from_diagonal = from_diagonal * (lax.axis_index("gx") > 0).astype(jnp.float32)
    own_tile = own_tile.at[:, :, :REACH, :].add(from_above)
    own_tile = own_tile.at[:, :, :, :REACH].add(from_left)
    own_tile = own_tile.at[:, :, :REACH, :REACH].add(from_diagonal)
    ranking = precedence(order)
    pieces = lax.all_to_all(own_tile[None], "gz", split_axis=3, concat_axis=0, tiled=True)
    depths = pieces[:, :, 3]
    cover = jnp.einsum("vbc,cvyx->bvyx", ranking, depths, precision=lax.Precision.HIGHEST)
    colors = jnp.sum(pieces[:, :, :3] * jnp.exp(-cover)[:, :, None], axis=0)
    opacity = 1.0 - jnp.exp(-jnp.sum(depths, axis=0))
    image = jnp.concatenate([colors, opacity[:, None]], axis=1)
    return image[:, :, None]


class Route:
    def __init__(self, dims, side, step, start, count, slab, half):
        bz = dims[2]
        self.side, self.step, self.half = side, step, half
        self.rows, self.slab = pl.ds(start, count), pl.ds(slab, count)
        self.groups = LANES // (SUB * bz)
        self.tiles = range(start // SUB, (start + count) // SUB)
        self.first = slab // SUB
        self.folds = range(
            self.tiles[0] // self.groups, self.tiles[-1] // self.groups + 1
        )
        self.size = (len(self.tiles) + len(self.folds)) * SUB
        self.base = self.sent = 0

    def there(self, y, ny):
        return y + self.step >= 0 if self.step < 0 else y + self.step < ny

    def comes(self, y, ny):
        return y - self.step < ny if self.step < 0 else y - self.step >= 0

    def wide(self, tile):
        return (tile - self.tiles[0]) * SUB

    def narrow(self, fold):
        return (len(self.tiles) + fold - self.folds[0]) * SUB


def routes_of(dims):
    rows = dims[3]
    strip = rows // 2
    routes = [
        Route(dims, 0, 0, 0, strip + SUB, HALO, 0),
        Route(dims, 0, 1, rows - HALO, HALO, 0, 1),
        Route(dims, 1, 0, strip - HALO, HALO + strip, 0, 0),
        Route(dims, 1, -1, 0, SUB, HALO + strip, 1),
    ]
    sent = 0
    for route in routes:
        route.sent = sent
        sent += route.size
    routes[1].base, routes[3].base = routes[0].size, routes[2].size
    return routes, sent, max(routes[0].size + routes[1].size, routes[2].size + routes[3].size)


MAIN, EDGE, BESIDE, COLS, ENDS, SLOTS = 0, 2, 4, 5, 9, 13


def exchange(
    dims, mine, here, p_ref, m_ref, cols_out, cols_in, ends_out, ends_in, sends, arrivals
):
    ny, nx, bz, rows = dims
    z, y, x = here
    has_left, has_right = x > 0, x < nx - 1
    routes = routes_of(dims)[0]

    def remote(src, dst, sent, arrival, who):
        return pltpu.make_async_remote_copy(
            src_ref=src,
            dst_ref=dst,
            send_sem=sends.at[sent],
            recv_sem=arrivals.at[arrival],
            device_id=who,
            device_id_type=MESH,
        )

    def part(brick, late):
        near = bz // 2 if late is None else bz - bz // 2
        if late is None:
            return 0, bz
        return (near, bz - near) if (brick == 1) == late else (0, near)

    def rows_of(brick, route, late):
        start, count = part(brick, late)
        slot = BESIDE if late is None else (EDGE if route.half else MAIN) + int(late)
        return remote(
            p_ref.at[pl.ds(start, count), route.rows],
            m_ref.at[pl.ds(1 + brick * bz + start, count), route.slab],
            slot, slot, (route.side, y + route.step, x),
        )

    def cols_of(brick, route):
        return remote(
            cols_out.at[pl.ds(route.sent, route.size)],
            cols_in.at[brick, pl.ds(route.base, route.size)],
            COLS + 2 * route.side + route.half, COLS + 2 * brick + route.half,
            (route.side, y + route.step, x + 1),
        )

    def ends_of(brick, route):
        return remote(
            ends_out,
            ends_in.at[brick, route.half],
            ENDS + 2 * route.side + route.half, ENDS + 2 * brick + route.half,
            (route.side, y + route.step, x - 1),
        )

    def both(a, b):
        return jnp.logical_and(a, b)

    def outgoing(same, kinds):
        for route in routes:
            if (route.side == mine) != same:
                continue
            there = route.there(y, ny)
            for kind in kinds:
                if kind == "cols":
                    yield both(there, has_right), cols_of(mine, route)
                elif kind == "ends":
                    yield both(there, has_left), ends_of(mine, route)
                elif not same:
                    yield there, rows_of(mine, route, kind == "late")
                elif route.half:
                    yield there, rows_of(mine, route, None)

    def incoming(brick, kinds):
        for route in routes:
            if route.side != mine:
                continue
            comes = route.comes(y, ny)
            for kind in kinds:
                if kind == "cols":
                    yield both(comes, has_left), cols_of(brick, route)
                elif kind == "ends":
                    yield both(comes, has_right), ends_of(brick, route)
                elif brick != mine:
                    yield comes, rows_of(brick, route, kind == "late")
                elif route.half:
                    yield comes, rows_of(brick, route, None)

    def apply(pairs, act):
        for there, copy in pairs:

            @pl.when(there)
            def _():
                act(copy)

    def send(same, *kinds):
        apply(outgoing(same, kinds), lambda copy: copy.start())

    def receive(brick, *kinds):
        apply(incoming(brick, kinds), lambda copy: copy.wait_recv())

    def close():
        apply(outgoing(True, ("early", "cols", "ends")), lambda copy: copy.wait_send())
        apply(outgoing(False, ("early", "late", "cols", "ends")), lambda copy: copy.wait_send())

    return send, receive, close


def partners_of(dims, here):
    ny, nx = dims[:2]
    z, y, x = here
    cross = 2 * z - 1
    for side, step in ((z, -1), (z, 0), (z, 1), (1 - z, 0), (1 - z, cross)):
        for over in (-1, 0, 1):
            if side is z and isinstance(step, int) and step == 0 and over == 0:
                continue
            there = jnp.logical_and(
                jnp.logical_and(y + step >= 0, y + step < ny),
                jnp.logical_and(x + over >= 0, x + over < nx),
            )
            yield there, (side, y + step, x + over)


def render(
    dims, light_in, palette_in, rate_in, shear_in, offset_in, order_in, p_ref, out_ref,
    light, palette, rate, shear, offset, order, tile_ref, m_ref, own_ref, cols_in, ends_in,
    cols_out, ends_out, h_ref, r_ref, dm, dh, back, sends, arrivals, local_sems, table_sems,
):
    ny, nx, bz, rows = dims
    strip = rows // 2
    tall = HALO + strip + SUB
    depth = 2 * bz
    blocks = (HALO + strip) // SUB
    wide_lanes = HALO - SUB
    z, y, x = lax.axis_index("gz"), lax.axis_index("gy"), lax.axis_index("gx")
    routes = routes_of(dims)[0]

    tables = [
        pltpu.make_async_copy(source, target, table_sems.at[i])
        for i, (source, target) in enumerate(
            (
                (light_in, light), (palette_in, palette), (rate_in, rate),
                (shear_in, shear), (offset_in, offset), (order_in, order),
            )
        )
    ]
    barrier = pltpu.get_barrier_semaphore()

    def sided(act):
        for mine in range(2):

            @pl.when(z == mine)
            def _():
                act(mine)

    count = 0
    for there, who in partners_of(dims, (z, y, x)):

        @pl.when(there)
        def _():
            pl.semaphore_signal(barrier, inc=1, device_id=who, device_id_type=MESH)

        count = count + there.astype(jnp.int32)

    steps = [
        exchange(
            dims, mine, (z, y, x), p_ref, m_ref, cols_out, cols_in, ends_out, ends_in,
            sends, arrivals,
        )
        for mine in range(2)
    ]

    def local_slab(mine):
        route = routes[2 * mine]
        return pltpu.make_async_copy(
            p_ref.at[:, route.rows], m_ref.at[pl.ds(1 + mine * bz, bz), route.slab],
            local_sems.at[1],
        )

    local_tile = pltpu.make_async_copy(p_ref, tile_ref, local_sems.at[0])
    local_tile.start()
    sided(lambda mine: local_slab(mine).start())
    for copy in tables:
        copy.start()

    empty = jnp.zeros((tall, LANES), jnp.float32)
    for ref in (m_ref, h_ref):
        ref[0] = empty
        ref[depth + 1] = empty

    def blank(mine):
        route = routes[2 * mine + 1]

        @pl.when(jnp.logical_not(route.comes(y, ny)))
        def _():
            m_ref[:, route.slab] = jnp.zeros((depth + 2, len(route.tiles) * SUB, LANES), jnp.float32)
            cols_in[:, route.base : route.base + route.size] = jnp.zeros(
                (2, route.size, LANES), jnp.float32
            )
            ends_in[:, 1] = jnp.zeros((2, SUB, LANES), jnp.float32)

    sided(blank)

    @pl.when(x == 0)
    def _():
        cols_in[...] = jnp.zeros(cols_in.shape, jnp.float32)

    @pl.when(x == nx - 1)
    def _():
        ends_in[...] = jnp.zeros(ends_in.shape, jnp.float32)

    lane = lax.broadcasted_iota(jnp.int32, (SUB, LANES), 1)
    last = lane == LANES - 1
    first = lane == 0
    groups = routes[0].groups
    tiles = rows // SUB

    def cell(j, t):
        return tile_ref[j, t * SUB : (t + 1) * SUB]

    def put(t_or_fold, is_wide, value):
        for route in routes:
            if t_or_fold in (route.tiles if is_wide else route.folds):
                at = route.sent + (route.wide if is_wide else route.narrow)(t_or_fold)
                cols_out[at : at + SUB] = value

    def merged(pieces):
        while len(pieces) > 1:
            pieces = [
                (a[0], jnp.where(lane >= b[0], b[1], a[1]))
                for a, b in zip(pieces[::2], pieces[1::2])
            ] + (pieces[-1:] if len(pieces) % 2 else [])
        return pieces[0][1]

    def turned(value, by):
        return pltpu.roll(value, by % LANES, 1) if by % LANES else value

    local_tile.wait()
    for t in range(tiles):
        put(
            t, True,
            merged(
                [(wide_lanes * j, turned(cell(j, t), wide_lanes * (j + 1))) for j in range(bz)]
            ),
        )
    for fold in range(tiles // groups):
        put(
            fold, False,
            merged(
                [
                    (
                        SUB * (bz * g + j),
                        turned(cell(j, fold * groups + g), SUB * (bz * g + j) + HALO),
                    )
                    for g in range(groups)
                    for j in range(bz)
                ]
            ),
        )
    ends_out[...] = merged(
        [(t * bz + j, turned(cell(j, t), t * bz + j)) for t in range(tiles) for j in range(bz)]
    )

    def unpack(mine, brick):
        for route in routes[2 * mine : 2 * mine + 2]:
            for t in route.tiles:
                row = (route.first + t - route.tiles[0]) * SUB
                at = route.base + route.wide(t)
                wide = cols_in[brick, at : at + SUB]
                at = route.base + route.narrow(t // groups)
                narrow = cols_in[brick, at : at + SUB]
                for j in range(bz):
                    h_ref[1 + brick * bz + j, row : row + SUB] = jnp.where(
                        lane >= LANES - wide_lanes,
                        turned(wide, -wide_lanes * (j + 1)),
                        turned(narrow, -SUB * (bz * (t % groups) + j) - HALO),
                    )
                r_ref[brick, row : row + SUB] = turned(
                    ends_in[brick, route.half], LANES - 1 - t * bz
                )

    pl.semaphore_wait(barrier, count)

    def opening(mine):
        send, receive, close = steps[mine]
        send(False, "early", "cols", "ends")
        send(True, "early", "cols", "ends")
        local_slab(mine).wait()
        receive(mine, "early", "cols", "ends")
        send(False, "late")
        own_ref[...] = m_ref[1 + mine * bz : 1 + (mine + 1) * bz]
        unpack(mine, mine)

    def middle(mine):
        send, receive, close = steps[mine]
        receive(1 - mine, "early", "cols", "ends")
        unpack(mine, 1 - mine)

    def ending(mine):
        send, receive, close = steps[mine]
        receive(1 - mine, "late")

    sided(opening)
    for copy in tables:
        copy.wait()

    towards = []
    for w in range(VIEWS):
        a, b, c = light[w, 0], light[w, 1], light[w, 2]
        inverse = lax.rsqrt(jnp.full((SUB, LANES), a * a + b * b + c * c + 1.0, jnp.float32))
        towards.append((a * inverse, b * inverse, c * inverse))

    def slopes(k, carry):
        for i in range(blocks):
            top = i * SUB
            here = m_ref[k + 1, top + 1 : top + 1 + SUB]
            side = h_ref[k + 1, top + 1 : top + 1 + SUB]
            beyond = pltpu.roll(
                r_ref[k // bz, top + 1 : top + 1 + SUB], (LANES - k % bz) % LANES, 1
            )
            here_r, here_l = pltpu.roll(here, LANES - 1, 1), pltpu.roll(here, 1, 1)
            side_r, side_l = pltpu.roll(side, LANES - 1, 1), pltpu.roll(side, 1, 1)
            for ref, cols, dots in (
                (m_ref, jnp.where(last, beyond, here_r) - jnp.where(first, side_l, here_l), dm),
                (h_ref, jnp.where(last, here_r, side_r) - side_l, dh),
            ):
                deep = ref[k + 2, top + 1 : top + 1 + SUB] - ref[k, top + 1 : top + 1 + SUB]
                down = ref[k + 1, top + 2 : top + 2 + SUB] - ref[k + 1, top : top + SUB]
                half = 0.5 * lax.rsqrt(0.25 * (deep * deep + down * down + cols * cols) + 1.0)
                deep, down, cols = deep * half, down * half, cols * half
                for w in range(VIEWS):
                    a, b, c = towards[w]
                    dots[w, k, top : top + SUB] = deep * a + down * b + cols * c
        return carry

    tile = 32
    per_view = strip // tile
    base_row = y * rows + z * strip
    base_col = x * LANES
    lanes = lax.broadcasted_iota(jnp.int32, (tile, LANES), 1)
    rows_at = lax.broadcasted_iota(jnp.int32, (tile, LANES), 0)
    bias = [0.5 * palette[0, c] for c in range(3)]
    gain = [0.5 * palette[1, c] for c in range(3)]

    def march(w, top, brick, cells, start, colors, through):
        ambient = jnp.zeros((tile, LANES), jnp.float32)
        rate2 = rate[w] * (-math.log2(math.e))
        off_r, off_c = offset[brick, 0, w], offset[brick, 1, w]
        inside = jnp.logical_and(rows_at >= off_r - base_row - top, lanes >= off_c - base_col)
        fall = jnp.where(inside, rate2, 0.0)
        for j in range(bz):
            k = brick * bz + j
            sr = off_r + shear[w, 0, k]
            sc = off_c + shear[w, 1, k]
            at = HALO + top - sr
            wrap = lanes >= LANES - sc
            value = jnp.where(wrap, h_ref[k + 1, pl.ds(at, tile)], cells[start + j, pl.ds(at, tile)])
            dot = jnp.where(wrap, dh[w, k, pl.ds(at - 1, tile)], dm[w, k, pl.ds(at - 1, tile)])
            value = pltpu.roll(value, sc, 1)
            dot = pltpu.roll(dot, sc, 1)
            kept = jnp.exp2(fall * (1.0 + jnp.tanh(value)))
            weight = (0.125 + 0.375 * dot * dot) * ((1.0 - kept) * through)
            through = through * kept
            ambient = ambient + weight
            colors = [
                colors[c] + weight * jnp.tanh(bias[c] + gain[c] * value) for c in range(3)
            ]
        return [color + ambient for color in colors], through

    def views(act):
        def one(step, carry):
            act(step // per_view, (step % per_view) * tile)
            return carry

        lax.fori_loop(0, VIEWS * per_view, one, 0)

    def own_layer(w, top):
        at = pl.ds(top, tile)
        zero = jnp.zeros((tile, LANES), jnp.float32)
        colors, through = march(w, top, z, own_ref, 0, [zero] * 3, zero + 1.0)
        ahead = order[0, w] == z
        for c in range(3):
            out_ref[w, c, at] = jnp.where(ahead, colors[c], 0.0)
            back[w, c, at] = jnp.where(ahead, 0.0, colors[c])
        out_ref[w, 3, at] = jnp.where(ahead, through, 1.0)
        back[w, 3, at] = jnp.where(ahead, 1.0, through)

    def other_layer(w, top):
        at = pl.ds(top, tile)
        colors, through = march(
            w, top, 1 - z, m_ref, 1 + (1 - z) * bz, [out_ref[w, c, at] for c in range(3)],
            out_ref[w, 3, at],
        )
        for c in range(3):
            out_ref[w, c, at] = colors[c] + through * back[w, c, at]
        out_ref[w, 3, at] = 1.0 - through * back[w, 3, at]

    def each(start, stop):
        lax.fori_loop(start, stop, slopes, 0)

    each(z * (bz + 1), z * (bz + 1) + bz - 1)
    sided(middle)
    each(bz - 1, bz + 1)
    views(own_layer)
    sided(ending)
    each((1 - z) * (bz + 1), (1 - z) * (bz + 1) + bz - 1)
    views(other_layer)
    sided(lambda mine: steps[mine][2]())


def two_bricks(mesh, pressure, light, palette, rate, shear, offset, order):
    bz, rows, cols = pressure.shape
    dims = (mesh.shape["gy"], mesh.shape["gx"], bz, rows)
    strip = rows // 2
    tall = HALO + strip + SUB
    depth = 2 * bz
    vmem = pl.BlockSpec(memory_space=pltpu.VMEM)
    hbm = pl.BlockSpec(memory_space=pltpu.HBM)
    f32 = jnp.float32
    _, sent, got = routes_of(dims)
    tables = (
        light,
        palette.T,
        rate,
        jnp.transpose(shear, (0, 2, 1)),
        jnp.transpose(offset, (1, 2, 0)),
        order.T,
    )
    image = pl.pallas_call(
        functools.partial(render, dims),
        out_shape=jax.ShapeDtypeStruct((VIEWS, 4, strip, LANES), f32),
        in_specs=[hbm] * 7,
        out_specs=vmem,
        scratch_shapes=[
            *[pltpu.SMEM(table.shape, table.dtype) for table in tables],
            pltpu.VMEM((bz, rows, LANES), f32),
            pltpu.VMEM((depth + 2, tall, LANES), f32),
            pltpu.VMEM((bz, tall, LANES), f32),
            pltpu.VMEM((2, got, LANES), f32),
            pltpu.VMEM((2, 2, SUB, LANES), f32),
            pltpu.VMEM((sent, LANES), f32),
            pltpu.VMEM((SUB, LANES), f32),
            pltpu.VMEM((depth + 2, tall, LANES), f32),
            pltpu.VMEM((2, tall, LANES), f32),
            pltpu.VMEM((VIEWS, depth, HALO + strip, LANES), f32),
            pltpu.VMEM((VIEWS, depth, HALO + strip, LANES), f32),
            pltpu.VMEM((VIEWS, 4, strip, LANES), f32),
            pltpu.SemaphoreType.DMA((SLOTS,)),
            pltpu.SemaphoreType.DMA((SLOTS,)),
            pltpu.SemaphoreType.DMA((2,)),
            pltpu.SemaphoreType.DMA((len(tables),)),
        ],
        compiler_params=pltpu.CompilerParams(collective_id=0, has_side_effects=True, vmem_limit_bytes=12 << 20),
        name="render",
    )(
        *[pltpu.with_memory_space_constraint(t, pltpu.HBM) for t in (*tables, pressure)]
    )
    return image[:, :, None]


def fits(mesh, shape):
    bz, rows, cols = shape
    return (
        mesh.shape["gz"] == 2
        and cols == LANES
        and rows % 64 == 0
        and 2 * HALO <= rows <= LANES
        and bz * (HALO - SUB) == LANES
        and bz * (rows // SUB) <= LANES
    )


def on_device(mesh, pressure, *rest):
    if fits(mesh, pressure.shape):
        return two_bricks(mesh, pressure, *rest)
    return many_bricks(pressure, *rest)


def solution(mesh):
    return jax.shard_map(
        functools.partial(on_device, mesh),
        mesh=mesh,
        in_specs=(P("gz", "gy", "gx"), P(), P(), P(), P(), P(), P()),
        out_specs=P(None, None, "gz", "gy", "gx"),
        check_vma=False,
    )
```

```python
import functools
import math

import jax
import jax.numpy as jnp
from jax import lax
from jax.experimental import pallas as pl
from jax.experimental.pallas import tpu as pltpu
from jax.sharding import PartitionSpec as P

VIEWS = 4
SHEAR = 8
REACH = 32
HALO = SHEAR + REACH
SUB = 8
LANES = 128
MESH = pl.DeviceIdType.MESH


def padded(cells, sides, width):
    for axis, dim in sides:
        count = lax.axis_size(axis)
        ends = count - 1
        head = lax.slice_in_dim(cells, 0, width, axis=dim)
        tail = lax.slice_in_dim(cells, cells.shape[dim] - width, cells.shape[dim], axis=dim)
        cells = jnp.concatenate(
            [
                lax.ppermute(tail, axis, [(i, (i + 1) % count) for i in range(ends)]),
                cells,
                lax.ppermute(head, axis, [((i + 1) % count, i) for i in range(ends)]),
            ],
            axis=dim,
        )
    return cells


def shifted(value, axis, steps):
    count = lax.axis_size(axis)
    first, last = (max(0, -steps), min(count, count - steps))
    return lax.ppermute(value, axis, [(source, source + steps) for source in range(first, last)])


def surface_terms(slab):
    inner = slab[1:-1, 1:-1, 1:-1]
    grad_depth = 0.5 * (slab[2:, 1:-1, 1:-1] - slab[:-2, 1:-1, 1:-1])
    grad_rows = 0.5 * (slab[1:-1, 2:, 1:-1] - slab[1:-1, :-2, 1:-1])
    grad_cols = 0.5 * (slab[1:-1, 1:-1, 2:] - slab[1:-1, 1:-1, :-2])
    factor = lax.rsqrt(
        grad_depth * grad_depth + grad_rows * grad_rows + grad_cols * grad_cols + 1.0
    )
    return (inner, (grad_depth * factor, grad_rows * factor, grad_cols * factor))


def render_layers(inner, normals, shifts, light, palette, rate, rows, cols):
    lengths = jnp.sqrt(jnp.sum(light * light, axis=1, keepdims=True) + 1.0)
    towards = light / lengths
    offsets = palette[:, 0][:, None, None]
    slopes = palette[:, 1][:, None, None]
    layers = []
    for view in range(light.shape[0]):

        def advance(carry, items):
            color, depth = carry
            value_slab, normal_depth, normal_rows, normal_cols, moved = items
            start = (SHEAR - moved[0], SHEAR - moved[1])
            value = lax.dynamic_slice(value_slab, start, (rows, cols))
            dot = (
                lax.dynamic_slice(normal_depth, start, (rows, cols)) * towards[view, 0]
                + lax.dynamic_slice(normal_rows, start, (rows, cols)) * towards[view, 1]
                + lax.dynamic_slice(normal_cols, start, (rows, cols)) * towards[view, 2]
            )
            shade = 0.25 + 0.75 * dot * dot
            density = rate[view] * (1.0 + jnp.tanh(value))
            alpha = 1.0 - jnp.exp(-density)
            weight = alpha * jnp.exp(-depth)
            hues = jax.nn.sigmoid(offsets + slopes * value[None]) * shade[None]
            return ((color + hues * weight[None], depth + density), None)

        start_carry = (
            jnp.zeros((3, rows, cols), jnp.float32),
            jnp.zeros((rows, cols), jnp.float32),
        )
        (color, depth), _ = lax.scan(
            advance, start_carry, (inner, normals[0], normals[1], normals[2], shifts[view])
        )
        layers.append(jnp.concatenate([color, depth[None]], axis=0))
    return jnp.stack(layers)


def precedence(order):
    bricks = order.shape[1]
    onehot = (order[:, :, None] == jnp.arange(bricks, dtype=jnp.int32)[None, None, :]).astype(
        jnp.float32
    )
    ranks = jnp.sum(onehot * jnp.arange(bricks, dtype=jnp.float32)[None, :, None], axis=1)
    return (ranks[:, None, :] < ranks[:, :, None]).astype(jnp.float32)


def many_bricks(pressure, light, palette, rate, shear, offset, order):
    depth_cells, rows, cols = pressure.shape
    brick = lax.axis_index("gz")
    zero = jnp.zeros((), jnp.int32)
    widened = padded(pressure, (("gy", 1), ("gx", 2)), SHEAR + 1)
    slab = padded(widened, (("gz", 0),), 1)
    inner, normals = surface_terms(slab)
    shifts = lax.dynamic_slice(shear, (zero, brick * depth_cells, zero), (VIEWS, depth_cells, 2))
    layers = render_layers(inner, normals, shifts, light, palette, rate, rows, cols)
    moved = lax.dynamic_index_in_dim(offset, brick, 1, keepdims=False)
    blank = jnp.zeros((4, rows + REACH, cols + REACH), jnp.float32)
    canvas = jnp.stack(
        [
            lax.dynamic_update_slice(blank, layers[view], (zero, moved[view, 0], moved[view, 1]))
            for view in range(VIEWS)
        ]
    )
    own_tile = canvas[:, :, :rows, :cols]
    from_above = shifted(canvas[:, :, rows:, :cols], "gy", 1)
    from_left = shifted(canvas[:, :, :rows, cols:], "gx", 1)
    from_diagonal = shifted(canvas[:, :, rows:, cols:], ("gy", "gx"), lax.axis_size("gx") + 1)
    from_diagonal = from_diagonal * (lax.axis_index("gx") > 0).astype(jnp.float32)
    own_tile = own_tile.at[:, :, :REACH, :].add(from_above)
    own_tile = own_tile.at[:, :, :, :REACH].add(from_left)
    own_tile = own_tile.at[:, :, :REACH, :REACH].add(from_diagonal)
    ranking = precedence(order)
    pieces = lax.all_to_all(own_tile[None], "gz", split_axis=3, concat_axis=0, tiled=True)
    depths = pieces[:, :, 3]
    cover = jnp.einsum("vbc,cvyx->bvyx", ranking, depths, precision=lax.Precision.HIGHEST)
    colors = jnp.sum(pieces[:, :, :3] * jnp.exp(-cover)[:, :, None], axis=0)
    opacity = 1.0 - jnp.exp(-jnp.sum(depths, axis=0))
    image = jnp.concatenate([colors, opacity[:, None]], axis=1)
    return image[:, :, None]


class Route:
    def __init__(self, dims, side, step, start, count, slab, half):
        bz = dims[2]
        self.side, self.step, self.half = side, step, half
        self.rows, self.slab = pl.ds(start, count), pl.ds(slab, count)
        self.groups = LANES // (SUB * bz)
        self.tiles = range(start // SUB, (start + count) // SUB)
        self.first = slab // SUB
        self.folds = range(
            self.tiles[0] // self.groups, self.tiles[-1] // self.groups + 1
        )
        self.size = (len(self.tiles) + len(self.folds)) * SUB
        self.base = self.sent = 0

    def there(self, y, ny):
        return y + self.step >= 0 if self.step < 0 else y + self.step < ny

    def comes(self, y, ny):
        return y - self.step < ny if self.step < 0 else y - self.step >= 0

    def wide(self, tile):
        return (tile - self.tiles[0]) * SUB

    def narrow(self, fold):
        return (len(self.tiles) + fold - self.folds[0]) * SUB


def routes_of(dims):
    rows = dims[3]
    strip = rows // 2
    routes = [
        Route(dims, 0, 0, 0, strip + SUB, HALO, 0),
        Route(dims, 0, 1, rows - HALO, HALO, 0, 1),
        Route(dims, 1, 0, strip - HALO, HALO + strip, 0, 0),
        Route(dims, 1, -1, 0, SUB, HALO + strip, 1),
    ]
    sent = 0
    for route in routes:
        route.sent = sent
        sent += route.size
    routes[1].base, routes[3].base = routes[0].size, routes[2].size
    return routes, sent, max(routes[0].size + routes[1].size, routes[2].size + routes[3].size)


MAIN, EDGE, BESIDE, COLS, ENDS, SLOTS = 0, 3, 6, 7, 11, 15
PARTS = 3
FACING, BELOW, RIGHT, ACROSS = range(4)


def exchange(
    dims, mine, here, p_ref, m_ref, cols_out, cols_in, ends_out, ends_in, sends, arrivals, ready
):
    ny, nx, bz, rows = dims
    z, y, x = here
    has_left, has_right = x > 0, x < nx - 1
    has_up, has_down = y > 0, y < ny - 1
    routes = routes_of(dims)[0]

    def remote(src, dst, sent, arrival, who):
        return pltpu.make_async_remote_copy(
            src_ref=src,
            dst_ref=dst,
            send_sem=sends.at[sent],
            recv_sem=arrivals.at[arrival],
            device_id=who,
            device_id_type=MESH,
        )

    def rows_of(brick, route, part):
        start = 0 if part is None else part
        count = bz if part is None else (bz - part if part == PARTS - 1 else 1)
        if part is not None and brick == 0:
            start = bz - start - count
        slot = BESIDE if part is None else (EDGE if route.half else MAIN) + part
        return remote(
            p_ref.at[pl.ds(start, count), route.rows],
            m_ref.at[pl.ds(1 + brick * bz + start, count), route.slab],
            slot, slot, (route.side, y + route.step, x),
        )

    def cols_of(brick, route):
        return remote(
            cols_out.at[pl.ds(route.sent, route.size)],
            cols_in.at[brick, pl.ds(route.base, route.size)],
            COLS + 2 * route.side + route.half, COLS + 2 * brick + route.half,
            (route.side, y + route.step, x + 1),
        )

    def ends_of(brick, route):
        return remote(
            ends_out,
            ends_in.at[brick, route.half],
            ENDS + 2 * route.side + route.half, ENDS + 2 * brick + route.half,
            (route.side, y + route.step, x - 1),
        )

    def rows_out(route):
        there = route.there(y, ny)
        if route.side != mine:
            return [(there, rows_of(mine, route, part)) for part in range(PARTS)]
        return [(there, rows_of(mine, route, None))] if route.half else []

    def cols_sent(same):
        return [
            (jnp.logical_and(r.there(y, ny), has_right), cols_of(mine, r))
            for r in routes
            if (r.side == mine) == same
        ]

    def ends_sent():
        return [(jnp.logical_and(r.there(y, ny), has_left), ends_of(mine, r)) for r in routes]

    def apply(pairs, act):
        for there, copy in pairs:

            @pl.when(there)
            def _():
                act(copy)

    def start(pairs):
        apply(pairs, lambda copy: copy.start())

    def heard(kind, there, count):
        @pl.when(there)
        def _():
            pl.semaphore_wait(ready.at[kind], count)

    mains, own_halo, halos = (
        (routes[2], routes[1], routes[3]) if mine == 0 else (routes[0], routes[3], routes[1])
    )
    next_ones = [1 + there.astype(jnp.int32) for there in (has_down, has_up)]

    def send_first():
        if mine == 0:
            start(rows_out(halos))
        else:
            start(rows_out(mains))
            start(rows_out(own_halo))

    def send_rest():
        if mine == 0:
            heard(FACING, y >= 0, 1)
            start(rows_out(mains))
            start(ends_sent())
            heard(BELOW, has_down, 1)
            start(rows_out(own_halo))
        else:
            start(ends_sent())
            heard(BELOW, has_down, 1)
            start(rows_out(halos))
        heard(RIGHT, has_right, next_ones[mine])
        start(cols_sent(True))
        heard(ACROSS, has_right, next_ones[1 - mine])
        apply(cols_sent(True), lambda copy: copy.wait_send())
        start(cols_sent(False))

    def receive(brick, parts, sides):
        pairs = []
        for route in routes:
            if route.side != mine:
                continue
            comes = route.comes(y, ny)
            if brick != mine:
                pairs += [(comes, rows_of(brick, route, part)) for part in parts]
            elif route.half:
                pairs += [(comes, rows_of(brick, route, None))]
            if sides:
                pairs += [
                    (jnp.logical_and(comes, has_left), cols_of(brick, route)),
                    (jnp.logical_and(comes, has_right), ends_of(brick, route)),
                ]
        apply(pairs, lambda copy: copy.wait_recv())

    def close():
        for route in routes:
            apply(rows_out(route), lambda copy: copy.wait_send())
        apply(ends_sent() + cols_sent(False), lambda copy: copy.wait_send())

    return send_first, send_rest, receive, close


def partners_of(dims, here, over):
    ny, nx = dims[:2]
    z, y, x = here
    steps = [(z, over, 0), (1 - z, z if over > 0 else z - 1, 0)]
    steps += [
        (side, step, over)
        for side, step in ((z, -1), (z, 0), (z, 1), (1 - z, 0), (1 - z, 2 * z - 1))
    ]
    for side, step, across in steps:
        yield inside_of(dims, y + step, x + across), (side, y + step, x + across)


def inside_of(dims, y, x):
    ny, nx = dims[:2]
    return jnp.logical_and(
        jnp.logical_and(y >= 0, y < ny), jnp.logical_and(x >= 0, x < nx)
    )


def answers_of(dims, here):
    z, y, x = here
    own = z == 0
    yield jnp.logical_and(own, y > 0), (z, y - 1, x), BELOW
    yield jnp.logical_and(own, y > 0), (1 - z, y - 1, x), BELOW
    yield jnp.logical_not(own), (1 - z, y, x), FACING
    for side, kind in ((z, RIGHT), (1 - z, ACROSS)):
        for step in (0, 2 * z - 1):
            yield inside_of(dims, y + step, x - 1), (side, y + step, x - 1), kind


def render(
    dims, light_in, palette_in, rate_in, shear_in, offset_in, order_in, p_ref, out_ref,
    light, palette, rate, shear, offset, order, tile_ref, m_ref, own_ref, cols_in, ends_in,
    cols_out, ends_out, h_ref, r_ref, dm, dh, back, sends, arrivals, ready, local_sems, table_sems,
):
    ny, nx, bz, rows = dims
    strip = rows // 2
    tall = HALO + strip + SUB
    depth = 2 * bz
    blocks = (HALO + strip) // SUB
    wide_lanes = HALO - SUB
    z, y, x = lax.axis_index("gz"), lax.axis_index("gy"), lax.axis_index("gx")
    routes = routes_of(dims)[0]

    tables = [
        pltpu.make_async_copy(source, target, table_sems.at[i])
        for i, (source, target) in enumerate(
            (
                (light_in, light), (palette_in, palette), (rate_in, rate),
                (shear_in, shear), (offset_in, offset), (order_in, order),
            )
        )
    ]
    barrier = pltpu.get_barrier_semaphore()

    def sided(act):
        for mine in range(2):

            @pl.when(z == mine)
            def _():
                act(mine)

    for there, who in partners_of(dims, (z, y, x), 1):

        @pl.when(there)
        def _():
            pl.semaphore_signal(barrier, inc=1, device_id=who, device_id_type=MESH)

    count = 0
    for there, _ in partners_of(dims, (z, y, x), -1):
        count = count + there.astype(jnp.int32)

    steps = [
        exchange(
            dims, mine, (z, y, x), p_ref, m_ref, cols_out, cols_in, ends_out, ends_in,
            sends, arrivals, ready,
        )
        for mine in range(2)
    ]

    def local_slab(mine):
        route = routes[2 * mine]
        return pltpu.make_async_copy(
            p_ref.at[:, route.rows], m_ref.at[pl.ds(1 + mine * bz, bz), route.slab],
            local_sems.at[1],
        )

    local_tile = pltpu.make_async_copy(p_ref, tile_ref, local_sems.at[0])
    local_tile.start()
    sided(lambda mine: local_slab(mine).start())
    for copy in tables:
        copy.start()

    @pl.when(count > 0)
    def _():
        pl.semaphore_wait(barrier, count)

    for there, who, kind in answers_of(dims, (z, y, x)):

        @pl.when(there)
        def _():
            pl.semaphore_signal(ready.at[kind], inc=1, device_id=who, device_id_type=MESH)


    sided(lambda mine: steps[mine][0]())

    empty = jnp.zeros((tall, LANES), jnp.float32)
    for ref in (m_ref, h_ref):
        ref[0] = empty
        ref[depth + 1] = empty

    def blank(mine):
        route = routes[2 * mine + 1]

        @pl.when(jnp.logical_not(route.comes(y, ny)))
        def _():
            m_ref[:, route.slab] = jnp.zeros((depth + 2, len(route.tiles) * SUB, LANES), jnp.float32)
            cols_in[:, route.base : route.base + route.size] = jnp.zeros(
                (2, route.size, LANES), jnp.float32
            )
            ends_in[:, 1] = jnp.zeros((2, SUB, LANES), jnp.float32)

    sided(blank)

    @pl.when(x == 0)
    def _():
        cols_in[...] = jnp.zeros(cols_in.shape, jnp.float32)

    @pl.when(x == nx - 1)
    def _():
        ends_in[...] = jnp.zeros(ends_in.shape, jnp.float32)

    lane = lax.broadcasted_iota(jnp.int32, (SUB, LANES), 1)
    last = lane == LANES - 1
    first = lane == 0
    groups = routes[0].groups
    tiles = rows // SUB

    def cell(j, t):
        return tile_ref[j, t * SUB : (t + 1) * SUB]

    def put(t_or_fold, is_wide, value):
        for route in routes:
            if t_or_fold in (route.tiles if is_wide else route.folds):
                at = route.sent + (route.wide if is_wide else route.narrow)(t_or_fold)
                cols_out[at : at + SUB] = value

    def merged(pieces):
        while len(pieces) > 1:
            pieces = [
                (a[0], jnp.where(lane >= b[0], b[1], a[1]))
                for a, b in zip(pieces[::2], pieces[1::2])
            ] + (pieces[-1:] if len(pieces) % 2 else [])
        return pieces[0][1]

    def turned(value, by):
        return pltpu.roll(value, by % LANES, 1) if by % LANES else value

    local_tile.wait()
    for t in range(tiles):
        put(
            t, True,
            merged(
                [(wide_lanes * j, turned(cell(j, t), wide_lanes * (j + 1))) for j in range(bz)]
            ),
        )
    for fold in range(tiles // groups):
        put(
            fold, False,
            merged(
                [
                    (
                        SUB * (bz * g + j),
                        turned(cell(j, fold * groups + g), SUB * (bz * g + j) + HALO),
                    )
                    for g in range(groups)
                    for j in range(bz)
                ]
            ),
        )
    ends_out[...] = merged(
        [(t * bz + j, turned(cell(j, t), t * bz + j)) for t in range(tiles) for j in range(bz)]
    )

    def unpack(mine, brick):
        for route in routes[2 * mine : 2 * mine + 2]:
            for t in route.tiles:
                row = (route.first + t - route.tiles[0]) * SUB
                at = route.base + route.wide(t)
                wide = cols_in[brick, at : at + SUB]
                at = route.base + route.narrow(t // groups)
                narrow = cols_in[brick, at : at + SUB]
                for j in range(bz):
                    h_ref[1 + brick * bz + j, row : row + SUB] = jnp.where(
                        lane >= LANES - wide_lanes,
                        turned(wide, -wide_lanes * (j + 1)),
                        turned(narrow, -SUB * (bz * (t % groups) + j) - HALO),
                    )
                r_ref[brick, row : row + SUB] = turned(
                    ends_in[brick, route.half], LANES - 1 - t * bz
                )

    def opening(mine):
        _, send_rest, receive, _ = steps[mine]
        send_rest()
        local_slab(mine).wait()
        receive(mine, (), True)
        own_ref[...] = m_ref[1 + mine * bz : 1 + (mine + 1) * bz]
        unpack(mine, mine)

    def middle(mine):
        receive = steps[mine][2]
        receive(1 - mine, range(PARTS - 1), True)
        unpack(mine, 1 - mine)

    def ending(mine):
        receive = steps[mine][2]
        receive(1 - mine, (PARTS - 1,), False)

    sided(opening)
    for copy in tables:
        copy.wait()

    towards = []
    for w in range(VIEWS):
        a, b, c = light[w, 0], light[w, 1], light[w, 2]
        inverse = lax.rsqrt(jnp.full((SUB, LANES), a * a + b * b + c * c + 1.0, jnp.float32))
        towards.append((a * inverse, b * inverse, c * inverse))

    def slopes(k, carry):
        for i in range(blocks):
            top = i * SUB
            here = m_ref[k + 1, top + 1 : top + 1 + SUB]
            side = h_ref[k + 1, top + 1 : top + 1 + SUB]
            beyond = pltpu.roll(
                r_ref[k // bz, top + 1 : top + 1 + SUB], (LANES - k % bz) % LANES, 1
            )
            here_r, here_l = pltpu.roll(here, LANES - 1, 1), pltpu.roll(here, 1, 1)
            side_r, side_l = pltpu.roll(side, LANES - 1, 1), pltpu.roll(side, 1, 1)
            for ref, cols, dots in (
                (m_ref, jnp.where(last, beyond, here_r) - jnp.where(first, side_l, here_l), dm),
                (h_ref, jnp.where(last, here_r, side_r) - side_l, dh),
            ):
                deep = ref[k + 2, top + 1 : top + 1 + SUB] - ref[k, top + 1 : top + 1 + SUB]
                down = ref[k + 1, top + 2 : top + 2 + SUB] - ref[k + 1, top : top + SUB]
                half = 0.5 * lax.rsqrt(0.25 * (deep * deep + down * down + cols * cols) + 1.0)
                deep, down, cols = deep * half, down * half, cols * half
                for w in range(VIEWS):
                    a, b, c = towards[w]
                    dots[w, k, top : top + SUB] = deep * a + down * b + cols * c
        return carry

    tile = 32
    per_view = strip // tile
    base_row = y * rows + z * strip
    base_col = x * LANES
    lanes = lax.broadcasted_iota(jnp.int32, (tile, LANES), 1)
    rows_at = lax.broadcasted_iota(jnp.int32, (tile, LANES), 0)
    bias = [0.5 * palette[0, c] for c in range(3)]
    gain = [0.5 * palette[1, c] for c in range(3)]

    def march(w, top, brick, cells, start, colors, through):
        ambient = jnp.zeros((tile, LANES), jnp.float32)
        rate2 = rate[w] * (-math.log2(math.e))
        off_r, off_c = offset[brick, 0, w], offset[brick, 1, w]
        inside = jnp.logical_and(rows_at >= off_r - base_row - top, lanes >= off_c - base_col)
        fall = jnp.where(inside, rate2, 0.0)
        for j in range(bz):
            k = brick * bz + j
            sr = off_r + shear[w, 0, k]
            sc = off_c + shear[w, 1, k]
            at = HALO + top - sr
            wrap = lanes >= LANES - sc
            value = jnp.where(wrap, h_ref[k + 1, pl.ds(at, tile)], cells[start + j, pl.ds(at, tile)])
            dot = jnp.where(wrap, dh[w, k, pl.ds(at - 1, tile)], dm[w, k, pl.ds(at - 1, tile)])
            value = pltpu.roll(value, sc, 1)
            dot = pltpu.roll(dot, sc, 1)
            kept = jnp.exp2(fall * (1.0 + jnp.tanh(value)))
            weight = (0.125 + 0.375 * dot * dot) * ((1.0 - kept) * through)
            through = through * kept
            ambient = ambient + weight
            colors = [
                colors[c] + weight * jnp.tanh(bias[c] + gain[c] * value) for c in range(3)
            ]
        return [color + ambient for color in colors], through

    def views(act):
        def one(step, carry):
            act(step // per_view, (step % per_view) * tile)
            return carry

        lax.fori_loop(0, VIEWS * per_view, one, 0, unroll=VIEWS * per_view)

    def own_layer(w, top):
        at = pl.ds(top, tile)
        zero = jnp.zeros((tile, LANES), jnp.float32)
        colors, through = march(w, top, z, own_ref, 0, [zero] * 3, zero + 1.0)
        ahead = order[0, w] == z
        for c in range(3):
            out_ref[w, c, at] = jnp.where(ahead, colors[c], 0.0)
            back[w, c, at] = jnp.where(ahead, 0.0, colors[c])
        out_ref[w, 3, at] = jnp.where(ahead, through, 1.0)
        back[w, 3, at] = jnp.where(ahead, 1.0, through)

    def other_layer(w, top):
        at = pl.ds(top, tile)
        colors, through = march(
            w, top, 1 - z, m_ref, 1 + (1 - z) * bz, [out_ref[w, c, at] for c in range(3)],
            out_ref[w, 3, at],
        )
        for c in range(3):
            out_ref[w, c, at] = colors[c] + through * back[w, c, at]
        out_ref[w, 3, at] = 1.0 - through * back[w, 3, at]

    def each(start, stop):
        lax.fori_loop(start, stop, slopes, 0)

    each(z * (bz + 1), z * (bz + 1) + bz - 1)
    sided(middle)
    each(bz - 1, bz + 1)
    views(own_layer)
    sided(ending)
    each((1 - z) * (bz + 1), (1 - z) * (bz + 1) + bz - 1)
    views(other_layer)
    sided(lambda mine: steps[mine][3]())


def two_bricks(mesh, pressure, light, palette, rate, shear, offset, order):
    bz, rows, cols = pressure.shape
    dims = (mesh.shape["gy"], mesh.shape["gx"], bz, rows)
    strip = rows // 2
    tall = HALO + strip + SUB
    depth = 2 * bz
    vmem = pl.BlockSpec(memory_space=pltpu.VMEM)
    hbm = pl.BlockSpec(memory_space=pltpu.HBM)
    f32 = jnp.float32
    _, sent, got = routes_of(dims)
    tables = (
        light,
        palette.T,
        rate,
        jnp.transpose(shear, (0, 2, 1)),
        jnp.transpose(offset, (1, 2, 0)),
        order.T,
    )
    image = pl.pallas_call(
        functools.partial(render, dims),
        out_shape=jax.ShapeDtypeStruct((VIEWS, 4, strip, LANES), f32),
        in_specs=[hbm] * 7,
        out_specs=vmem,
        scratch_shapes=[
            *[pltpu.SMEM(table.shape, table.dtype) for table in tables],
            pltpu.VMEM((bz, rows, LANES), f32),
            pltpu.VMEM((depth + 2, tall, LANES), f32),
            pltpu.VMEM((bz, tall, LANES), f32),
            pltpu.VMEM((2, got, LANES), f32),
            pltpu.VMEM((2, 2, SUB, LANES), f32),
            pltpu.VMEM((sent, LANES), f32),
            pltpu.VMEM((SUB, LANES), f32),
            pltpu.VMEM((depth + 2, tall, LANES), f32),
            pltpu.VMEM((2, tall, LANES), f32),
            pltpu.VMEM((VIEWS, depth, HALO + strip, LANES), f32),
            pltpu.VMEM((VIEWS, depth, HALO + strip, LANES), f32),
            pltpu.VMEM((VIEWS, 4, strip, LANES), f32),
            pltpu.SemaphoreType.DMA((SLOTS,)),
            pltpu.SemaphoreType.DMA((SLOTS,)),
            pltpu.SemaphoreType.REGULAR((4,)),
            pltpu.SemaphoreType.DMA((2,)),
            pltpu.SemaphoreType.DMA((len(tables),)),
        ],
        compiler_params=pltpu.CompilerParams(collective_id=0, has_side_effects=True, vmem_limit_bytes=12 << 20),
        name="render",
    )(
        *[pltpu.with_memory_space_constraint(t, pltpu.HBM) for t in (*tables, pressure)]
    )
    return image[:, :, None]


def fits(mesh, shape):
    bz, rows, cols = shape
    return (
        mesh.shape["gz"] == 2
        and cols == LANES
        and rows % 64 == 0
        and 2 * HALO <= rows <= LANES
        and bz * (HALO - SUB) == LANES
        and bz * (rows // SUB) <= LANES
    )


def on_device(mesh, pressure, *rest):
    if fits(mesh, pressure.shape):
        return two_bricks(mesh, pressure, *rest)
    return many_bricks(pressure, *rest)


def solution(mesh):
    return jax.shard_map(
        functools.partial(on_device, mesh),
        mesh=mesh,
        in_specs=(P("gz", "gy", "gx"), P(), P(), P(), P(), P(), P()),
        out_specs=P(None, None, "gz", "gy", "gx"),
        check_vma=False,
    )
```

```python
import functools
import math

import jax
import jax.numpy as jnp
from jax import lax
from jax.experimental import pallas as pl
from jax.experimental.pallas import tpu as pltpu
from jax.sharding import PartitionSpec as P

VIEWS = 4
SHEAR = 8
REACH = 32
HALO = SHEAR + REACH
SUB = 8
LANES = 128
MESH = pl.DeviceIdType.MESH


def padded(cells, sides, width):
    for axis, dim in sides:
        count = lax.axis_size(axis)
        ends = count - 1
        head = lax.slice_in_dim(cells, 0, width, axis=dim)
        tail = lax.slice_in_dim(cells, cells.shape[dim] - width, cells.shape[dim], axis=dim)
        cells = jnp.concatenate(
            [
                lax.ppermute(tail, axis, [(i, (i + 1) % count) for i in range(ends)]),
                cells,
                lax.ppermute(head, axis, [((i + 1) % count, i) for i in range(ends)]),
            ],
            axis=dim,
        )
    return cells


def shifted(value, axis, steps):
    count = lax.axis_size(axis)
    first, last = (max(0, -steps), min(count, count - steps))
    return lax.ppermute(value, axis, [(source, source + steps) for source in range(first, last)])


def surface_terms(slab):
    inner = slab[1:-1, 1:-1, 1:-1]
    grad_depth = 0.5 * (slab[2:, 1:-1, 1:-1] - slab[:-2, 1:-1, 1:-1])
    grad_rows = 0.5 * (slab[1:-1, 2:, 1:-1] - slab[1:-1, :-2, 1:-1])
    grad_cols = 0.5 * (slab[1:-1, 1:-1, 2:] - slab[1:-1, 1:-1, :-2])
    factor = lax.rsqrt(
        grad_depth * grad_depth + grad_rows * grad_rows + grad_cols * grad_cols + 1.0
    )
    return (inner, (grad_depth * factor, grad_rows * factor, grad_cols * factor))


def render_layers(inner, normals, shifts, light, palette, rate, rows, cols):
    lengths = jnp.sqrt(jnp.sum(light * light, axis=1, keepdims=True) + 1.0)
    towards = light / lengths
    offsets = palette[:, 0][:, None, None]
    slopes = palette[:, 1][:, None, None]
    layers = []
    for view in range(light.shape[0]):

        def advance(carry, items):
            color, depth = carry
            value_slab, normal_depth, normal_rows, normal_cols, moved = items
            start = (SHEAR - moved[0], SHEAR - moved[1])
            value = lax.dynamic_slice(value_slab, start, (rows, cols))
            dot = (
                lax.dynamic_slice(normal_depth, start, (rows, cols)) * towards[view, 0]
                + lax.dynamic_slice(normal_rows, start, (rows, cols)) * towards[view, 1]
                + lax.dynamic_slice(normal_cols, start, (rows, cols)) * towards[view, 2]
            )
            shade = 0.25 + 0.75 * dot * dot
            density = rate[view] * (1.0 + jnp.tanh(value))
            alpha = 1.0 - jnp.exp(-density)
            weight = alpha * jnp.exp(-depth)
            hues = jax.nn.sigmoid(offsets + slopes * value[None]) * shade[None]
            return ((color + hues * weight[None], depth + density), None)

        start_carry = (
            jnp.zeros((3, rows, cols), jnp.float32),
            jnp.zeros((rows, cols), jnp.float32),
        )
        (color, depth), _ = lax.scan(
            advance, start_carry, (inner, normals[0], normals[1], normals[2], shifts[view])
        )
        layers.append(jnp.concatenate([color, depth[None]], axis=0))
    return jnp.stack(layers)


def precedence(order):
    bricks = order.shape[1]
    onehot = (order[:, :, None] == jnp.arange(bricks, dtype=jnp.int32)[None, None, :]).astype(
        jnp.float32
    )
    ranks = jnp.sum(onehot * jnp.arange(bricks, dtype=jnp.float32)[None, :, None], axis=1)
    return (ranks[:, None, :] < ranks[:, :, None]).astype(jnp.float32)


def many_bricks(pressure, light, palette, rate, shear, offset, order):
    depth_cells, rows, cols = pressure.shape
    brick = lax.axis_index("gz")
    zero = jnp.zeros((), jnp.int32)
    widened = padded(pressure, (("gy", 1), ("gx", 2)), SHEAR + 1)
    slab = padded(widened, (("gz", 0),), 1)
    inner, normals = surface_terms(slab)
    shifts = lax.dynamic_slice(shear, (zero, brick * depth_cells, zero), (VIEWS, depth_cells, 2))
    layers = render_layers(inner, normals, shifts, light, palette, rate, rows, cols)
    moved = lax.dynamic_index_in_dim(offset, brick, 1, keepdims=False)
    blank = jnp.zeros((4, rows + REACH, cols + REACH), jnp.float32)
    canvas = jnp.stack(
        [
            lax.dynamic_update_slice(blank, layers[view], (zero, moved[view, 0], moved[view, 1]))
            for view in range(VIEWS)
        ]
    )
    own_tile = canvas[:, :, :rows, :cols]
    from_above = shifted(canvas[:, :, rows:, :cols], "gy", 1)
    from_left = shifted(canvas[:, :, :rows, cols:], "gx", 1)
    from_diagonal = shifted(canvas[:, :, rows:, cols:], ("gy", "gx"), lax.axis_size("gx") + 1)
    from_diagonal = from_diagonal * (lax.axis_index("gx") > 0).astype(jnp.float32)
    own_tile = own_tile.at[:, :, :REACH, :].add(from_above)
    own_tile = own_tile.at[:, :, :, :REACH].add(from_left)
    own_tile = own_tile.at[:, :, :REACH, :REACH].add(from_diagonal)
    ranking = precedence(order)
    pieces = lax.all_to_all(own_tile[None], "gz", split_axis=3, concat_axis=0, tiled=True)
    depths = pieces[:, :, 3]
    cover = jnp.einsum("vbc,cvyx->bvyx", ranking, depths, precision=lax.Precision.HIGHEST)
    colors = jnp.sum(pieces[:, :, :3] * jnp.exp(-cover)[:, :, None], axis=0)
    opacity = 1.0 - jnp.exp(-jnp.sum(depths, axis=0))
    image = jnp.concatenate([colors, opacity[:, None]], axis=1)
    return image[:, :, None]


class Route:
    def __init__(self, dims, side, step, start, count, slab, half):
        bz = dims[2]
        self.side, self.step, self.half = side, step, half
        self.rows, self.slab = pl.ds(start, count), pl.ds(slab, count)
        self.groups = LANES // (SUB * bz)
        self.tiles = range(start // SUB, (start + count) // SUB)
        self.first = slab // SUB
        self.folds = range(
            self.tiles[0] // self.groups, self.tiles[-1] // self.groups + 1
        )
        self.size = (len(self.tiles) + len(self.folds)) * SUB
        self.base = self.sent = 0

    def there(self, y, ny):
        return y + self.step >= 0 if self.step < 0 else y + self.step < ny

    def comes(self, y, ny):
        return y - self.step < ny if self.step < 0 else y - self.step >= 0

    def wide(self, tile):
        return (tile - self.tiles[0]) * SUB

    def narrow(self, fold):
        return (len(self.tiles) + fold - self.folds[0]) * SUB


def routes_of(dims):
    rows = dims[3]
    strip = rows // 2
    routes = [
        Route(dims, 0, 0, 0, strip + SUB, HALO, 0),
        Route(dims, 0, 1, rows - HALO, HALO, 0, 1),
        Route(dims, 1, 0, strip - HALO, HALO + strip, 0, 0),
        Route(dims, 1, -1, 0, SUB, HALO + strip, 1),
    ]
    sent = 0
    for route in routes:
        route.sent = sent
        sent += route.size
    routes[1].base, routes[3].base = routes[0].size, routes[2].size
    return routes, sent, max(routes[0].size + routes[1].size, routes[2].size + routes[3].size)


MAIN, EDGE, BESIDE, COLS, ENDS, SLOTS = 0, 2, 4, 5, 9, 13
PARTS = 2
BELOW, RIGHT, ACROSS = range(3)


def exchange(
    dims, mine, here, p_ref, m_ref, cols_out, cols_in, ends_out, ends_in, sends, arrivals, ready
):
    ny, nx, bz, rows = dims
    z, y, x = here
    has_left, has_right = x > 0, x < nx - 1
    has_up, has_down = y > 0, y < ny - 1
    routes = routes_of(dims)[0]

    def remote(src, dst, arrival, who):
        return pltpu.make_async_remote_copy(
            src_ref=src,
            dst_ref=dst,
            send_sem=sends,
            recv_sem=arrivals.at[arrival],
            device_id=who,
            device_id_type=MESH,
        )

    def rows_of(brick, route, part):
        start = part * (bz // PARTS) if part else 0
        count = bz if part is None else bz // PARTS
        if part is not None and brick == 0:
            start = bz - start - count
        slot = BESIDE if part is None else (EDGE if route.half else MAIN) + part
        return remote(
            p_ref.at[pl.ds(start, count), route.rows],
            m_ref.at[pl.ds(1 + brick * bz + start, count), route.slab],
            slot, (route.side, y + route.step, x),
        )

    def cols_of(brick, route):
        return remote(
            cols_out.at[pl.ds(route.sent, route.size)],
            cols_in.at[brick, pl.ds(route.base, route.size)],
            COLS + 2 * brick + route.half,
            (route.side, y + route.step, x + 1),
        )

    def ends_of(brick, route):
        return remote(
            ends_out,
            ends_in.at[brick, route.half],
            ENDS + 2 * brick + route.half,
            (route.side, y + route.step, x - 1),
        )

    def rows_out(route, late=False):
        there = route.there(y, ny)
        if route.side != mine:
            parts = (PARTS - 1,) if late else range(PARTS - 1)
            return [(there, rows_of(mine, route, part)) for part in parts]
        return [(there, rows_of(mine, route, None))] if route.half else []

    def cols_sent(same):
        return [
            (jnp.logical_and(r.there(y, ny), has_right), cols_of(mine, r))
            for r in routes
            if (r.side == mine) == same
        ]

    def ends_sent():
        return [(jnp.logical_and(r.there(y, ny), has_left), ends_of(mine, r)) for r in routes]

    def apply(pairs, act):
        for there, copy in pairs:

            @pl.when(there)
            def _():
                act(copy)

    def start(pairs):
        apply(pairs, lambda copy: copy.start())

    def heard(kind, there, count):
        @pl.when(there)
        def _():
            pl.semaphore_wait(ready.at[kind], count)

    mains, own_halo, halos = (
        (routes[2], routes[1], routes[3]) if mine == 0 else (routes[0], routes[3], routes[1])
    )
    next_ones = [1 + there.astype(jnp.int32) for there in (has_down, has_up)]

    def send_first():
        if mine == 0:
            start(rows_out(mains))
            start(rows_out(halos))
        else:
            start(rows_out(mains))
            start(rows_out(own_halo))

    def send_rest():
        if mine == 0:
            start(ends_sent())
            heard(BELOW, has_down, 1)
            start(rows_out(own_halo))
        else:
            start(ends_sent())
            heard(BELOW, has_down, 1)
            start(rows_out(halos))
        heard(RIGHT, has_right, next_ones[mine])
        start(cols_sent(True))
        heard(ACROSS, has_right, next_ones[1 - mine])
        start(cols_sent(False))
        start(rows_out(mains, True) + rows_out(halos, True))

    def receive(brick, parts, sides):
        pairs = []
        for route in routes:
            if route.side != mine:
                continue
            comes = route.comes(y, ny)
            if brick != mine:
                pairs += [(comes, rows_of(brick, route, part)) for part in parts]
            elif route.half:
                pairs += [(comes, rows_of(brick, route, None))]
            if sides:
                pairs += [
                    (jnp.logical_and(comes, has_left), cols_of(brick, route)),
                    (jnp.logical_and(comes, has_right), ends_of(brick, route)),
                ]
        apply(pairs, lambda copy: copy.wait_recv())

    def close():
        for late in (False, True):
            apply(rows_out(mains, late) + rows_out(halos, late), lambda copy: copy.wait_send())
        apply(rows_out(own_halo), lambda copy: copy.wait_send())
        apply(ends_sent() + cols_sent(True) + cols_sent(False), lambda copy: copy.wait_send())

    return send_first, send_rest, receive, close


def partners_of(dims, here, over):
    ny, nx = dims[:2]
    z, y, x = here
    steps = [(z, over, 0), (1 - z, 0, 0)]
    diagonal = z == 1 if over > 0 else z == 0
    yield jnp.logical_and(diagonal, inside_of(dims, y + over, x)), (1 - z, y + over, x)
    steps += [
        (side, step, over)
        for side, step in ((z, -1), (z, 0), (z, 1), (1 - z, 0), (1 - z, 2 * z - 1))
    ]
    for side, step, across in steps:
        yield inside_of(dims, y + step, x + across), (side, y + step, x + across)


def inside_of(dims, y, x):
    ny, nx = dims[:2]
    return jnp.logical_and(
        jnp.logical_and(y >= 0, y < ny), jnp.logical_and(x >= 0, x < nx)
    )


def answers_of(dims, here):
    z, y, x = here
    own = z == 0
    yield jnp.logical_and(own, y > 0), (z, y - 1, x), BELOW
    yield jnp.logical_and(own, y > 0), (1 - z, y - 1, x), BELOW
    for side, kind in ((z, RIGHT), (1 - z, ACROSS)):
        for step in (0, 2 * z - 1):
            yield inside_of(dims, y + step, x - 1), (side, y + step, x - 1), kind


def render(
    dims, light_in, palette_in, rate_in, shear_in, offset_in, order_in, p_ref, out_ref,
    light, palette, rate, shear, offset, order, tile_ref, m_ref, own_ref, cols_in, ends_in,
    cols_out, ends_out, h_ref, r_ref, dm, dh, back, sends, arrivals, ready, local_sems, table_sem,
):
    ny, nx, bz, rows = dims
    strip = rows // 2
    tall = HALO + strip + SUB
    depth = 2 * bz
    blocks = (HALO + strip) // SUB
    wide_lanes = HALO - SUB
    z, y, x = lax.axis_index("gz"), lax.axis_index("gy"), lax.axis_index("gx")
    routes = routes_of(dims)[0]

    tables = [
        pltpu.make_async_copy(source, target, table_sem)
        for source, target in (
            (light_in, light), (palette_in, palette), (rate_in, rate),
            (shear_in, shear), (offset_in, offset), (order_in, order),
        )
    ]
    barrier = pltpu.get_barrier_semaphore()

    def sided(act):
        for mine in range(2):

            @pl.when(z == mine)
            def _():
                act(mine)

    for there, who in partners_of(dims, (z, y, x), 1):

        @pl.when(there)
        def _():
            pl.semaphore_signal(barrier, inc=1, device_id=who, device_id_type=MESH)

    count = 0
    for there, _ in partners_of(dims, (z, y, x), -1):
        count = count + there.astype(jnp.int32)

    steps = [
        exchange(
            dims, mine, (z, y, x), p_ref, m_ref, cols_out, cols_in, ends_out, ends_in,
            sends, arrivals, ready,
        )
        for mine in range(2)
    ]

    def local_slab(mine):
        route = routes[2 * mine]
        return pltpu.make_async_copy(
            p_ref.at[:, route.rows], m_ref.at[pl.ds(1 + mine * bz, bz), route.slab],
            local_sems.at[1],
        )

    local_tile = pltpu.make_async_copy(p_ref, tile_ref, local_sems.at[0])
    local_tile.start()
    sided(lambda mine: local_slab(mine).start())
    for copy in tables:
        copy.start()

    @pl.when(count > 0)
    def _():
        pl.semaphore_wait(barrier, count)

    for there, who, kind in answers_of(dims, (z, y, x)):

        @pl.when(there)
        def _():
            pl.semaphore_signal(ready.at[kind], inc=1, device_id=who, device_id_type=MESH)


    sided(lambda mine: steps[mine][0]())

    empty = jnp.zeros((tall, LANES), jnp.float32)
    for ref in (m_ref, h_ref):
        ref[0] = empty
        ref[depth + 1] = empty

    def blank(mine):
        route = routes[2 * mine + 1]

        @pl.when(jnp.logical_not(route.comes(y, ny)))
        def _():
            m_ref[:, route.slab] = jnp.zeros((depth + 2, len(route.tiles) * SUB, LANES), jnp.float32)
            cols_in[:, route.base : route.base + route.size] = jnp.zeros(
                (2, route.size, LANES), jnp.float32
            )
            ends_in[:, 1] = jnp.zeros((2, SUB, LANES), jnp.float32)

    sided(blank)

    @pl.when(x == 0)
    def _():
        cols_in[...] = jnp.zeros(cols_in.shape, jnp.float32)

    @pl.when(x == nx - 1)
    def _():
        ends_in[...] = jnp.zeros(ends_in.shape, jnp.float32)

    lane = lax.broadcasted_iota(jnp.int32, (SUB, LANES), 1)
    last = lane == LANES - 1
    first = lane == 0
    groups = routes[0].groups
    tiles = rows // SUB

    def cell(j, t):
        return tile_ref[j, t * SUB : (t + 1) * SUB]

    def put(t_or_fold, is_wide, value):
        for route in routes:
            if t_or_fold in (route.tiles if is_wide else route.folds):
                at = route.sent + (route.wide if is_wide else route.narrow)(t_or_fold)
                cols_out[at : at + SUB] = value

    def merged(pieces):
        while len(pieces) > 1:
            pieces = [
                (a[0], jnp.where(lane >= b[0], b[1], a[1]))
                for a, b in zip(pieces[::2], pieces[1::2])
            ] + (pieces[-1:] if len(pieces) % 2 else [])
        return pieces[0][1]

    def turned(value, by):
        return pltpu.roll(value, by % LANES, 1) if by % LANES else value

    local_tile.wait()
    for t in range(tiles):
        put(
            t, True,
            merged(
                [(wide_lanes * j, turned(cell(j, t), wide_lanes * (j + 1))) for j in range(bz)]
            ),
        )
    for fold in range(tiles // groups):
        put(
            fold, False,
            merged(
                [
                    (
                        SUB * (bz * g + j),
                        turned(cell(j, fold * groups + g), SUB * (bz * g + j) + HALO),
                    )
                    for g in range(groups)
                    for j in range(bz)
                ]
            ),
        )
    ends_out[...] = merged(
        [(t * bz + j, turned(cell(j, t), t * bz + j)) for t in range(tiles) for j in range(bz)]
    )

    def unpack(mine, brick):
        for route in routes[2 * mine : 2 * mine + 2]:
            for t in route.tiles:
                row = (route.first + t - route.tiles[0]) * SUB
                at = route.base + route.wide(t)
                wide = cols_in[brick, at : at + SUB]
                at = route.base + route.narrow(t // groups)
                narrow = cols_in[brick, at : at + SUB]
                for j in range(bz):
                    h_ref[1 + brick * bz + j, row : row + SUB] = jnp.where(
                        lane >= LANES - wide_lanes,
                        turned(wide, -wide_lanes * (j + 1)),
                        turned(narrow, -SUB * (bz * (t % groups) + j) - HALO),
                    )
                r_ref[brick, row : row + SUB] = turned(
                    ends_in[brick, route.half], LANES - 1 - t * bz
                )

    def opening(mine):
        _, send_rest, receive, _ = steps[mine]
        send_rest()
        local_slab(mine).wait()
        receive(mine, (), True)
        own_ref[...] = m_ref[1 + mine * bz : 1 + (mine + 1) * bz]
        unpack(mine, mine)

    def middle(mine):
        receive = steps[mine][2]
        receive(1 - mine, range(PARTS - 1), True)
        unpack(mine, 1 - mine)

    def ending(mine):
        receive = steps[mine][2]
        receive(1 - mine, (PARTS - 1,), False)

    sided(opening)
    for copy in tables:
        copy.wait()

    towards = []
    for w in range(VIEWS):
        a, b, c = light[w, 0], light[w, 1], light[w, 2]
        inverse = lax.rsqrt(jnp.full((SUB, LANES), a * a + b * b + c * c + 1.0, jnp.float32))
        towards.append((a * inverse, b * inverse, c * inverse))

    def slopes(k, carry):
        for i in range(blocks):
            top = i * SUB
            here = m_ref[k + 1, top + 1 : top + 1 + SUB]
            side = h_ref[k + 1, top + 1 : top + 1 + SUB]
            beyond = pltpu.roll(
                r_ref[k // bz, top + 1 : top + 1 + SUB], (LANES - k % bz) % LANES, 1
            )
            here_r, here_l = pltpu.roll(here, LANES - 1, 1), pltpu.roll(here, 1, 1)
            side_r, side_l = pltpu.roll(side, LANES - 1, 1), pltpu.roll(side, 1, 1)
            for ref, cols, dots in (
                (m_ref, jnp.where(last, beyond, here_r) - jnp.where(first, side_l, here_l), dm),
                (h_ref, jnp.where(last, here_r, side_r) - side_l, dh),
            ):
                deep = ref[k + 2, top + 1 : top + 1 + SUB] - ref[k, top + 1 : top + 1 + SUB]
                down = ref[k + 1, top + 2 : top + 2 + SUB] - ref[k + 1, top : top + SUB]
                half = 0.5 * lax.rsqrt(0.25 * (deep * deep + down * down + cols * cols) + 1.0)
                deep, down, cols = deep * half, down * half, cols * half
                for w in range(VIEWS):
                    a, b, c = towards[w]
                    dots[w, k, top : top + SUB] = deep * a + down * b + cols * c
        return carry

    tile = 32
    per_view = strip // tile
    base_row = y * rows + z * strip
    base_col = x * LANES
    lanes = lax.broadcasted_iota(jnp.int32, (tile, LANES), 1)
    rows_at = lax.broadcasted_iota(jnp.int32, (tile, LANES), 0)
    bias = [0.5 * palette[0, c] for c in range(3)]
    gain = [0.5 * palette[1, c] for c in range(3)]

    def march(w, top, brick, cells, start, colors, through):
        ambient = jnp.zeros((tile, LANES), jnp.float32)
        rate2 = rate[w] * (-math.log2(math.e))
        off_r, off_c = offset[brick, 0, w], offset[brick, 1, w]
        inside = jnp.logical_and(rows_at >= off_r - base_row - top, lanes >= off_c - base_col)
        fall = jnp.where(inside, rate2, 0.0)
        for j in range(bz):
            k = brick * bz + j
            sr = off_r + shear[w, 0, k]
            sc = off_c + shear[w, 1, k]
            at = HALO + top - sr
            wrap = lanes >= LANES - sc
            value = jnp.where(wrap, h_ref[k + 1, pl.ds(at, tile)], cells[start + j, pl.ds(at, tile)])
            dot = jnp.where(wrap, dh[w, k, pl.ds(at - 1, tile)], dm[w, k, pl.ds(at - 1, tile)])
            value = pltpu.roll(value, sc, 1)
            dot = pltpu.roll(dot, sc, 1)
            kept = jnp.exp2(fall * (1.0 + jnp.tanh(value)))
            weight = (0.125 + 0.375 * dot * dot) * ((1.0 - kept) * through)
            through = through * kept
            ambient = ambient + weight
            colors = [
                colors[c] + weight * jnp.tanh(bias[c] + gain[c] * value) for c in range(3)
            ]
        return [color + ambient for color in colors], through

    def views(act):
        def one(step, carry):
            act(step // per_view, (step % per_view) * tile)
            return carry

        lax.fori_loop(0, VIEWS * per_view, one, 0, unroll=VIEWS * per_view)

    def own_layer(w, top):
        at = pl.ds(top, tile)
        zero = jnp.zeros((tile, LANES), jnp.float32)
        colors, through = march(w, top, z, own_ref, 0, [zero] * 3, zero + 1.0)
        ahead = order[0, w] == z
        for c in range(3):
            out_ref[w, c, at] = jnp.where(ahead, colors[c], 0.0)
            back[w, c, at] = jnp.where(ahead, 0.0, colors[c])
        out_ref[w, 3, at] = jnp.where(ahead, through, 1.0)
        back[w, 3, at] = jnp.where(ahead, 1.0, through)

    def other_layer(w, top):
        at = pl.ds(top, tile)
        colors, through = march(
            w, top, 1 - z, m_ref, 1 + (1 - z) * bz, [out_ref[w, c, at] for c in range(3)],
            out_ref[w, 3, at],
        )
        for c in range(3):
            out_ref[w, c, at] = colors[c] + through * back[w, c, at]
        out_ref[w, 3, at] = 1.0 - through * back[w, 3, at]

    def each(start, stop):
        lax.fori_loop(start, stop, slopes, 0)

    each(z * (bz + 1), z * (bz + 1) + bz - 1)
    sided(middle)
    each(bz - 1, bz + 1)
    views(own_layer)
    sided(ending)
    each((1 - z) * (bz + 1), (1 - z) * (bz + 1) + bz - 1)
    views(other_layer)
    sided(lambda mine: steps[mine][3]())


def two_bricks(mesh, pressure, light, palette, rate, shear, offset, order):
    bz, rows, cols = pressure.shape
    dims = (mesh.shape["gy"], mesh.shape["gx"], bz, rows)
    strip = rows // 2
    tall = HALO + strip + SUB
    depth = 2 * bz
    vmem = pl.BlockSpec(memory_space=pltpu.VMEM)
    hbm = pl.BlockSpec(memory_space=pltpu.HBM)
    f32 = jnp.float32
    _, sent, got = routes_of(dims)
    tables = (
        light,
        palette.T,
        rate,
        jnp.transpose(shear, (0, 2, 1)),
        jnp.transpose(offset, (1, 2, 0)),
        order.T,
    )
    image = pl.pallas_call(
        functools.partial(render, dims),
        out_shape=jax.ShapeDtypeStruct((VIEWS, 4, strip, LANES), f32),
        in_specs=[hbm] * 7,
        out_specs=vmem,
        scratch_shapes=[
            *[pltpu.SMEM(table.shape, table.dtype) for table in tables],
            pltpu.VMEM((bz, rows, LANES), f32),
            pltpu.VMEM((depth + 2, tall, LANES), f32),
            pltpu.VMEM((bz, tall, LANES), f32),
            pltpu.VMEM((2, got, LANES), f32),
            pltpu.VMEM((2, 2, SUB, LANES), f32),
            pltpu.VMEM((sent, LANES), f32),
            pltpu.VMEM((SUB, LANES), f32),
            pltpu.VMEM((depth + 2, tall, LANES), f32),
            pltpu.VMEM((2, tall, LANES), f32),
            pltpu.VMEM((VIEWS, depth, HALO + strip, LANES), f32),
            pltpu.VMEM((VIEWS, depth, HALO + strip, LANES), f32),
            pltpu.VMEM((VIEWS, 4, strip, LANES), f32),
            pltpu.SemaphoreType.DMA,
            pltpu.SemaphoreType.DMA((SLOTS,)),
            pltpu.SemaphoreType.REGULAR((3,)),
            pltpu.SemaphoreType.DMA((2,)),
            pltpu.SemaphoreType.DMA,
        ],
        compiler_params=pltpu.CompilerParams(collective_id=0, has_side_effects=True, vmem_limit_bytes=12 << 20),
        name="render",
    )(
        *[pltpu.with_memory_space_constraint(t, pltpu.HBM) for t in (*tables, pressure)]
    )
    return image[:, :, None]


def fits(mesh, shape):
    bz, rows, cols = shape
    return (
        mesh.shape["gz"] == 2
        and cols == LANES
        and rows % 64 == 0
        and 2 * HALO <= rows <= LANES
        and bz * (HALO - SUB) == LANES
        and bz * (rows // SUB) <= LANES
    )


def on_device(mesh, pressure, *rest):
    if fits(mesh, pressure.shape):
        return two_bricks(mesh, pressure, *rest)
    return many_bricks(pressure, *rest)


def solution(mesh):
    return jax.shard_map(
        functools.partial(on_device, mesh),
        mesh=mesh,
        in_specs=(P("gz", "gy", "gx"), P(), P(), P(), P(), P(), P()),
        out_specs=P(None, None, "gz", "gy", "gx"),
        check_vma=False,
    )
```

```python
import functools
import math

import jax
import jax.numpy as jnp
from jax import lax
from jax.experimental import pallas as pl
from jax.experimental.pallas import tpu as pltpu
from jax.sharding import PartitionSpec as P

VIEWS = 4
SHEAR = 8
REACH = 32
HALO = SHEAR + REACH
SUB = 8
LANES = 128
MESH = pl.DeviceIdType.MESH


def padded(cells, sides, width):
    for axis, dim in sides:
        count = lax.axis_size(axis)
        ends = count - 1
        head = lax.slice_in_dim(cells, 0, width, axis=dim)
        tail = lax.slice_in_dim(cells, cells.shape[dim] - width, cells.shape[dim], axis=dim)
        cells = jnp.concatenate(
            [
                lax.ppermute(tail, axis, [(i, (i + 1) % count) for i in range(ends)]),
                cells,
                lax.ppermute(head, axis, [((i + 1) % count, i) for i in range(ends)]),
            ],
            axis=dim,
        )
    return cells


def shifted(value, axis, steps):
    count = lax.axis_size(axis)
    first, last = (max(0, -steps), min(count, count - steps))
    return lax.ppermute(value, axis, [(source, source + steps) for source in range(first, last)])


def surface_terms(slab):
    inner = slab[1:-1, 1:-1, 1:-1]
    grad_depth = 0.5 * (slab[2:, 1:-1, 1:-1] - slab[:-2, 1:-1, 1:-1])
    grad_rows = 0.5 * (slab[1:-1, 2:, 1:-1] - slab[1:-1, :-2, 1:-1])
    grad_cols = 0.5 * (slab[1:-1, 1:-1, 2:] - slab[1:-1, 1:-1, :-2])
    factor = lax.rsqrt(
        grad_depth * grad_depth + grad_rows * grad_rows + grad_cols * grad_cols + 1.0
    )
    return (inner, (grad_depth * factor, grad_rows * factor, grad_cols * factor))


def render_layers(inner, normals, shifts, light, palette, rate, rows, cols):
    lengths = jnp.sqrt(jnp.sum(light * light, axis=1, keepdims=True) + 1.0)
    towards = light / lengths
    offsets = palette[:, 0][:, None, None]
    slopes = palette[:, 1][:, None, None]
    layers = []
    for view in range(light.shape[0]):

        def advance(carry, items):
            color, depth = carry
            value_slab, normal_depth, normal_rows, normal_cols, moved = items
            start = (SHEAR - moved[0], SHEAR - moved[1])
            value = lax.dynamic_slice(value_slab, start, (rows, cols))
            dot = (
                lax.dynamic_slice(normal_depth, start, (rows, cols)) * towards[view, 0]
                + lax.dynamic_slice(normal_rows, start, (rows, cols)) * towards[view, 1]
                + lax.dynamic_slice(normal_cols, start, (rows, cols)) * towards[view, 2]
            )
            shade = 0.25 + 0.75 * dot * dot
            density = rate[view] * (1.0 + jnp.tanh(value))
            alpha = 1.0 - jnp.exp(-density)
            weight = alpha * jnp.exp(-depth)
            hues = jax.nn.sigmoid(offsets + slopes * value[None]) * shade[None]
            return ((color + hues * weight[None], depth + density), None)

        start_carry = (
            jnp.zeros((3, rows, cols), jnp.float32),
            jnp.zeros((rows, cols), jnp.float32),
        )
        (color, depth), _ = lax.scan(
            advance, start_carry, (inner, normals[0], normals[1], normals[2], shifts[view])
        )
        layers.append(jnp.concatenate([color, depth[None]], axis=0))
    return jnp.stack(layers)


def precedence(order):
    bricks = order.shape[1]
    onehot = (order[:, :, None] == jnp.arange(bricks, dtype=jnp.int32)[None, None, :]).astype(
        jnp.float32
    )
    ranks = jnp.sum(onehot * jnp.arange(bricks, dtype=jnp.float32)[None, :, None], axis=1)
    return (ranks[:, None, :] < ranks[:, :, None]).astype(jnp.float32)


def many_bricks(pressure, light, palette, rate, shear, offset, order):
    depth_cells, rows, cols = pressure.shape
    brick = lax.axis_index("gz")
    zero = jnp.zeros((), jnp.int32)
    widened = padded(pressure, (("gy", 1), ("gx", 2)), SHEAR + 1)
    slab = padded(widened, (("gz", 0),), 1)
    inner, normals = surface_terms(slab)
    shifts = lax.dynamic_slice(shear, (zero, brick * depth_cells, zero), (VIEWS, depth_cells, 2))
    layers = render_layers(inner, normals, shifts, light, palette, rate, rows, cols)
    moved = lax.dynamic_index_in_dim(offset, brick, 1, keepdims=False)
    blank = jnp.zeros((4, rows + REACH, cols + REACH), jnp.float32)
    canvas = jnp.stack(
        [
            lax.dynamic_update_slice(blank, layers[view], (zero, moved[view, 0], moved[view, 1]))
            for view in range(VIEWS)
        ]
    )
    own_tile = canvas[:, :, :rows, :cols]
    from_above = shifted(canvas[:, :, rows:, :cols], "gy", 1)
    from_left = shifted(canvas[:, :, :rows, cols:], "gx", 1)
    from_diagonal = shifted(canvas[:, :, rows:, cols:], ("gy", "gx"), lax.axis_size("gx") + 1)
    from_diagonal = from_diagonal * (lax.axis_index("gx") > 0).astype(jnp.float32)
    own_tile = own_tile.at[:, :, :REACH, :].add(from_above)
    own_tile = own_tile.at[:, :, :, :REACH].add(from_left)
    own_tile = own_tile.at[:, :, :REACH, :REACH].add(from_diagonal)
    ranking = precedence(order)
    pieces = lax.all_to_all(own_tile[None], "gz", split_axis=3, concat_axis=0, tiled=True)
    depths = pieces[:, :, 3]
    cover = jnp.einsum("vbc,cvyx->bvyx", ranking, depths, precision=lax.Precision.HIGHEST)
    colors = jnp.sum(pieces[:, :, :3] * jnp.exp(-cover)[:, :, None], axis=0)
    opacity = 1.0 - jnp.exp(-jnp.sum(depths, axis=0))
    image = jnp.concatenate([colors, opacity[:, None]], axis=1)
    return image[:, :, None]


class Route:
    def __init__(self, dims, side, step, start, count, slab, half):
        bz = dims[2]
        self.side, self.step, self.half = side, step, half
        self.rows, self.slab = pl.ds(start, count), pl.ds(slab, count)
        self.groups = LANES // (SUB * bz)
        self.tiles = range(start // SUB, (start + count) // SUB)
        self.first = slab // SUB
        self.folds = range(
            self.tiles[0] // self.groups, self.tiles[-1] // self.groups + 1
        )
        self.size = (len(self.tiles) + len(self.folds)) * SUB
        self.base = self.sent = 0

    def there(self, y, ny):
        return y + self.step >= 0 if self.step < 0 else y + self.step < ny

    def comes(self, y, ny):
        return y - self.step < ny if self.step < 0 else y - self.step >= 0

    def wide(self, tile):
        return (tile - self.tiles[0]) * SUB

    def narrow(self, fold):
        return (len(self.tiles) + fold - self.folds[0]) * SUB


def routes_of(dims):
    rows = dims[3]
    strip = rows // 2
    routes = [
        Route(dims, 0, 0, 0, strip + SUB, HALO, 0),
        Route(dims, 0, 1, rows - HALO, HALO, 0, 1),
        Route(dims, 1, 0, strip - HALO, HALO + strip, 0, 0),
        Route(dims, 1, -1, 0, SUB, HALO + strip, 1),
    ]
    sent = 0
    for route in routes:
        route.sent = sent
        sent += route.size
    routes[1].base, routes[3].base = routes[0].size, routes[2].size
    return routes, sent, max(routes[0].size + routes[1].size, routes[2].size + routes[3].size)


MAIN, EDGE, BESIDE, COLS, ENDS, SLOTS = 0, 3, 6, 7, 11, 15
PARTS = 3
BELOW, RIGHT, ACROSS = range(3)


def exchange(
    dims, mine, here, p_ref, m_ref, cols_out, cols_in, ends_out, ends_in, sends, arrivals, ready
):
    ny, nx, bz, rows = dims
    z, y, x = here
    has_left, has_right = x > 0, x < nx - 1
    has_up, has_down = y > 0, y < ny - 1
    routes = routes_of(dims)[0]

    def remote(src, dst, arrival, who):
        return pltpu.make_async_remote_copy(
            src_ref=src,
            dst_ref=dst,
            send_sem=sends,
            recv_sem=arrivals.at[arrival],
            device_id=who,
            device_id_type=MESH,
        )

    def rows_of(brick, route, part):
        first = bz - PARTS + 1
        start = first + part - 1 if part else 0
        count = bz if part is None else 1 if part else first
        if part is not None and brick == 0:
            start = bz - start - count
        slot = BESIDE if part is None else (EDGE if route.half else MAIN) + part
        return remote(
            p_ref.at[pl.ds(start, count), route.rows],
            m_ref.at[pl.ds(1 + brick * bz + start, count), route.slab],
            slot, (route.side, y + route.step, x),
        )

    def cols_of(brick, route):
        return remote(
            cols_out.at[pl.ds(route.sent, route.size)],
            cols_in.at[brick, pl.ds(route.base, route.size)],
            COLS + 2 * brick + route.half,
            (route.side, y + route.step, x + 1),
        )

    def ends_of(brick, route):
        return remote(
            ends_out,
            ends_in.at[brick, route.half],
            ENDS + 2 * brick + route.half,
            (route.side, y + route.step, x - 1),
        )

    def rows_out(route, part=0):
        there = route.there(y, ny)
        if route.side != mine:
            return [(there, rows_of(mine, route, part))]
        return [(there, rows_of(mine, route, None))] if route.half else []

    def cols_sent(same):
        return [
            (jnp.logical_and(r.there(y, ny), has_right), cols_of(mine, r))
            for r in routes
            if (r.side == mine) == same
        ]

    def ends_sent():
        return [(jnp.logical_and(r.there(y, ny), has_left), ends_of(mine, r)) for r in routes]

    def apply(pairs, act):
        for there, copy in pairs:

            @pl.when(there)
            def _():
                act(copy)

    def start(pairs):
        apply(pairs, lambda copy: copy.start())

    def heard(kind, there, count):
        @pl.when(there)
        def _():
            pl.semaphore_wait(ready.at[kind], count)

    mains, own_halo, halos = (
        (routes[2], routes[1], routes[3]) if mine == 0 else (routes[0], routes[3], routes[1])
    )
    next_ones = [1 + there.astype(jnp.int32) for there in (has_down, has_up)]

    def send_first():
        if mine == 0:
            start(rows_out(mains))
            start(rows_out(halos))
        else:
            start(rows_out(mains))
            start(rows_out(own_halo))

    def send_rest():
        if mine == 0:
            start(ends_sent())
            heard(BELOW, has_down, 1)
            start(rows_out(own_halo))
        else:
            start(ends_sent())
            heard(BELOW, has_down, 1)
            start(rows_out(halos))
        heard(RIGHT, has_right, next_ones[mine])
        start(cols_sent(True))
        heard(ACROSS, has_right, next_ones[1 - mine])
        start(cols_sent(False))
        start(rows_out(mains, 1) + rows_out(halos, 1))

    def send_last():
        start(rows_out(mains, 2) + rows_out(halos, 2))

    def receive(brick, parts, sides):
        pairs = []
        for route in routes:
            if route.side != mine:
                continue
            comes = route.comes(y, ny)
            if brick != mine:
                pairs += [(comes, rows_of(brick, route, part)) for part in parts]
            elif route.half:
                pairs += [(comes, rows_of(brick, route, None))]
            if sides:
                pairs += [
                    (jnp.logical_and(comes, has_left), cols_of(brick, route)),
                    (jnp.logical_and(comes, has_right), ends_of(brick, route)),
                ]
        apply(pairs, lambda copy: copy.wait_recv())

    def close():
        for part in range(PARTS):
            apply(rows_out(mains, part) + rows_out(halos, part), lambda copy: copy.wait_send())
        apply(rows_out(own_halo), lambda copy: copy.wait_send())
        apply(ends_sent() + cols_sent(True) + cols_sent(False), lambda copy: copy.wait_send())

    return send_first, send_rest, send_last, receive, close


def partners_of(dims, here, over):
    ny, nx = dims[:2]
    z, y, x = here
    steps = [(z, over, 0), (1 - z, 0, 0)]
    diagonal = z == 1 if over > 0 else z == 0
    yield jnp.logical_and(diagonal, inside_of(dims, y + over, x)), (1 - z, y + over, x)
    steps += [
        (side, step, over)
        for side, step in ((z, -1), (z, 0), (z, 1), (1 - z, 0), (1 - z, 2 * z - 1))
    ]
    for side, step, across in steps:
        yield inside_of(dims, y + step, x + across), (side, y + step, x + across)


def inside_of(dims, y, x):
    ny, nx = dims[:2]
    return jnp.logical_and(
        jnp.logical_and(y >= 0, y < ny), jnp.logical_and(x >= 0, x < nx)
    )


def answers_of(dims, here):
    z, y, x = here
    own = z == 0
    yield jnp.logical_and(own, y > 0), (z, y - 1, x), BELOW
    yield jnp.logical_and(own, y > 0), (1 - z, y - 1, x), BELOW
    for side, kind in ((z, RIGHT), (1 - z, ACROSS)):
        for step in (0, 2 * z - 1):
            yield inside_of(dims, y + step, x - 1), (side, y + step, x - 1), kind


def render(
    dims, light_in, palette_in, rate_in, shear_in, offset_in, order_in, p_ref, out_ref,
    light, palette, rate, shear, offset, order, tile_ref, m_ref, own_ref, cols_in, ends_in,
    cols_out, ends_out, h_ref, r_ref, dm, dh, back, sends, arrivals, ready, local_sems, table_sem,
):
    ny, nx, bz, rows = dims
    strip = rows // 2
    tall = HALO + strip + SUB
    depth = 2 * bz
    blocks = (HALO + strip) // SUB
    wide_lanes = HALO - SUB
    z, y, x = lax.axis_index("gz"), lax.axis_index("gy"), lax.axis_index("gx")
    routes = routes_of(dims)[0]

    tables = [
        pltpu.make_async_copy(source, target, table_sem)
        for source, target in (
            (light_in, light), (palette_in, palette), (rate_in, rate),
            (shear_in, shear), (offset_in, offset), (order_in, order),
        )
    ]
    barrier = pltpu.get_barrier_semaphore()

    def sided(act):
        for mine in range(2):

            @pl.when(z == mine)
            def _():
                act(mine)

    for there, who in partners_of(dims, (z, y, x), 1):

        @pl.when(there)
        def _():
            pl.semaphore_signal(barrier, inc=1, device_id=who, device_id_type=MESH)

    count = 0
    for there, _ in partners_of(dims, (z, y, x), -1):
        count = count + there.astype(jnp.int32)

    steps = [
        exchange(
            dims, mine, (z, y, x), p_ref, m_ref, cols_out, cols_in, ends_out, ends_in,
            sends, arrivals, ready,
        )
        for mine in range(2)
    ]

    def local_slab(mine):
        route = routes[2 * mine]
        return pltpu.make_async_copy(
            p_ref.at[:, route.rows], m_ref.at[pl.ds(1 + mine * bz, bz), route.slab],
            local_sems.at[1],
        )

    local_tile = pltpu.make_async_copy(p_ref, tile_ref, local_sems.at[0])
    local_tile.start()
    sided(lambda mine: local_slab(mine).start())
    for copy in tables:
        copy.start()

    @pl.when(count > 0)
    def _():
        pl.semaphore_wait(barrier, count)

    for there, who, kind in answers_of(dims, (z, y, x)):

        @pl.when(there)
        def _():
            pl.semaphore_signal(ready.at[kind], inc=1, device_id=who, device_id_type=MESH)


    sided(lambda mine: steps[mine][0]())

    empty = jnp.zeros((tall, LANES), jnp.float32)
    for ref in (m_ref, h_ref):
        ref[0] = empty
        ref[depth + 1] = empty

    def blank(mine):
        route = routes[2 * mine + 1]

        @pl.when(jnp.logical_not(route.comes(y, ny)))
        def _():
            m_ref[:, route.slab] = jnp.zeros((depth + 2, len(route.tiles) * SUB, LANES), jnp.float32)
            cols_in[:, route.base : route.base + route.size] = jnp.zeros(
                (2, route.size, LANES), jnp.float32
            )
            ends_in[:, 1] = jnp.zeros((2, SUB, LANES), jnp.float32)

    sided(blank)

    @pl.when(x == 0)
    def _():
        cols_in[...] = jnp.zeros(cols_in.shape, jnp.float32)

    @pl.when(x == nx - 1)
    def _():
        ends_in[...] = jnp.zeros(ends_in.shape, jnp.float32)

    lane = lax.broadcasted_iota(jnp.int32, (SUB, LANES), 1)
    last = lane == LANES - 1
    first = lane == 0
    groups = routes[0].groups
    tiles = rows // SUB

    def cell(j, t):
        return tile_ref[j, t * SUB : (t + 1) * SUB]

    def put(t_or_fold, is_wide, value):
        for route in routes:
            if t_or_fold in (route.tiles if is_wide else route.folds):
                at = route.sent + (route.wide if is_wide else route.narrow)(t_or_fold)
                cols_out[at : at + SUB] = value

    def merged(pieces):
        while len(pieces) > 1:
            pieces = [
                (a[0], jnp.where(lane >= b[0], b[1], a[1]))
                for a, b in zip(pieces[::2], pieces[1::2])
            ] + (pieces[-1:] if len(pieces) % 2 else [])
        return pieces[0][1]

    def turned(value, by):
        return pltpu.roll(value, by % LANES, 1) if by % LANES else value

    local_tile.wait()
    for t in range(tiles):
        put(
            t, True,
            merged(
                [(wide_lanes * j, turned(cell(j, t), wide_lanes * (j + 1))) for j in range(bz)]
            ),
        )
    for fold in range(tiles // groups):
        put(
            fold, False,
            merged(
                [
                    (
                        SUB * (bz * g + j),
                        turned(cell(j, fold * groups + g), SUB * (bz * g + j) + HALO),
                    )
                    for g in range(groups)
                    for j in range(bz)
                ]
            ),
        )
    ends_out[...] = merged(
        [(t * bz + j, turned(cell(j, t), t * bz + j)) for t in range(tiles) for j in range(bz)]
    )

    def unpack(mine, brick):
        for route in routes[2 * mine : 2 * mine + 2]:
            for t in route.tiles:
                row = (route.first + t - route.tiles[0]) * SUB
                at = route.base + route.wide(t)
                wide = cols_in[brick, at : at + SUB]
                at = route.base + route.narrow(t // groups)
                narrow = cols_in[brick, at : at + SUB]
                for j in range(bz):
                    h_ref[1 + brick * bz + j, row : row + SUB] = jnp.where(
                        lane >= LANES - wide_lanes,
                        turned(wide, -wide_lanes * (j + 1)),
                        turned(narrow, -SUB * (bz * (t % groups) + j) - HALO),
                    )
                r_ref[brick, row : row + SUB] = turned(
                    ends_in[brick, route.half], LANES - 1 - t * bz
                )

    def opening(mine):
        _, send_rest, send_last, receive, _ = steps[mine]
        send_rest()
        local_slab(mine).wait()
        receive(mine, (), True)
        send_last()
        own_ref[...] = m_ref[1 + mine * bz : 1 + (mine + 1) * bz]
        unpack(mine, mine)

    def middle(mine):
        receive = steps[mine][3]
        receive(1 - mine, (0,), True)
        unpack(mine, 1 - mine)

    def ending(mine, part):
        receive = steps[mine][3]
        receive(1 - mine, (part,), False)

    sided(opening)
    for copy in tables:
        copy.wait()

    towards = []
    for w in range(VIEWS):
        a, b, c = light[w, 0], light[w, 1], light[w, 2]
        inverse = lax.rsqrt(jnp.full((SUB, LANES), a * a + b * b + c * c + 1.0, jnp.float32))
        towards.append((a * inverse, b * inverse, c * inverse))

    def slopes(k, carry):
        for i in range(blocks):
            top = i * SUB
            here = m_ref[k + 1, top + 1 : top + 1 + SUB]
            side = h_ref[k + 1, top + 1 : top + 1 + SUB]
            beyond = pltpu.roll(
                r_ref[k // bz, top + 1 : top + 1 + SUB], (LANES - k % bz) % LANES, 1
            )
            here_r, here_l = pltpu.roll(here, LANES - 1, 1), pltpu.roll(here, 1, 1)
            side_r, side_l = pltpu.roll(side, LANES - 1, 1), pltpu.roll(side, 1, 1)
            for ref, cols, dots in (
                (m_ref, jnp.where(last, beyond, here_r) - jnp.where(first, side_l, here_l), dm),
                (h_ref, jnp.where(last, here_r, side_r) - side_l, dh),
            ):
                deep = ref[k + 2, top + 1 : top + 1 + SUB] - ref[k, top + 1 : top + 1 + SUB]
                down = ref[k + 1, top + 2 : top + 2 + SUB] - ref[k + 1, top : top + SUB]
                half = 0.5 * lax.rsqrt(0.25 * (deep * deep + down * down + cols * cols) + 1.0)
                deep, down, cols = deep * half, down * half, cols * half
                for w in range(VIEWS):
                    a, b, c = towards[w]
                    dots[w, k, top : top + SUB] = deep * a + down * b + cols * c
        return carry

    tile = 32
    per_view = strip // tile
    base_row = y * rows + z * strip
    base_col = x * LANES
    lanes = lax.broadcasted_iota(jnp.int32, (tile, LANES), 1)
    rows_at = lax.broadcasted_iota(jnp.int32, (tile, LANES), 0)
    bias = [0.5 * palette[0, c] for c in range(3)]
    gain = [0.5 * palette[1, c] for c in range(3)]

    def march(w, top, brick, cells, start, colors, through):
        ambient = jnp.zeros((tile, LANES), jnp.float32)
        rate2 = rate[w] * (-math.log2(math.e))
        off_r, off_c = offset[brick, 0, w], offset[brick, 1, w]
        inside = jnp.logical_and(rows_at >= off_r - base_row - top, lanes >= off_c - base_col)
        fall = jnp.where(inside, rate2, 0.0)
        for j in range(bz):
            k = brick * bz + j
            sr = off_r + shear[w, 0, k]
            sc = off_c + shear[w, 1, k]
            at = HALO + top - sr
            wrap = lanes >= LANES - sc
            value = jnp.where(wrap, h_ref[k + 1, pl.ds(at, tile)], cells[start + j, pl.ds(at, tile)])
            dot = jnp.where(wrap, dh[w, k, pl.ds(at - 1, tile)], dm[w, k, pl.ds(at - 1, tile)])
            value = pltpu.roll(value, sc, 1)
            dot = pltpu.roll(dot, sc, 1)
            kept = jnp.exp2(fall * (1.0 + jnp.tanh(value)))
            weight = (0.125 + 0.375 * dot * dot) * ((1.0 - kept) * through)
            through = through * kept
            ambient = ambient + weight
            colors = [
                colors[c] + weight * jnp.tanh(bias[c] + gain[c] * value) for c in range(3)
            ]
        return [color + ambient for color in colors], through

    def views(act):
        def one(step, carry):
            act(step // per_view, (step % per_view) * tile)
            return carry

        lax.fori_loop(0, VIEWS * per_view, one, 0, unroll=VIEWS * per_view)

    def own_layer(w, top):
        at = pl.ds(top, tile)
        zero = jnp.zeros((tile, LANES), jnp.float32)
        colors, through = march(w, top, z, own_ref, 0, [zero] * 3, zero + 1.0)
        ahead = order[0, w] == z
        for c in range(3):
            out_ref[w, c, at] = jnp.where(ahead, colors[c], 0.0)
            back[w, c, at] = jnp.where(ahead, 0.0, colors[c])
        out_ref[w, 3, at] = jnp.where(ahead, through, 1.0)
        back[w, 3, at] = jnp.where(ahead, 1.0, through)

    def other_layer(w, top):
        at = pl.ds(top, tile)
        colors, through = march(
            w, top, 1 - z, m_ref, 1 + (1 - z) * bz, [out_ref[w, c, at] for c in range(3)],
            out_ref[w, 3, at],
        )
        for c in range(3):
            out_ref[w, c, at] = colors[c] + through * back[w, c, at]
        out_ref[w, 3, at] = 1.0 - through * back[w, 3, at]

    def each(start, stop):
        lax.fori_loop(start, stop, slopes, 0)

    each(z * (bz + 1), z * (bz + 1) + bz - 1)
    sided(middle)
    each(bz - 1, bz + 1)
    views(own_layer)
    sided(lambda mine: ending(mine, 1))
    each(bz + 1 - 3 * z, bz + 2 - 3 * z)
    sided(lambda mine: ending(mine, 2))
    each((1 - z) * (depth - 2), (1 - z) * (depth - 2) + 2)
    views(other_layer)
    sided(lambda mine: steps[mine][4]())


def two_bricks(mesh, pressure, light, palette, rate, shear, offset, order):
    bz, rows, cols = pressure.shape
    dims = (mesh.shape["gy"], mesh.shape["gx"], bz, rows)
    strip = rows // 2
    tall = HALO + strip + SUB
    depth = 2 * bz
    vmem = pl.BlockSpec(memory_space=pltpu.VMEM)
    hbm = pl.BlockSpec(memory_space=pltpu.HBM)
    f32 = jnp.float32
    _, sent, got = routes_of(dims)
    tables = (
        light,
        palette.T,
        rate,
        jnp.transpose(shear, (0, 2, 1)),
        jnp.transpose(offset, (1, 2, 0)),
        order.T,
    )
    image = pl.pallas_call(
        functools.partial(render, dims),
        out_shape=jax.ShapeDtypeStruct((VIEWS, 4, strip, LANES), f32),
        in_specs=[hbm] * 7,
        out_specs=vmem,
        scratch_shapes=[
            *[pltpu.SMEM(table.shape, table.dtype) for table in tables],
            pltpu.VMEM((bz, rows, LANES), f32),
            pltpu.VMEM((depth + 2, tall, LANES), f32),
            pltpu.VMEM((bz, tall, LANES), f32),
            pltpu.VMEM((2, got, LANES), f32),
            pltpu.VMEM((2, 2, SUB, LANES), f32),
            pltpu.VMEM((sent, LANES), f32),
            pltpu.VMEM((SUB, LANES), f32),
            pltpu.VMEM((depth + 2, tall, LANES), f32),
            pltpu.VMEM((2, tall, LANES), f32),
            pltpu.VMEM((VIEWS, depth, HALO + strip, LANES), f32),
            pltpu.VMEM((VIEWS, depth, HALO + strip, LANES), f32),
            pltpu.VMEM((VIEWS, 4, strip, LANES), f32),
            pltpu.SemaphoreType.DMA,
            pltpu.SemaphoreType.DMA((SLOTS,)),
            pltpu.SemaphoreType.REGULAR((3,)),
            pltpu.SemaphoreType.DMA((2,)),
            pltpu.SemaphoreType.DMA,
        ],
        compiler_params=pltpu.CompilerParams(collective_id=0, has_side_effects=True, vmem_limit_bytes=12 << 20),
        name="render",
    )(
        *[pltpu.with_memory_space_constraint(t, pltpu.HBM) for t in (*tables, pressure)]
    )
    return image[:, :, None]


def fits(mesh, shape):
    bz, rows, cols = shape
    return (
        mesh.shape["gz"] == 2
        and cols == LANES
        and rows % 64 == 0
        and 2 * HALO <= rows <= LANES
        and bz * (HALO - SUB) == LANES
        and bz * (rows // SUB) <= LANES
    )


def on_device(mesh, pressure, *rest):
    if fits(mesh, pressure.shape):
        return two_bricks(mesh, pressure, *rest)
    return many_bricks(pressure, *rest)


def solution(mesh):
    return jax.shard_map(
        functools.partial(on_device, mesh),
        mesh=mesh,
        in_specs=(P("gz", "gy", "gx"), P(), P(), P(), P(), P(), P()),
        out_specs=P(None, None, "gz", "gy", "gx"),
        check_vma=False,
    )
```

```python
import functools
import math

import jax
import jax.numpy as jnp
from jax import lax
from jax.experimental import pallas as pl
from jax.experimental.pallas import tpu as pltpu
from jax.sharding import PartitionSpec as P

VIEWS = 4
SHEAR = 8
REACH = 32
HALO = SHEAR + REACH
SUB = 8
LANES = 128
MESH = pl.DeviceIdType.MESH


def padded(cells, sides, width):
    for axis, dim in sides:
        count = lax.axis_size(axis)
        ends = count - 1
        head = lax.slice_in_dim(cells, 0, width, axis=dim)
        tail = lax.slice_in_dim(cells, cells.shape[dim] - width, cells.shape[dim], axis=dim)
        cells = jnp.concatenate(
            [
                lax.ppermute(tail, axis, [(i, (i + 1) % count) for i in range(ends)]),
                cells,
                lax.ppermute(head, axis, [((i + 1) % count, i) for i in range(ends)]),
            ],
            axis=dim,
        )
    return cells


def shifted(value, axis, steps):
    count = lax.axis_size(axis)
    first, last = (max(0, -steps), min(count, count - steps))
    return lax.ppermute(value, axis, [(source, source + steps) for source in range(first, last)])


def surface_terms(slab):
    inner = slab[1:-1, 1:-1, 1:-1]
    grad_depth = 0.5 * (slab[2:, 1:-1, 1:-1] - slab[:-2, 1:-1, 1:-1])
    grad_rows = 0.5 * (slab[1:-1, 2:, 1:-1] - slab[1:-1, :-2, 1:-1])
    grad_cols = 0.5 * (slab[1:-1, 1:-1, 2:] - slab[1:-1, 1:-1, :-2])
    factor = lax.rsqrt(
        grad_depth * grad_depth + grad_rows * grad_rows + grad_cols * grad_cols + 1.0
    )
    return (inner, (grad_depth * factor, grad_rows * factor, grad_cols * factor))


def render_layers(inner, normals, shifts, light, palette, rate, rows, cols):
    lengths = jnp.sqrt(jnp.sum(light * light, axis=1, keepdims=True) + 1.0)
    towards = light / lengths
    offsets = palette[:, 0][:, None, None]
    slopes = palette[:, 1][:, None, None]
    layers = []
    for view in range(light.shape[0]):

        def advance(carry, items):
            color, depth = carry
            value_slab, normal_depth, normal_rows, normal_cols, moved = items
            start = (SHEAR - moved[0], SHEAR - moved[1])
            value = lax.dynamic_slice(value_slab, start, (rows, cols))
            dot = (
                lax.dynamic_slice(normal_depth, start, (rows, cols)) * towards[view, 0]
                + lax.dynamic_slice(normal_rows, start, (rows, cols)) * towards[view, 1]
                + lax.dynamic_slice(normal_cols, start, (rows, cols)) * towards[view, 2]
            )
            shade = 0.25 + 0.75 * dot * dot
            density = rate[view] * (1.0 + jnp.tanh(value))
            alpha = 1.0 - jnp.exp(-density)
            weight = alpha * jnp.exp(-depth)
            hues = jax.nn.sigmoid(offsets + slopes * value[None]) * shade[None]
            return ((color + hues * weight[None], depth + density), None)

        start_carry = (
            jnp.zeros((3, rows, cols), jnp.float32),
            jnp.zeros((rows, cols), jnp.float32),
        )
        (color, depth), _ = lax.scan(
            advance, start_carry, (inner, normals[0], normals[1], normals[2], shifts[view])
        )
        layers.append(jnp.concatenate([color, depth[None]], axis=0))
    return jnp.stack(layers)


def precedence(order):
    bricks = order.shape[1]
    onehot = (order[:, :, None] == jnp.arange(bricks, dtype=jnp.int32)[None, None, :]).astype(
        jnp.float32
    )
    ranks = jnp.sum(onehot * jnp.arange(bricks, dtype=jnp.float32)[None, :, None], axis=1)
    return (ranks[:, None, :] < ranks[:, :, None]).astype(jnp.float32)


def many_bricks(pressure, light, palette, rate, shear, offset, order):
    depth_cells, rows, cols = pressure.shape
    brick = lax.axis_index("gz")
    zero = jnp.zeros((), jnp.int32)
    widened = padded(pressure, (("gy", 1), ("gx", 2)), SHEAR + 1)
    slab = padded(widened, (("gz", 0),), 1)
    inner, normals = surface_terms(slab)
    shifts = lax.dynamic_slice(shear, (zero, brick * depth_cells, zero), (VIEWS, depth_cells, 2))
    layers = render_layers(inner, normals, shifts, light, palette, rate, rows, cols)
    moved = lax.dynamic_index_in_dim(offset, brick, 1, keepdims=False)
    blank = jnp.zeros((4, rows + REACH, cols + REACH), jnp.float32)
    canvas = jnp.stack(
        [
            lax.dynamic_update_slice(blank, layers[view], (zero, moved[view, 0], moved[view, 1]))
            for view in range(VIEWS)
        ]
    )
    own_tile = canvas[:, :, :rows, :cols]
    from_above = shifted(canvas[:, :, rows:, :cols], "gy", 1)
    from_left = shifted(canvas[:, :, :rows, cols:], "gx", 1)
    from_diagonal = shifted(canvas[:, :, rows:, cols:], ("gy", "gx"), lax.axis_size("gx") + 1)
    from_diagonal = from_diagonal * (lax.axis_index("gx") > 0).astype(jnp.float32)
    own_tile = own_tile.at[:, :, :REACH, :].add(from_above)
    own_tile = own_tile.at[:, :, :, :REACH].add(from_left)
    own_tile = own_tile.at[:, :, :REACH, :REACH].add(from_diagonal)
    ranking = precedence(order)
    pieces = lax.all_to_all(own_tile[None], "gz", split_axis=3, concat_axis=0, tiled=True)
    depths = pieces[:, :, 3]
    cover = jnp.einsum("vbc,cvyx->bvyx", ranking, depths, precision=lax.Precision.HIGHEST)
    colors = jnp.sum(pieces[:, :, :3] * jnp.exp(-cover)[:, :, None], axis=0)
    opacity = 1.0 - jnp.exp(-jnp.sum(depths, axis=0))
    image = jnp.concatenate([colors, opacity[:, None]], axis=1)
    return image[:, :, None]


class Route:
    def __init__(self, dims, side, step, start, count, slab, half):
        bz = dims[2]
        self.side, self.step, self.half = side, step, half
        self.rows, self.slab = pl.ds(start, count), pl.ds(slab, count)
        self.groups = LANES // (SUB * bz)
        self.tiles = range(start // SUB, (start + count) // SUB)
        self.first = slab // SUB
        self.folds = range(
            self.tiles[0] // self.groups, self.tiles[-1] // self.groups + 1
        )
        self.size = (len(self.tiles) + len(self.folds)) * SUB
        self.base = self.sent = 0

    def there(self, y, ny):
        return y + self.step >= 0 if self.step < 0 else y + self.step < ny

    def comes(self, y, ny):
        return y - self.step < ny if self.step < 0 else y - self.step >= 0

    def wide(self, tile):
        return (tile - self.tiles[0]) * SUB

    def narrow(self, fold):
        return (len(self.tiles) + fold - self.folds[0]) * SUB


def routes_of(dims):
    rows = dims[3]
    strip = rows // 2
    routes = [
        Route(dims, 0, 0, 0, strip + SUB, HALO, 0),
        Route(dims, 0, 1, rows - HALO, HALO, 0, 1),
        Route(dims, 1, 0, strip - HALO, HALO + strip, 0, 0),
        Route(dims, 1, -1, 0, SUB, HALO + strip, 1),
    ]
    sent = 0
    for route in routes:
        route.sent = sent
        sent += route.size
    routes[1].base, routes[3].base = routes[0].size, routes[2].size
    return routes, sent, max(routes[0].size + routes[1].size, routes[2].size + routes[3].size)


MAIN, EDGE, BESIDE, COLS, ENDS, SLOTS = 0, 3, 6, 7, 11, 15
PARTS = 3
BELOW, RIGHT, ACROSS, FACING = range(4)


def exchange(
    dims, mine, here, p_ref, m_ref, cols_out, cols_in, ends_out, ends_in, sends, arrivals, ready
):
    ny, nx, bz, rows = dims
    z, y, x = here
    has_left, has_right = x > 0, x < nx - 1
    has_up, has_down = y > 0, y < ny - 1
    routes = routes_of(dims)[0]

    def remote(src, dst, arrival, who):
        return pltpu.make_async_remote_copy(
            src_ref=src,
            dst_ref=dst,
            send_sem=sends,
            recv_sem=arrivals.at[arrival],
            device_id=who,
            device_id_type=MESH,
        )

    def rows_of(brick, route, part):
        first = bz - PARTS + 1
        start = first + part - 1 if part else 0
        count = bz if part is None else 1 if part else first
        if part is not None and brick == 0:
            start = bz - start - count
        slot = BESIDE if part is None else (EDGE if route.half else MAIN) + part
        return remote(
            p_ref.at[pl.ds(start, count), route.rows],
            m_ref.at[pl.ds(1 + brick * bz + start, count), route.slab],
            slot, (route.side, y + route.step, x),
        )

    def cols_of(brick, route):
        return remote(
            cols_out.at[pl.ds(route.sent, route.size)],
            cols_in.at[brick, pl.ds(route.base, route.size)],
            COLS + 2 * brick + route.half,
            (route.side, y + route.step, x + 1),
        )

    def ends_of(brick, route):
        return remote(
            ends_out,
            ends_in.at[brick, route.half],
            ENDS + 2 * brick + route.half,
            (route.side, y + route.step, x - 1),
        )

    def rows_out(route, part=0):
        there = route.there(y, ny)
        if route.side != mine:
            return [(there, rows_of(mine, route, part))]
        return [(there, rows_of(mine, route, None))] if route.half else []

    def cols_sent(same):
        return [
            (jnp.logical_and(r.there(y, ny), has_right), cols_of(mine, r))
            for r in routes
            if (r.side == mine) == same
        ]

    def ends_sent():
        return [(jnp.logical_and(r.there(y, ny), has_left), ends_of(mine, r)) for r in routes]

    def apply(pairs, act):
        for there, copy in pairs:

            @pl.when(there)
            def _():
                act(copy)

    def start(pairs):
        apply(pairs, lambda copy: copy.start())

    def heard(kind, there, count):
        @pl.when(there)
        def _():
            pl.semaphore_wait(ready.at[kind], count)

    mains, own_halo, halos = (
        (routes[2], routes[1], routes[3]) if mine == 0 else (routes[0], routes[3], routes[1])
    )
    also_down = jnp.logical_and(has_right, has_down)

    def send_first():
        start(rows_out(mains))
        if mine == 1:
            start(rows_out(own_halo))

    def send_rest():
        if mine == 0:
            heard(FACING, y >= 0, 1)
            start(rows_out(halos))
            heard(BELOW, has_down, 1)
            start(rows_out(own_halo) + ends_sent())
            heard(RIGHT, has_right, 1 + has_down.astype(jnp.int32))
            start(cols_sent(True))
            heard(ACROSS, has_right, 1)
        else:
            heard(BELOW, has_down, 1)
            start(rows_out(halos) + ends_sent())
            heard(RIGHT, has_right, 1)
            start(cols_sent(True))
            heard(ACROSS, also_down, 1)
        start(cols_sent(False))
        start(rows_out(mains, 1) + rows_out(halos, 1))

    def send_last():
        start(rows_out(mains, 2) + rows_out(halos, 2))

    def receive(brick, parts, sides):
        pairs = []
        for route in routes:
            if route.side != mine:
                continue
            comes = route.comes(y, ny)
            if brick != mine:
                pairs += [(comes, rows_of(brick, route, part)) for part in parts]
            elif route.half:
                pairs += [(comes, rows_of(brick, route, None))]
            if sides:
                pairs += [
                    (jnp.logical_and(comes, has_left), cols_of(brick, route)),
                    (jnp.logical_and(comes, has_right), ends_of(brick, route)),
                ]
        apply(pairs, lambda copy: copy.wait_recv())

    def close():
        for part in range(PARTS):
            apply(rows_out(mains, part) + rows_out(halos, part), lambda copy: copy.wait_send())
        apply(rows_out(own_halo), lambda copy: copy.wait_send())
        apply(ends_sent() + cols_sent(True) + cols_sent(False), lambda copy: copy.wait_send())

    return send_first, send_rest, send_last, receive, close


def answers_of(dims, here):
    z, y, x = here
    up, left, lower = y > 0, x > 0, z == 0
    both = jnp.logical_and(up, left)
    upper = jnp.logical_not(lower)
    yield up, (z, y - 1, x), BELOW
    yield left, (z, y, x - 1), RIGHT
    yield jnp.logical_and(both, lower), (z, y - 1, x - 1), RIGHT
    yield jnp.logical_and(both, upper), (z, y - 1, x - 1), ACROSS
    yield jnp.logical_and(left, upper), (1 - z, y, x - 1), ACROSS
    yield upper, (1 - z, y, x), FACING


def render(
    dims, light_in, palette_in, rate_in, shear_in, offset_in, order_in, p_ref, out_ref,
    light, palette, rate, shear, offset, order, tile_ref, m_ref, own_ref, cols_in, ends_in,
    cols_out, ends_out, h_ref, r_ref, dm, dh, back, sends, arrivals, ready, local_sems, table_sem,
):
    ny, nx, bz, rows = dims
    strip = rows // 2
    tall = HALO + strip + SUB
    depth = 2 * bz
    blocks = (HALO + strip) // SUB
    wide_lanes = HALO - SUB
    z, y, x = lax.axis_index("gz"), lax.axis_index("gy"), lax.axis_index("gx")
    routes = routes_of(dims)[0]

    tables = [
        pltpu.make_async_copy(source, target, table_sem)
        for source, target in (
            (light_in, light), (palette_in, palette), (rate_in, rate),
            (shear_in, shear), (offset_in, offset), (order_in, order),
        )
    ]
    barrier = pltpu.get_barrier_semaphore()

    def sided(act):
        for mine in range(2):

            @pl.when(z == mine)
            def _():
                act(mine)

    def greet(there, who):
        @pl.when(there)
        def _():
            pl.semaphore_signal(barrier, inc=1, device_id=who, device_id_type=MESH)

    greet(z >= 0, (1 - z, y, x))
    greet(y < ny - 1, (z, y + 1, x))

    steps = [
        exchange(
            dims, mine, (z, y, x), p_ref, m_ref, cols_out, cols_in, ends_out, ends_in,
            sends, arrivals, ready,
        )
        for mine in range(2)
    ]

    def local_slab(mine):
        route = routes[2 * mine]
        return pltpu.make_async_copy(
            p_ref.at[:, route.rows], m_ref.at[pl.ds(1 + mine * bz, bz), route.slab],
            local_sems.at[1],
        )

    local_tile = pltpu.make_async_copy(p_ref, tile_ref, local_sems.at[0])
    local_tile.start()
    sided(lambda mine: local_slab(mine).start())
    for copy in tables:
        copy.start()

    pl.semaphore_wait(barrier, 1 + (y > 0).astype(jnp.int32) + (x > 0).astype(jnp.int32))
    greet(x < nx - 1, (z, y, x + 1))
    for there, who, kind in answers_of(dims, (z, y, x)):

        @pl.when(there)
        def _():
            pl.semaphore_signal(ready.at[kind], inc=1, device_id=who, device_id_type=MESH)


    sided(lambda mine: steps[mine][0]())

    empty = jnp.zeros((tall, LANES), jnp.float32)
    for ref in (m_ref, h_ref):
        ref[0] = empty
        ref[depth + 1] = empty

    def blank(mine):
        route = routes[2 * mine + 1]

        @pl.when(jnp.logical_not(route.comes(y, ny)))
        def _():
            m_ref[:, route.slab] = jnp.zeros((depth + 2, len(route.tiles) * SUB, LANES), jnp.float32)
            cols_in[:, route.base : route.base + route.size] = jnp.zeros(
                (2, route.size, LANES), jnp.float32
            )
            ends_in[:, 1] = jnp.zeros((2, SUB, LANES), jnp.float32)

    sided(blank)

    @pl.when(x == 0)
    def _():
        cols_in[...] = jnp.zeros(cols_in.shape, jnp.float32)

    @pl.when(x == nx - 1)
    def _():
        ends_in[...] = jnp.zeros(ends_in.shape, jnp.float32)

    lane = lax.broadcasted_iota(jnp.int32, (SUB, LANES), 1)
    last = lane == LANES - 1
    first = lane == 0
    groups = routes[0].groups
    tiles = rows // SUB

    def cell(j, t):
        return tile_ref[j, t * SUB : (t + 1) * SUB]

    def put(t_or_fold, is_wide, value):
        for route in routes:
            if t_or_fold in (route.tiles if is_wide else route.folds):
                at = route.sent + (route.wide if is_wide else route.narrow)(t_or_fold)
                cols_out[at : at + SUB] = value

    def merged(pieces):
        while len(pieces) > 1:
            pieces = [
                (a[0], jnp.where(lane >= b[0], b[1], a[1]))
                for a, b in zip(pieces[::2], pieces[1::2])
            ] + (pieces[-1:] if len(pieces) % 2 else [])
        return pieces[0][1]

    def turned(value, by):
        return pltpu.roll(value, by % LANES, 1) if by % LANES else value

    local_tile.wait()
    for t in range(tiles):
        put(
            t, True,
            merged(
                [(wide_lanes * j, turned(cell(j, t), wide_lanes * (j + 1))) for j in range(bz)]
            ),
        )
    for fold in range(tiles // groups):
        put(
            fold, False,
            merged(
                [
                    (
                        SUB * (bz * g + j),
                        turned(cell(j, fold * groups + g), SUB * (bz * g + j) + HALO),
                    )
                    for g in range(groups)
                    for j in range(bz)
                ]
            ),
        )
    ends_out[...] = merged(
        [(t * bz + j, turned(cell(j, t), t * bz + j)) for t in range(tiles) for j in range(bz)]
    )

    def unpack(mine, brick):
        for route in routes[2 * mine : 2 * mine + 2]:
            for t in route.tiles:
                row = (route.first + t - route.tiles[0]) * SUB
                at = route.base + route.wide(t)
                wide = cols_in[brick, at : at + SUB]
                at = route.base + route.narrow(t // groups)
                narrow = cols_in[brick, at : at + SUB]
                for j in range(bz):
                    h_ref[1 + brick * bz + j, row : row + SUB] = jnp.where(
                        lane >= LANES - wide_lanes,
                        turned(wide, -wide_lanes * (j + 1)),
                        turned(narrow, -SUB * (bz * (t % groups) + j) - HALO),
                    )
                r_ref[brick, row : row + SUB] = turned(
                    ends_in[brick, route.half], LANES - 1 - t * bz
                )

    def opening(mine):
        _, send_rest, send_last, receive, _ = steps[mine]
        send_rest()
        local_slab(mine).wait()
        receive(mine, (), True)
        send_last()
        own_ref[...] = m_ref[1 + mine * bz : 1 + (mine + 1) * bz]
        unpack(mine, mine)

    def middle(mine):
        receive = steps[mine][3]
        receive(1 - mine, (0,), True)
        unpack(mine, 1 - mine)

    def ending(mine, part):
        receive = steps[mine][3]
        receive(1 - mine, (part,), False)

    sided(opening)
    for copy in tables:
        copy.wait()

    towards = []
    for w in range(VIEWS):
        a, b, c = light[w, 0], light[w, 1], light[w, 2]
        inverse = lax.rsqrt(jnp.full((SUB, LANES), a * a + b * b + c * c + 1.0, jnp.float32))
        towards.append((a * inverse, b * inverse, c * inverse))

    def slopes(k, carry):
        for i in range(blocks):
            top = i * SUB
            here = m_ref[k + 1, top + 1 : top + 1 + SUB]
            side = h_ref[k + 1, top + 1 : top + 1 + SUB]
            beyond = pltpu.roll(
                r_ref[k // bz, top + 1 : top + 1 + SUB], (LANES - k % bz) % LANES, 1
            )
            here_r, here_l = pltpu.roll(here, LANES - 1, 1), pltpu.roll(here, 1, 1)
            side_r, side_l = pltpu.roll(side, LANES - 1, 1), pltpu.roll(side, 1, 1)
            for ref, cols, dots in (
                (m_ref, jnp.where(last, beyond, here_r) - jnp.where(first, side_l, here_l), dm),
                (h_ref, jnp.where(last, here_r, side_r) - side_l, dh),
            ):
                deep = ref[k + 2, top + 1 : top + 1 + SUB] - ref[k, top + 1 : top + 1 + SUB]
                down = ref[k + 1, top + 2 : top + 2 + SUB] - ref[k + 1, top : top + SUB]
                half = lax.rsqrt(deep * deep + down * down + cols * cols + 4.0)
                deep, down, cols = deep * half, down * half, cols * half
                for w in range(VIEWS):
                    a, b, c = towards[w]
                    dots[w, k, top : top + SUB] = deep * a + down * b + cols * c
        return carry

    tile = 32
    per_view = strip // tile
    base_row = y * rows + z * strip
    base_col = x * LANES
    lanes = lax.broadcasted_iota(jnp.int32, (tile, LANES), 1)
    rows_at = lax.broadcasted_iota(jnp.int32, (tile, LANES), 0)
    bias = [0.5 * palette[0, c] for c in range(3)]
    gain = [0.5 * palette[1, c] for c in range(3)]

    def march(w, top, brick, cells, start, colors, through):
        ambient = jnp.zeros((tile, LANES), jnp.float32)
        rate2 = rate[w] * (-math.log2(math.e))
        off_r, off_c = offset[brick, 0, w], offset[brick, 1, w]
        inside = jnp.logical_and(rows_at >= off_r - base_row - top, lanes >= off_c - base_col)
        fall = jnp.where(inside, rate2, 0.0)
        for j in range(bz):
            k = brick * bz + j
            sr = off_r + shear[w, 0, k]
            sc = off_c + shear[w, 1, k]
            at = HALO + top - sr
            wrap = lanes >= LANES - sc
            value = jnp.where(wrap, h_ref[k + 1, pl.ds(at, tile)], cells[start + j, pl.ds(at, tile)])
            dot = jnp.where(wrap, dh[w, k, pl.ds(at - 1, tile)], dm[w, k, pl.ds(at - 1, tile)])
            value = pltpu.roll(value, sc, 1)
            dot = pltpu.roll(dot, sc, 1)
            kept = jnp.exp2(fall * (1.0 + jnp.tanh(value)))
            weight = (0.125 + 0.375 * dot * dot) * ((1.0 - kept) * through)
            through = through * kept
            ambient = ambient + weight
            colors = [
                colors[c] + weight * jnp.tanh(bias[c] + gain[c] * value) for c in range(3)
            ]
        return [color + ambient for color in colors], through

    def views(act):
        def one(step, carry):
            act(step // per_view, (step % per_view) * tile)
            return carry

        lax.fori_loop(0, VIEWS * per_view, one, 0, unroll=VIEWS * per_view)

    def own_layer(w, top):
        at = pl.ds(top, tile)
        zero = jnp.zeros((tile, LANES), jnp.float32)
        colors, through = march(w, top, z, own_ref, 0, [zero] * 3, zero + 1.0)
        ahead = order[0, w] == z
        for c in range(3):
            out_ref[w, c, at] = jnp.where(ahead, colors[c], 0.0)
            back[w, c, at] = jnp.where(ahead, 0.0, colors[c])
        out_ref[w, 3, at] = jnp.where(ahead, through, 1.0)
        back[w, 3, at] = jnp.where(ahead, 1.0, through)

    def other_layer(w, top):
        at = pl.ds(top, tile)
        colors, through = march(
            w, top, 1 - z, m_ref, 1 + (1 - z) * bz, [out_ref[w, c, at] for c in range(3)],
            out_ref[w, 3, at],
        )
        for c in range(3):
            out_ref[w, c, at] = colors[c] + through * back[w, c, at]
        out_ref[w, 3, at] = 1.0 - through * back[w, 3, at]

    def each(start, stop):
        lax.fori_loop(start, stop, slopes, 0)

    each(z * (bz + 1), z * (bz + 1) + bz - 1)
    sided(middle)
    each(bz - 1, bz + 1)
    views(own_layer)
    sided(lambda mine: ending(mine, 1))
    each(bz + 1 - 3 * z, bz + 2 - 3 * z)
    sided(lambda mine: ending(mine, 2))
    each((1 - z) * (depth - 2), (1 - z) * (depth - 2) + 2)
    views(other_layer)
    sided(lambda mine: steps[mine][4]())


def two_bricks(mesh, pressure, light, palette, rate, shear, offset, order):
    bz, rows, cols = pressure.shape
    dims = (mesh.shape["gy"], mesh.shape["gx"], bz, rows)
    strip = rows // 2
    tall = HALO + strip + SUB
    depth = 2 * bz
    vmem = pl.BlockSpec(memory_space=pltpu.VMEM)
    hbm = pl.BlockSpec(memory_space=pltpu.HBM)
    f32 = jnp.float32
    _, sent, got = routes_of(dims)
    tables = (
        light,
        palette.T,
        rate,
        jnp.transpose(shear, (0, 2, 1)),
        jnp.transpose(offset, (1, 2, 0)),
        order.T,
    )
    image = pl.pallas_call(
        functools.partial(render, dims),
        out_shape=jax.ShapeDtypeStruct((VIEWS, 4, strip, LANES), f32),
        in_specs=[hbm] * 7,
        out_specs=vmem,
        scratch_shapes=[
            *[pltpu.SMEM(table.shape, table.dtype) for table in tables],
            pltpu.VMEM((bz, rows, LANES), f32),
            pltpu.VMEM((depth + 2, tall, LANES), f32),
            pltpu.VMEM((bz, tall, LANES), f32),
            pltpu.VMEM((2, got, LANES), f32),
            pltpu.VMEM((2, 2, SUB, LANES), f32),
            pltpu.VMEM((sent, LANES), f32),
            pltpu.VMEM((SUB, LANES), f32),
            pltpu.VMEM((depth + 2, tall, LANES), f32),
            pltpu.VMEM((2, tall, LANES), f32),
            pltpu.VMEM((VIEWS, depth, HALO + strip, LANES), f32),
            pltpu.VMEM((VIEWS, depth, HALO + strip, LANES), f32),
            pltpu.VMEM((VIEWS, 4, strip, LANES), f32),
            pltpu.SemaphoreType.DMA,
            pltpu.SemaphoreType.DMA((SLOTS,)),
            pltpu.SemaphoreType.REGULAR((4,)),
            pltpu.SemaphoreType.DMA((2,)),
            pltpu.SemaphoreType.DMA,
        ],
        compiler_params=pltpu.CompilerParams(collective_id=0, has_side_effects=True, vmem_limit_bytes=12 << 20),
        name="render",
    )(
        *[pltpu.with_memory_space_constraint(t, pltpu.HBM) for t in (*tables, pressure)]
    )
    return image[:, :, None]


def fits(mesh, shape):
    bz, rows, cols = shape
    return (
        mesh.shape["gz"] == 2
        and cols == LANES
        and rows % 64 == 0
        and 2 * HALO <= rows <= LANES
        and bz * (HALO - SUB) == LANES
        and bz * (rows // SUB) <= LANES
    )


def on_device(mesh, pressure, *rest):
    if fits(mesh, pressure.shape):
        return two_bricks(mesh, pressure, *rest)
    return many_bricks(pressure, *rest)


def solution(mesh):
    return jax.shard_map(
        functools.partial(on_device, mesh),
        mesh=mesh,
        in_specs=(P("gz", "gy", "gx"), P(), P(), P(), P(), P(), P()),
        out_specs=P(None, None, "gz", "gy", "gx"),
        check_vma=False,
    )
```

```python
import functools
import math

import jax
import jax.numpy as jnp
from jax import lax
from jax.experimental import pallas as pl
from jax.experimental.pallas import tpu as pltpu
from jax.sharding import PartitionSpec as P

VIEWS = 4
SHEAR = 8
REACH = 32
HALO = SHEAR + REACH
SUB = 8
LANES = 128
MESH = pl.DeviceIdType.MESH


def padded(cells, sides, width):
    for axis, dim in sides:
        count = lax.axis_size(axis)
        ends = count - 1
        head = lax.slice_in_dim(cells, 0, width, axis=dim)
        tail = lax.slice_in_dim(cells, cells.shape[dim] - width, cells.shape[dim], axis=dim)
        cells = jnp.concatenate(
            [
                lax.ppermute(tail, axis, [(i, (i + 1) % count) for i in range(ends)]),
                cells,
                lax.ppermute(head, axis, [((i + 1) % count, i) for i in range(ends)]),
            ],
            axis=dim,
        )
    return cells


def shifted(value, axis, steps):
    count = lax.axis_size(axis)
    first, last = (max(0, -steps), min(count, count - steps))
    return lax.ppermute(value, axis, [(source, source + steps) for source in range(first, last)])


def surface_terms(slab):
    inner = slab[1:-1, 1:-1, 1:-1]
    grad_depth = 0.5 * (slab[2:, 1:-1, 1:-1] - slab[:-2, 1:-1, 1:-1])
    grad_rows = 0.5 * (slab[1:-1, 2:, 1:-1] - slab[1:-1, :-2, 1:-1])
    grad_cols = 0.5 * (slab[1:-1, 1:-1, 2:] - slab[1:-1, 1:-1, :-2])
    factor = lax.rsqrt(
        grad_depth * grad_depth + grad_rows * grad_rows + grad_cols * grad_cols + 1.0
    )
    return (inner, (grad_depth * factor, grad_rows * factor, grad_cols * factor))


def render_layers(inner, normals, shifts, light, palette, rate, rows, cols):
    lengths = jnp.sqrt(jnp.sum(light * light, axis=1, keepdims=True) + 1.0)
    towards = light / lengths
    offsets = palette[:, 0][:, None, None]
    slopes = palette[:, 1][:, None, None]
    layers = []
    for view in range(light.shape[0]):

        def advance(carry, items):
            color, depth = carry
            value_slab, normal_depth, normal_rows, normal_cols, moved = items
            start = (SHEAR - moved[0], SHEAR - moved[1])
            value = lax.dynamic_slice(value_slab, start, (rows, cols))
            dot = (
                lax.dynamic_slice(normal_depth, start, (rows, cols)) * towards[view, 0]
                + lax.dynamic_slice(normal_rows, start, (rows, cols)) * towards[view, 1]
                + lax.dynamic_slice(normal_cols, start, (rows, cols)) * towards[view, 2]
            )
            shade = 0.25 + 0.75 * dot * dot
            density = rate[view] * (1.0 + jnp.tanh(value))
            alpha = 1.0 - jnp.exp(-density)
            weight = alpha * jnp.exp(-depth)
            hues = jax.nn.sigmoid(offsets + slopes * value[None]) * shade[None]
            return ((color + hues * weight[None], depth + density), None)

        start_carry = (
            jnp.zeros((3, rows, cols), jnp.float32),
            jnp.zeros((rows, cols), jnp.float32),
        )
        (color, depth), _ = lax.scan(
            advance, start_carry, (inner, normals[0], normals[1], normals[2], shifts[view])
        )
        layers.append(jnp.concatenate([color, depth[None]], axis=0))
    return jnp.stack(layers)


def precedence(order):
    bricks = order.shape[1]
    onehot = (order[:, :, None] == jnp.arange(bricks, dtype=jnp.int32)[None, None, :]).astype(
        jnp.float32
    )
    ranks = jnp.sum(onehot * jnp.arange(bricks, dtype=jnp.float32)[None, :, None], axis=1)
    return (ranks[:, None, :] < ranks[:, :, None]).astype(jnp.float32)


def many_bricks(pressure, light, palette, rate, shear, offset, order):
    depth_cells, rows, cols = pressure.shape
    brick = lax.axis_index("gz")
    zero = jnp.zeros((), jnp.int32)
    widened = padded(pressure, (("gy", 1), ("gx", 2)), SHEAR + 1)
    slab = padded(widened, (("gz", 0),), 1)
    inner, normals = surface_terms(slab)
    shifts = lax.dynamic_slice(shear, (zero, brick * depth_cells, zero), (VIEWS, depth_cells, 2))
    layers = render_layers(inner, normals, shifts, light, palette, rate, rows, cols)
    moved = lax.dynamic_index_in_dim(offset, brick, 1, keepdims=False)
    blank = jnp.zeros((4, rows + REACH, cols + REACH), jnp.float32)
    canvas = jnp.stack(
        [
            lax.dynamic_update_slice(blank, layers[view], (zero, moved[view, 0], moved[view, 1]))
            for view in range(VIEWS)
        ]
    )
    own_tile = canvas[:, :, :rows, :cols]
    from_above = shifted(canvas[:, :, rows:, :cols], "gy", 1)
    from_left = shifted(canvas[:, :, :rows, cols:], "gx", 1)
    from_diagonal = shifted(canvas[:, :, rows:, cols:], ("gy", "gx"), lax.axis_size("gx") + 1)
    from_diagonal = from_diagonal * (lax.axis_index("gx") > 0).astype(jnp.float32)
    own_tile = own_tile.at[:, :, :REACH, :].add(from_above)
    own_tile = own_tile.at[:, :, :, :REACH].add(from_left)
    own_tile = own_tile.at[:, :, :REACH, :REACH].add(from_diagonal)
    ranking = precedence(order)
    pieces = lax.all_to_all(own_tile[None], "gz", split_axis=3, concat_axis=0, tiled=True)
    depths = pieces[:, :, 3]
    cover = jnp.einsum("vbc,cvyx->bvyx", ranking, depths, precision=lax.Precision.HIGHEST)
    colors = jnp.sum(pieces[:, :, :3] * jnp.exp(-cover)[:, :, None], axis=0)
    opacity = 1.0 - jnp.exp(-jnp.sum(depths, axis=0))
    image = jnp.concatenate([colors, opacity[:, None]], axis=1)
    return image[:, :, None]


class Route:
    def __init__(self, dims, side, step, start, count, slab, half):
        bz = dims[2]
        self.side, self.step, self.half = side, step, half
        self.slab = pl.ds(slab, count)
        needed = count - SUB + 1 if start == 0 else count
        self.rows, self.lands = pl.ds(start, needed), pl.ds(slab, needed)
        self.groups = LANES // (SUB * bz)
        self.tiles = range(start // SUB, (start + count) // SUB)
        self.first = slab // SUB
        self.folds = range(
            self.tiles[0] // self.groups, self.tiles[-1] // self.groups + 1
        )
        self.size = (len(self.tiles) + len(self.folds)) * SUB
        self.base = self.sent = 0

    def there(self, y, ny):
        return y + self.step >= 0 if self.step < 0 else y + self.step < ny

    def comes(self, y, ny):
        return y - self.step < ny if self.step < 0 else y - self.step >= 0

    def wide(self, tile):
        return (tile - self.tiles[0]) * SUB

    def narrow(self, fold):
        return (len(self.tiles) + fold - self.folds[0]) * SUB


def routes_of(dims):
    rows = dims[3]
    strip = rows // 2
    routes = [
        Route(dims, 0, 0, 0, strip + SUB, HALO, 0),
        Route(dims, 0, 1, rows - HALO, HALO, 0, 1),
        Route(dims, 1, 0, strip - HALO, HALO + strip, 0, 0),
        Route(dims, 1, -1, 0, SUB, HALO + strip, 1),
    ]
    sent = 0
    for route in routes:
        route.sent = sent
        sent += route.size
    routes[1].base, routes[3].base = routes[0].size, routes[2].size
    return routes, sent, max(routes[0].size + routes[1].size, routes[2].size + routes[3].size)


MAIN, EDGE, BESIDE, COLS, ENDS, SLOTS = 0, 3, 6, 7, 11, 15
PARTS = 3
BELOW, RIGHT, ACROSS = range(3)


def exchange(
    dims, mine, here, p_ref, m_ref, cols_out, cols_in, ends_out, ends_in, sends, arrivals, ready
):
    ny, nx, bz, rows = dims
    z, y, x = here
    has_left, has_right = x > 0, x < nx - 1
    has_up, has_down = y > 0, y < ny - 1
    routes = routes_of(dims)[0]

    def remote(src, dst, arrival, who):
        return pltpu.make_async_remote_copy(
            src_ref=src,
            dst_ref=dst,
            send_sem=sends,
            recv_sem=arrivals.at[arrival],
            device_id=who,
            device_id_type=MESH,
        )

    def rows_of(brick, route, part):
        first = bz - PARTS + 1
        start = first + part - 1 if part else 0
        count = bz if part is None else 1 if part else first
        if part is not None and brick == 0:
            start = bz - start - count
        slot = BESIDE if part is None else (EDGE if route.half else MAIN) + part
        return remote(
            p_ref.at[pl.ds(start, count), route.rows],
            m_ref.at[pl.ds(1 + brick * bz + start, count), route.lands],
            slot, (route.side, y + route.step, x),
        )

    def cols_of(brick, route):
        return remote(
            cols_out.at[pl.ds(route.sent, route.size)],
            cols_in.at[brick, pl.ds(route.base, route.size)],
            COLS + 2 * brick + route.half,
            (route.side, y + route.step, x + 1),
        )

    def ends_of(brick, route):
        return remote(
            ends_out,
            ends_in.at[brick, route.half],
            ENDS + 2 * brick + route.half,
            (route.side, y + route.step, x - 1),
        )

    def rows_out(route, part=0):
        there = route.there(y, ny)
        if route.side != mine:
            return [(there, rows_of(mine, route, part))]
        return [(there, rows_of(mine, route, None))] if route.half else []

    def cols_sent(same):
        return [
            (jnp.logical_and(r.there(y, ny), has_right), cols_of(mine, r))
            for r in routes
            if (r.side == mine) == same
        ]

    def ends_sent():
        return [(jnp.logical_and(r.there(y, ny), has_left), ends_of(mine, r)) for r in routes]

    def apply(pairs, act):
        for there, copy in pairs:

            @pl.when(there)
            def _():
                act(copy)

    def start(pairs):
        apply(pairs, lambda copy: copy.start())

    def heard(kind, there, count):
        @pl.when(there)
        def _():
            pl.semaphore_wait(ready.at[kind], count)

    mains, own_halo, halos = (
        (routes[2], routes[1], routes[3]) if mine == 0 else (routes[0], routes[3], routes[1])
    )
    next_ones = [1 + there.astype(jnp.int32) for there in (has_down, has_up)]

    def send_first():
        if mine == 0:
            start(rows_out(mains))
            start(rows_out(halos))
        else:
            start(rows_out(mains))
            start(rows_out(own_halo))

    def send_rest():
        if mine == 0:
            start(ends_sent())
            heard(BELOW, has_down, 1)
            start(rows_out(own_halo))
        else:
            start(ends_sent())
            heard(BELOW, has_down, 1)
            start(rows_out(halos))
        heard(RIGHT, has_right, next_ones[mine])
        start(cols_sent(True))
        heard(ACROSS, has_right, next_ones[1 - mine])
        start(cols_sent(False))
        start(rows_out(mains, 1) + rows_out(halos, 1))

    def send_last():
        start(rows_out(mains, 2) + rows_out(halos, 2))

    def receive(brick, parts, sides):
        pairs = []
        for route in routes:
            if route.side != mine:
                continue
            comes = route.comes(y, ny)
            if brick != mine:
                pairs += [(comes, rows_of(brick, route, part)) for part in parts]
            elif route.half:
                pairs += [(comes, rows_of(brick, route, None))]
            if sides:
                pairs += [
                    (jnp.logical_and(comes, has_left), cols_of(brick, route)),
                    (jnp.logical_and(comes, has_right), ends_of(brick, route)),
                ]
        apply(pairs, lambda copy: copy.wait_recv())

    def close():
        for part in range(PARTS):
            apply(rows_out(mains, part) + rows_out(halos, part), lambda copy: copy.wait_send())
        apply(rows_out(own_halo), lambda copy: copy.wait_send())
        apply(ends_sent() + cols_sent(True) + cols_sent(False), lambda copy: copy.wait_send())

    return send_first, send_rest, send_last, receive, close


def partners_of(dims, here, over):
    ny, nx = dims[:2]
    z, y, x = here
    steps = [(z, over, 0), (1 - z, 0, 0)]
    diagonal = z == 1 if over > 0 else z == 0
    yield jnp.logical_and(diagonal, inside_of(dims, y + over, x)), (1 - z, y + over, x)
    steps += [
        (side, step, over)
        for side, step in ((z, -1), (z, 0), (z, 1), (1 - z, 0), (1 - z, 2 * z - 1))
    ]
    for side, step, across in steps:
        yield inside_of(dims, y + step, x + across), (side, y + step, x + across)


def inside_of(dims, y, x):
    ny, nx = dims[:2]
    return jnp.logical_and(
        jnp.logical_and(y >= 0, y < ny), jnp.logical_and(x >= 0, x < nx)
    )


def answers_of(dims, here):
    z, y, x = here
    own = z == 0
    yield jnp.logical_and(own, y > 0), (z, y - 1, x), BELOW
    yield jnp.logical_and(own, y > 0), (1 - z, y - 1, x), BELOW
    for side, kind in ((z, RIGHT), (1 - z, ACROSS)):
        for step in (0, 2 * z - 1):
            yield inside_of(dims, y + step, x - 1), (side, y + step, x - 1), kind


def render(
    dims, light_in, palette_in, rate_in, shear_in, offset_in, order_in, p_ref, out_ref,
    light, palette, rate, shear, offset, order, tile_ref, m_ref, own_ref, cols_in, ends_in,
    cols_out, ends_out, h_ref, r_ref, dm, dh, back, sends, arrivals, ready, local_sems, table_sem,
):
    ny, nx, bz, rows = dims
    strip = rows // 2
    tall = HALO + strip + SUB
    depth = 2 * bz
    blocks = (HALO + strip) // SUB
    wide_lanes = HALO - SUB
    z, y, x = lax.axis_index("gz"), lax.axis_index("gy"), lax.axis_index("gx")
    routes = routes_of(dims)[0]

    tables = [
        pltpu.make_async_copy(source, target, table_sem)
        for source, target in (
            (light_in, light), (palette_in, palette), (rate_in, rate),
            (shear_in, shear), (offset_in, offset), (order_in, order),
        )
    ]
    barrier = pltpu.get_barrier_semaphore()

    def sided(act):
        for mine in range(2):

            @pl.when(z == mine)
            def _():
                act(mine)

    for there, who in partners_of(dims, (z, y, x), 1):

        @pl.when(there)
        def _():
            pl.semaphore_signal(barrier, inc=1, device_id=who, device_id_type=MESH)

    count = 0
    for there, _ in partners_of(dims, (z, y, x), -1):
        count = count + there.astype(jnp.int32)

    steps = [
        exchange(
            dims, mine, (z, y, x), p_ref, m_ref, cols_out, cols_in, ends_out, ends_in,
            sends, arrivals, ready,
        )
        for mine in range(2)
    ]

    def local_slab(mine):
        route = routes[2 * mine]
        return pltpu.make_async_copy(
            p_ref.at[:, route.rows], m_ref.at[pl.ds(1 + mine * bz, bz), route.lands],
            local_sems.at[1],
        )

    local_tile = pltpu.make_async_copy(p_ref, tile_ref, local_sems.at[0])
    local_tile.start()
    sided(lambda mine: local_slab(mine).start())
    for copy in tables:
        copy.start()

    @pl.when(count > 0)
    def _():
        pl.semaphore_wait(barrier, count)

    for there, who, kind in answers_of(dims, (z, y, x)):

        @pl.when(there)
        def _():
            pl.semaphore_signal(ready.at[kind], inc=1, device_id=who, device_id_type=MESH)


    sided(lambda mine: steps[mine][0]())

    empty = jnp.zeros((tall, LANES), jnp.float32)
    for ref in (m_ref, h_ref):
        ref[0] = empty
        ref[depth + 1] = empty

    def blank(mine):
        route = routes[2 * mine + 1]

        @pl.when(jnp.logical_not(route.comes(y, ny)))
        def _():
            m_ref[:, route.slab] = jnp.zeros((depth + 2, len(route.tiles) * SUB, LANES), jnp.float32)
            cols_in[:, route.base : route.base + route.size] = jnp.zeros(
                (2, route.size, LANES), jnp.float32
            )
            ends_in[:, 1] = jnp.zeros((2, SUB, LANES), jnp.float32)

    sided(blank)

    @pl.when(x == 0)
    def _():
        cols_in[...] = jnp.zeros(cols_in.shape, jnp.float32)

    @pl.when(x == nx - 1)
    def _():
        ends_in[...] = jnp.zeros(ends_in.shape, jnp.float32)

    lane = lax.broadcasted_iota(jnp.int32, (SUB, LANES), 1)
    last = lane == LANES - 1
    first = lane == 0
    groups = routes[0].groups
    tiles = rows // SUB

    def cell(j, t):
        return tile_ref[j, t * SUB : (t + 1) * SUB]

    def put(t_or_fold, is_wide, value):
        for route in routes:
            if t_or_fold in (route.tiles if is_wide else route.folds):
                at = route.sent + (route.wide if is_wide else route.narrow)(t_or_fold)
                cols_out[at : at + SUB] = value

    def merged(pieces):
        while len(pieces) > 1:
            pieces = [
                (a[0], jnp.where(lane >= b[0], b[1], a[1]))
                for a, b in zip(pieces[::2], pieces[1::2])
            ] + (pieces[-1:] if len(pieces) % 2 else [])
        return pieces[0][1]

    def turned(value, by):
        return pltpu.roll(value, by % LANES, 1) if by % LANES else value

    local_tile.wait()
    for t in range(tiles):
        put(
            t, True,
            merged(
                [(wide_lanes * j, turned(cell(j, t), wide_lanes * (j + 1))) for j in range(bz)]
            ),
        )
    for fold in range(tiles // groups):
        put(
            fold, False,
            merged(
                [
                    (
                        SUB * (bz * g + j),
                        turned(cell(j, fold * groups + g), SUB * (bz * g + j) + HALO),
                    )
                    for g in range(groups)
                    for j in range(bz)
                ]
            ),
        )
    ends_out[...] = merged(
        [(t * bz + j, turned(cell(j, t), t * bz + j)) for t in range(tiles) for j in range(bz)]
    )

    def unpack(mine, brick):
        for route in routes[2 * mine : 2 * mine + 2]:
            for t in route.tiles:
                row = (route.first + t - route.tiles[0]) * SUB
                at = route.base + route.wide(t)
                wide = cols_in[brick, at : at + SUB]
                at = route.base + route.narrow(t // groups)
                narrow = cols_in[brick, at : at + SUB]
                for j in range(bz):
                    h_ref[1 + brick * bz + j, row : row + SUB] = jnp.where(
                        lane >= LANES - wide_lanes,
                        turned(wide, -wide_lanes * (j + 1)),
                        turned(narrow, -SUB * (bz * (t % groups) + j) - HALO),
                    )
                r_ref[brick, row : row + SUB] = turned(
                    ends_in[brick, route.half], LANES - 1 - t * bz
                )

    def opening(mine):
        _, send_rest, send_last, receive, _ = steps[mine]
        send_rest()
        local_slab(mine).wait()
        receive(mine, (), True)
        send_last()
        own_ref[...] = m_ref[1 + mine * bz : 1 + (mine + 1) * bz]
        unpack(mine, mine)

    def middle(mine):
        receive = steps[mine][3]
        receive(1 - mine, (0,), True)
        unpack(mine, 1 - mine)

    def ending(mine, part):
        receive = steps[mine][3]
        receive(1 - mine, (part,), False)

    sided(opening)
    for copy in tables:
        copy.wait()

    towards = []
    for w in range(VIEWS):
        a, b, c = light[w, 0], light[w, 1], light[w, 2]
        inverse = lax.rsqrt(jnp.full((SUB, LANES), a * a + b * b + c * c + 1.0, jnp.float32))
        towards.append((a * inverse, b * inverse, c * inverse))

    def slopes(k, carry):
        for i in range(blocks):
            top = i * SUB
            here = m_ref[k + 1, top + 1 : top + 1 + SUB]
            side = h_ref[k + 1, top + 1 : top + 1 + SUB]
            beyond = pltpu.roll(
                r_ref[k // bz, top + 1 : top + 1 + SUB], (LANES - k % bz) % LANES, 1
            )
            here_r, here_l = pltpu.roll(here, LANES - 1, 1), pltpu.roll(here, 1, 1)
            side_r, side_l = pltpu.roll(side, LANES - 1, 1), pltpu.roll(side, 1, 1)
            for ref, cols, dots in (
                (m_ref, jnp.where(last, beyond, here_r) - jnp.where(first, side_l, here_l), dm),
                (h_ref, jnp.where(last, here_r, side_r) - side_l, dh),
            ):
                deep = ref[k + 2, top + 1 : top + 1 + SUB] - ref[k, top + 1 : top + 1 + SUB]
                down = ref[k + 1, top + 2 : top + 2 + SUB] - ref[k + 1, top : top + SUB]
                half = lax.rsqrt(deep * deep + down * down + cols * cols + 4.0)
                deep, down, cols = deep * half, down * half, cols * half
                for w in range(VIEWS):
                    a, b, c = towards[w]
                    dots[w, k, top : top + SUB] = deep * a + down * b + cols * c
        return carry

    tile = 32
    per_view = strip // tile
    base_row = y * rows + z * strip
    base_col = x * LANES
    lanes = lax.broadcasted_iota(jnp.int32, (tile, LANES), 1)
    rows_at = lax.broadcasted_iota(jnp.int32, (tile, LANES), 0)
    bias = [0.5 * palette[0, c] for c in range(3)]
    gain = [0.5 * palette[1, c] for c in range(3)]

    def march(w, top, brick, cells, start, colors, through):
        ambient = jnp.zeros((tile, LANES), jnp.float32)
        rate2 = rate[w] * (-math.log2(math.e))
        off_r, off_c = offset[brick, 0, w], offset[brick, 1, w]
        inside = jnp.logical_and(rows_at >= off_r - base_row - top, lanes >= off_c - base_col)
        fall = jnp.where(inside, rate2, 0.0)
        for j in range(bz):
            k = brick * bz + j
            sr = off_r + shear[w, 0, k]
            sc = off_c + shear[w, 1, k]
            at = HALO + top - sr
            wrap = lanes >= LANES - sc
            value = jnp.where(wrap, h_ref[k + 1, pl.ds(at, tile)], cells[start + j, pl.ds(at, tile)])
            dot = jnp.where(wrap, dh[w, k, pl.ds(at - 1, tile)], dm[w, k, pl.ds(at - 1, tile)])
            value = pltpu.roll(value, sc, 1)
            dot = pltpu.roll(dot, sc, 1)
            kept = jnp.exp2(fall * (1.0 + jnp.tanh(value)))
            weight = (0.125 + 0.375 * dot * dot) * ((1.0 - kept) * through)
            through = through * kept
            ambient = ambient + weight
            colors = [
                colors[c] + weight * jnp.tanh(bias[c] + gain[c] * value) for c in range(3)
            ]
        return [color + ambient for color in colors], through

    def views(act):
        def one(step, carry):
            act(step // per_view, (step % per_view) * tile)
            return carry

        lax.fori_loop(0, VIEWS * per_view, one, 0, unroll=VIEWS * per_view)

    def own_layer(w, top):
        at = pl.ds(top, tile)
        zero = jnp.zeros((tile, LANES), jnp.float32)
        colors, through = march(w, top, z, own_ref, 0, [zero] * 3, zero + 1.0)
        ahead = order[0, w] == z
        for c in range(3):
            out_ref[w, c, at] = jnp.where(ahead, colors[c], 0.0)
            back[w, c, at] = jnp.where(ahead, 0.0, colors[c])
        out_ref[w, 3, at] = jnp.where(ahead, through, 1.0)
        back[w, 3, at] = jnp.where(ahead, 1.0, through)

    def other_layer(w, top):
        at = pl.ds(top, tile)
        colors, through = march(
            w, top, 1 - z, m_ref, 1 + (1 - z) * bz, [out_ref[w, c, at] for c in range(3)],
            out_ref[w, 3, at],
        )
        for c in range(3):
            out_ref[w, c, at] = colors[c] + through * back[w, c, at]
        out_ref[w, 3, at] = 1.0 - through * back[w, 3, at]

    def each(start, stop):
        lax.fori_loop(start, stop, slopes, 0)

    each(z * (bz + 1), z * (bz + 1) + bz - 1)
    sided(middle)
    each(bz - 1, bz + 1)
    views(own_layer)
    sided(lambda mine: ending(mine, 1))
    each(bz + 1 - 3 * z, bz + 2 - 3 * z)
    sided(lambda mine: ending(mine, 2))
    each((1 - z) * (depth - 2), (1 - z) * (depth - 2) + 2)
    views(other_layer)
    sided(lambda mine: steps[mine][4]())


def two_bricks(mesh, pressure, light, palette, rate, shear, offset, order):
    bz, rows, cols = pressure.shape
    dims = (mesh.shape["gy"], mesh.shape["gx"], bz, rows)
    strip = rows // 2
    tall = HALO + strip + SUB
    depth = 2 * bz
    vmem = pl.BlockSpec(memory_space=pltpu.VMEM)
    hbm = pl.BlockSpec(memory_space=pltpu.HBM)
    f32 = jnp.float32
    _, sent, got = routes_of(dims)
    tables = (
        light,
        palette.T,
        rate,
        jnp.transpose(shear, (0, 2, 1)),
        jnp.transpose(offset, (1, 2, 0)),
        order.T,
    )
    image = pl.pallas_call(
        functools.partial(render, dims),
        out_shape=jax.ShapeDtypeStruct((VIEWS, 4, strip, LANES), f32),
        in_specs=[hbm] * 7,
        out_specs=vmem,
        scratch_shapes=[
            *[pltpu.SMEM(table.shape, table.dtype) for table in tables],
            pltpu.VMEM((bz, rows, LANES), f32),
            pltpu.VMEM((depth + 2, tall, LANES), f32),
            pltpu.VMEM((bz, tall, LANES), f32),
            pltpu.VMEM((2, got, LANES), f32),
            pltpu.VMEM((2, 2, SUB, LANES), f32),
            pltpu.VMEM((sent, LANES), f32),
            pltpu.VMEM((SUB, LANES), f32),
            pltpu.VMEM((depth + 2, tall, LANES), f32),
            pltpu.VMEM((2, tall, LANES), f32),
            pltpu.VMEM((VIEWS, depth, HALO + strip, LANES), f32),
            pltpu.VMEM((VIEWS, depth, HALO + strip, LANES), f32),
            pltpu.VMEM((VIEWS, 4, strip, LANES), f32),
            pltpu.SemaphoreType.DMA,
            pltpu.SemaphoreType.DMA((SLOTS,)),
            pltpu.SemaphoreType.REGULAR((3,)),
            pltpu.SemaphoreType.DMA((2,)),
            pltpu.SemaphoreType.DMA,
        ],
        compiler_params=pltpu.CompilerParams(collective_id=0, has_side_effects=True, vmem_limit_bytes=12 << 20),
        name="render",
    )(
        *[pltpu.with_memory_space_constraint(t, pltpu.HBM) for t in (*tables, pressure)]
    )
    return image[:, :, None]


def fits(mesh, shape):
    bz, rows, cols = shape
    return (
        mesh.shape["gz"] == 2
        and cols == LANES
        and rows % 64 == 0
        and 2 * HALO <= rows <= LANES
        and bz * (HALO - SUB) == LANES
        and bz * (rows // SUB) <= LANES
    )


def on_device(mesh, pressure, *rest):
    if fits(mesh, pressure.shape):
        return two_bricks(mesh, pressure, *rest)
    return many_bricks(pressure, *rest)


def solution(mesh):
    return jax.shard_map(
        functools.partial(on_device, mesh),
        mesh=mesh,
        in_specs=(P("gz", "gy", "gx"), P(), P(), P(), P(), P(), P()),
        out_specs=P(None, None, "gz", "gy", "gx"),
        check_vma=False,
    )
```

```python
import functools
import math

import jax
import jax.numpy as jnp
from jax import lax
from jax.experimental import pallas as pl
from jax.experimental.pallas import tpu as pltpu
from jax.sharding import PartitionSpec as P

VIEWS = 4
SHEAR = 8
REACH = 32
HALO = SHEAR + REACH
SUB = 8
LANES = 128
MESH = pl.DeviceIdType.MESH


def padded(cells, sides, width):
    for axis, dim in sides:
        count = lax.axis_size(axis)
        ends = count - 1
        head = lax.slice_in_dim(cells, 0, width, axis=dim)
        tail = lax.slice_in_dim(cells, cells.shape[dim] - width, cells.shape[dim], axis=dim)
        cells = jnp.concatenate(
            [
                lax.ppermute(tail, axis, [(i, (i + 1) % count) for i in range(ends)]),
                cells,
                lax.ppermute(head, axis, [((i + 1) % count, i) for i in range(ends)]),
            ],
            axis=dim,
        )
    return cells


def shifted(value, axis, steps):
    count = lax.axis_size(axis)
    first, last = (max(0, -steps), min(count, count - steps))
    return lax.ppermute(value, axis, [(source, source + steps) for source in range(first, last)])


def surface_terms(slab):
    inner = slab[1:-1, 1:-1, 1:-1]
    grad_depth = 0.5 * (slab[2:, 1:-1, 1:-1] - slab[:-2, 1:-1, 1:-1])
    grad_rows = 0.5 * (slab[1:-1, 2:, 1:-1] - slab[1:-1, :-2, 1:-1])
    grad_cols = 0.5 * (slab[1:-1, 1:-1, 2:] - slab[1:-1, 1:-1, :-2])
    factor = lax.rsqrt(
        grad_depth * grad_depth + grad_rows * grad_rows + grad_cols * grad_cols + 1.0
    )
    return (inner, (grad_depth * factor, grad_rows * factor, grad_cols * factor))


def render_layers(inner, normals, shifts, light, palette, rate, rows, cols):
    lengths = jnp.sqrt(jnp.sum(light * light, axis=1, keepdims=True) + 1.0)
    towards = light / lengths
    offsets = palette[:, 0][:, None, None]
    slopes = palette[:, 1][:, None, None]
    layers = []
    for view in range(light.shape[0]):

        def advance(carry, items):
            color, depth = carry
            value_slab, normal_depth, normal_rows, normal_cols, moved = items
            start = (SHEAR - moved[0], SHEAR - moved[1])
            value = lax.dynamic_slice(value_slab, start, (rows, cols))
            dot = (
                lax.dynamic_slice(normal_depth, start, (rows, cols)) * towards[view, 0]
                + lax.dynamic_slice(normal_rows, start, (rows, cols)) * towards[view, 1]
                + lax.dynamic_slice(normal_cols, start, (rows, cols)) * towards[view, 2]
            )
            shade = 0.25 + 0.75 * dot * dot
            density = rate[view] * (1.0 + jnp.tanh(value))
            alpha = 1.0 - jnp.exp(-density)
            weight = alpha * jnp.exp(-depth)
            hues = jax.nn.sigmoid(offsets + slopes * value[None]) * shade[None]
            return ((color + hues * weight[None], depth + density), None)

        start_carry = (
            jnp.zeros((3, rows, cols), jnp.float32),
            jnp.zeros((rows, cols), jnp.float32),
        )
        (color, depth), _ = lax.scan(
            advance, start_carry, (inner, normals[0], normals[1], normals[2], shifts[view])
        )
        layers.append(jnp.concatenate([color, depth[None]], axis=0))
    return jnp.stack(layers)


def precedence(order):
    bricks = order.shape[1]
    onehot = (order[:, :, None] == jnp.arange(bricks, dtype=jnp.int32)[None, None, :]).astype(
        jnp.float32
    )
    ranks = jnp.sum(onehot * jnp.arange(bricks, dtype=jnp.float32)[None, :, None], axis=1)
    return (ranks[:, None, :] < ranks[:, :, None]).astype(jnp.float32)


def many_bricks(pressure, light, palette, rate, shear, offset, order):
    depth_cells, rows, cols = pressure.shape
    brick = lax.axis_index("gz")
    zero = jnp.zeros((), jnp.int32)
    widened = padded(pressure, (("gy", 1), ("gx", 2)), SHEAR + 1)
    slab = padded(widened, (("gz", 0),), 1)
    inner, normals = surface_terms(slab)
    shifts = lax.dynamic_slice(shear, (zero, brick * depth_cells, zero), (VIEWS, depth_cells, 2))
    layers = render_layers(inner, normals, shifts, light, palette, rate, rows, cols)
    moved = lax.dynamic_index_in_dim(offset, brick, 1, keepdims=False)
    blank = jnp.zeros((4, rows + REACH, cols + REACH), jnp.float32)
    canvas = jnp.stack(
        [
            lax.dynamic_update_slice(blank, layers[view], (zero, moved[view, 0], moved[view, 1]))
            for view in range(VIEWS)
        ]
    )
    own_tile = canvas[:, :, :rows, :cols]
    from_above = shifted(canvas[:, :, rows:, :cols], "gy", 1)
    from_left = shifted(canvas[:, :, :rows, cols:], "gx", 1)
    from_diagonal = shifted(canvas[:, :, rows:, cols:], ("gy", "gx"), lax.axis_size("gx") + 1)
    from_diagonal = from_diagonal * (lax.axis_index("gx") > 0).astype(jnp.float32)
    own_tile = own_tile.at[:, :, :REACH, :].add(from_above)
    own_tile = own_tile.at[:, :, :, :REACH].add(from_left)
    own_tile = own_tile.at[:, :, :REACH, :REACH].add(from_diagonal)
    ranking = precedence(order)
    pieces = lax.all_to_all(own_tile[None], "gz", split_axis=3, concat_axis=0, tiled=True)
    depths = pieces[:, :, 3]
    cover = jnp.einsum("vbc,cvyx->bvyx", ranking, depths, precision=lax.Precision.HIGHEST)
    colors = jnp.sum(pieces[:, :, :3] * jnp.exp(-cover)[:, :, None], axis=0)
    opacity = 1.0 - jnp.exp(-jnp.sum(depths, axis=0))
    image = jnp.concatenate([colors, opacity[:, None]], axis=1)
    return image[:, :, None]


class Route:
    def __init__(self, dims, side, step, start, count, slab, half):
        bz = dims[2]
        self.side, self.step, self.half = side, step, half
        self.slab = pl.ds(slab, count)
        needed = count - SUB + 1 if start == 0 else count
        self.rows, self.lands = pl.ds(start, needed), pl.ds(slab, needed)
        self.groups = LANES // (SUB * bz)
        self.tiles = range(start // SUB, (start + count) // SUB)
        self.first = slab // SUB
        self.folds = range(
            self.tiles[0] // self.groups, self.tiles[-1] // self.groups + 1
        )
        self.size = (len(self.tiles) + len(self.folds)) * SUB
        self.base = self.sent = 0

    def there(self, y, ny):
        return y + self.step >= 0 if self.step < 0 else y + self.step < ny

    def comes(self, y, ny):
        return y - self.step < ny if self.step < 0 else y - self.step >= 0

    def wide(self, tile):
        return (tile - self.tiles[0]) * SUB

    def narrow(self, fold):
        return (len(self.tiles) + fold - self.folds[0]) * SUB


def routes_of(dims):
    rows = dims[3]
    strip = rows // 2
    routes = [
        Route(dims, 0, 0, 0, strip + SUB, HALO, 0),
        Route(dims, 0, 1, rows - HALO, HALO, 0, 1),
        Route(dims, 1, 0, strip - HALO, HALO + strip, 0, 0),
        Route(dims, 1, -1, 0, SUB, HALO + strip, 1),
    ]
    sent = 0
    for route in routes:
        route.sent = sent
        sent += route.size
    routes[1].base, routes[3].base = routes[0].size, routes[2].size
    return routes, sent, max(routes[0].size + routes[1].size, routes[2].size + routes[3].size)


MAIN, EDGE, BESIDE, COLS, ENDS, SLOTS = 0, 3, 6, 7, 11, 15
PARTS = 3
BELOW, RIGHT, ACROSS = range(3)


def exchange(
    dims, mine, here, p_ref, m_ref, cols_out, cols_in, ends_out, ends_in, sends, arrivals, ready
):
    ny, nx, bz, rows = dims
    z, y, x = here
    has_left, has_right = x > 0, x < nx - 1
    has_up, has_down = y > 0, y < ny - 1
    routes = routes_of(dims)[0]

    def remote(src, dst, arrival, who):
        return pltpu.make_async_remote_copy(
            src_ref=src,
            dst_ref=dst,
            send_sem=sends,
            recv_sem=arrivals.at[arrival],
            device_id=who,
            device_id_type=MESH,
        )

    def rows_of(brick, route, part):
        first = bz - PARTS + 1
        start = first + part - 1 if part else 0
        count = bz if part is None else 1 if part else first
        if part is not None and brick == 0:
            start = bz - start - count
        slot = BESIDE if part is None else (EDGE if route.half else MAIN) + part
        return remote(
            p_ref.at[pl.ds(start, count), route.rows],
            m_ref.at[pl.ds(1 + brick * bz + start, count), route.lands],
            slot, (route.side, y + route.step, x),
        )

    def cols_of(brick, route):
        return remote(
            cols_out.at[pl.ds(route.sent, route.size)],
            cols_in.at[brick, pl.ds(route.base, route.size)],
            COLS + 2 * brick + route.half,
            (route.side, y + route.step, x + 1),
        )

    def ends_of(brick, route):
        return remote(
            ends_out,
            ends_in.at[brick, route.half],
            ENDS + 2 * brick + route.half,
            (route.side, y + route.step, x - 1),
        )

    def rows_out(route, part=0):
        there = route.there(y, ny)
        if route.side != mine:
            return [(there, rows_of(mine, route, part))]
        return [(there, rows_of(mine, route, None))] if route.half else []

    def cols_sent(same):
        return [
            (jnp.logical_and(r.there(y, ny), has_right), cols_of(mine, r))
            for r in routes
            if (r.side == mine) == same
        ]

    def ends_sent():
        return [(jnp.logical_and(r.there(y, ny), has_left), ends_of(mine, r)) for r in routes]

    def apply(pairs, act):
        for there, copy in pairs:

            @pl.when(there)
            def _():
                act(copy)

    def start(pairs):
        apply(pairs, lambda copy: copy.start())

    def heard(kind, there, count):
        @pl.when(there)
        def _():
            pl.semaphore_wait(ready.at[kind], count)

    mains, own_halo, halos = (
        (routes[2], routes[1], routes[3]) if mine == 0 else (routes[0], routes[3], routes[1])
    )
    next_ones = [1 + there.astype(jnp.int32) for there in (has_down, has_up)]

    def send_first():
        if mine == 0:
            start(rows_out(halos))
            start(rows_out(mains))
        else:
            start(rows_out(mains))
            start(rows_out(own_halo))

    def send_rest():
        if mine == 0:
            start(ends_sent())
            heard(BELOW, has_down, 1)
            start(rows_out(own_halo))
        else:
            start(ends_sent())
        heard(RIGHT, has_right, next_ones[mine])
        start(cols_sent(True))
        if mine == 1:
            heard(BELOW, has_down, 1)
            start(rows_out(halos))
        heard(ACROSS, has_right, next_ones[1 - mine])
        start(cols_sent(False))
        for part in range(1, PARTS):
            start(rows_out(halos, part) + rows_out(mains, part))

    def receive(brick, parts, sides):
        pairs = []
        for route in routes:
            if route.side != mine:
                continue
            comes = route.comes(y, ny)
            if brick != mine:
                pairs += [(comes, rows_of(brick, route, part)) for part in parts]
            elif route.half:
                pairs += [(comes, rows_of(brick, route, None))]
            if sides:
                pairs += [
                    (jnp.logical_and(comes, has_left), cols_of(brick, route)),
                    (jnp.logical_and(comes, has_right), ends_of(brick, route)),
                ]
        apply(pairs, lambda copy: copy.wait_recv())

    def close():
        for part in range(PARTS):
            apply(rows_out(mains, part) + rows_out(halos, part), lambda copy: copy.wait_send())
        apply(rows_out(own_halo), lambda copy: copy.wait_send())
        apply(ends_sent() + cols_sent(True) + cols_sent(False), lambda copy: copy.wait_send())

    return send_first, send_rest, receive, close


def partners_of(dims, here, over):
    ny, nx = dims[:2]
    z, y, x = here
    steps = [(z, over, 0), (1 - z, 0, 0)]
    diagonal = z == 1 if over > 0 else z == 0
    yield jnp.logical_and(diagonal, inside_of(dims, y + over, x)), (1 - z, y + over, x)
    steps += [
        (side, step, over)
        for side, step in ((z, -1), (z, 0), (z, 1), (1 - z, 0), (1 - z, 2 * z - 1))
    ]
    for side, step, across in steps:
        yield inside_of(dims, y + step, x + across), (side, y + step, x + across)


def inside_of(dims, y, x):
    ny, nx = dims[:2]
    return jnp.logical_and(
        jnp.logical_and(y >= 0, y < ny), jnp.logical_and(x >= 0, x < nx)
    )


def answers_of(dims, here):
    z, y, x = here
    own = z == 0
    yield jnp.logical_and(own, y > 0), (z, y - 1, x), BELOW
    yield jnp.logical_and(own, y > 0), (1 - z, y - 1, x), BELOW
    for side, kind in ((z, RIGHT), (1 - z, ACROSS)):
        for step in (0, 2 * z - 1):
            yield inside_of(dims, y + step, x - 1), (side, y + step, x - 1), kind


def render(
    dims, light_in, palette_in, rate_in, shear_in, offset_in, order_in, p_ref, out_ref,
    light, palette, rate, shear, offset, order, tile_ref, m_ref, own_ref, cols_in, ends_in,
    cols_out, ends_out, h_ref, r_ref, dm, dh, back, sends, arrivals, ready, local_sems, table_sem,
):
    ny, nx, bz, rows = dims
    strip = rows // 2
    tall = HALO + strip + SUB
    depth = 2 * bz
    blocks = (HALO + strip) // SUB
    wide_lanes = HALO - SUB
    z, y, x = lax.axis_index("gz"), lax.axis_index("gy"), lax.axis_index("gx")
    routes = routes_of(dims)[0]

    tables = [
        pltpu.make_async_copy(source, target, table_sem)
        for source, target in (
            (light_in, light), (palette_in, palette), (rate_in, rate),
            (shear_in, shear), (offset_in, offset), (order_in, order),
        )
    ]
    barrier = pltpu.get_barrier_semaphore()

    def sided(act):
        for mine in range(2):

            @pl.when(z == mine)
            def _():
                act(mine)

    for there, who in partners_of(dims, (z, y, x), 1):

        @pl.when(there)
        def _():
            pl.semaphore_signal(barrier, inc=1, device_id=who, device_id_type=MESH)

    count = 0
    for there, _ in partners_of(dims, (z, y, x), -1):
        count = count + there.astype(jnp.int32)

    steps = [
        exchange(
            dims, mine, (z, y, x), p_ref, m_ref, cols_out, cols_in, ends_out, ends_in,
            sends, arrivals, ready,
        )
        for mine in range(2)
    ]

    def local_slab(mine):
        route = routes[2 * mine]
        return pltpu.make_async_copy(
            p_ref.at[:, route.rows], m_ref.at[pl.ds(1 + mine * bz, bz), route.lands],
            local_sems.at[1],
        )

    local_tile = pltpu.make_async_copy(p_ref, tile_ref, local_sems.at[0])
    local_tile.start()
    sided(lambda mine: local_slab(mine).start())
    for copy in tables:
        copy.start()

    @pl.when(count > 0)
    def _():
        pl.semaphore_wait(barrier, count)

    for there, who, kind in answers_of(dims, (z, y, x)):

        @pl.when(there)
        def _():
            pl.semaphore_signal(ready.at[kind], inc=1, device_id=who, device_id_type=MESH)


    sided(lambda mine: steps[mine][0]())

    empty = jnp.zeros((tall, LANES), jnp.float32)
    for ref in (m_ref, h_ref):
        ref[0] = empty
        ref[depth + 1] = empty

    def blank(mine):
        route = routes[2 * mine + 1]

        @pl.when(jnp.logical_not(route.comes(y, ny)))
        def _():
            m_ref[:, route.slab] = jnp.zeros((depth + 2, len(route.tiles) * SUB, LANES), jnp.float32)
            cols_in[:, route.base : route.base + route.size] = jnp.zeros(
                (2, route.size, LANES), jnp.float32
            )
            ends_in[:, 1] = jnp.zeros((2, SUB, LANES), jnp.float32)

    sided(blank)

    @pl.when(x == 0)
    def _():
        cols_in[...] = jnp.zeros(cols_in.shape, jnp.float32)

    @pl.when(x == nx - 1)
    def _():
        ends_in[...] = jnp.zeros(ends_in.shape, jnp.float32)

    lane = lax.broadcasted_iota(jnp.int32, (SUB, LANES), 1)
    last = lane == LANES - 1
    first = lane == 0
    groups = routes[0].groups
    tiles = rows // SUB

    def cell(j, t):
        return tile_ref[j, t * SUB : (t + 1) * SUB]

    def put(t_or_fold, is_wide, value):
        for route in routes:
            if t_or_fold in (route.tiles if is_wide else route.folds):
                at = route.sent + (route.wide if is_wide else route.narrow)(t_or_fold)
                cols_out[at : at + SUB] = value

    def merged(pieces):
        while len(pieces) > 1:
            pieces = [
                (a[0], jnp.where(lane >= b[0], b[1], a[1]))
                for a, b in zip(pieces[::2], pieces[1::2])
            ] + (pieces[-1:] if len(pieces) % 2 else [])
        return pieces[0][1]

    def turned(value, by):
        return pltpu.roll(value, by % LANES, 1) if by % LANES else value

    local_tile.wait()
    for t in range(tiles):
        put(
            t, True,
            merged(
                [(wide_lanes * j, turned(cell(j, t), wide_lanes * (j + 1))) for j in range(bz)]
            ),
        )
    for fold in range(tiles // groups):
        put(
            fold, False,
            merged(
                [
                    (
                        SUB * (bz * g + j),
                        turned(cell(j, fold * groups + g), SUB * (bz * g + j) + HALO),
                    )
                    for g in range(groups)
                    for j in range(bz)
                ]
            ),
        )
    ends_out[...] = merged(
        [(t * bz + j, turned(cell(j, t), t * bz + j)) for t in range(tiles) for j in range(bz)]
    )

    def unpack(mine, brick):
        for route in routes[2 * mine : 2 * mine + 2]:
            for t in route.tiles:
                row = (route.first + t - route.tiles[0]) * SUB
                at = route.base + route.wide(t)
                wide = cols_in[brick, at : at + SUB]
                at = route.base + route.narrow(t // groups)
                narrow = cols_in[brick, at : at + SUB]
                for j in range(bz):
                    h_ref[1 + brick * bz + j, row : row + SUB] = jnp.where(
                        lane >= LANES - wide_lanes,
                        turned(wide, -wide_lanes * (j + 1)),
                        turned(narrow, -SUB * (bz * (t % groups) + j) - HALO),
                    )
                r_ref[brick, row : row + SUB] = turned(
                    ends_in[brick, route.half], LANES - 1 - t * bz
                )

    def opening(mine):
        _, send_rest, receive, _ = steps[mine]
        send_rest()
        local_slab(mine).wait()
        receive(mine, (), True)
        own_ref[...] = m_ref[1 + mine * bz : 1 + (mine + 1) * bz]
        unpack(mine, mine)

    def middle(mine):
        receive = steps[mine][2]
        receive(1 - mine, (0,), True)
        unpack(mine, 1 - mine)

    def ending(mine, part):
        receive = steps[mine][2]
        receive(1 - mine, (part,), False)

    sided(opening)
    for copy in tables:
        copy.wait()

    towards = []
    for w in range(VIEWS):
        a, b, c = light[w, 0], light[w, 1], light[w, 2]
        inverse = lax.rsqrt(jnp.full((SUB, LANES), a * a + b * b + c * c + 1.0, jnp.float32))
        towards.append((a * inverse, b * inverse, c * inverse))

    def slopes(k, carry):
        for i in range(blocks):
            top = i * SUB
            here = m_ref[k + 1, top + 1 : top + 1 + SUB]
            side = h_ref[k + 1, top + 1 : top + 1 + SUB]
            beyond = pltpu.roll(
                r_ref[k // bz, top + 1 : top + 1 + SUB], (LANES - k % bz) % LANES, 1
            )
            here_r, here_l = pltpu.roll(here, LANES - 1, 1), pltpu.roll(here, 1, 1)
            side_r, side_l = pltpu.roll(side, LANES - 1, 1), pltpu.roll(side, 1, 1)
            for ref, cols, dots in (
                (m_ref, jnp.where(last, beyond, here_r) - jnp.where(first, side_l, here_l), dm),
                (h_ref, jnp.where(last, here_r, side_r) - side_l, dh),
            ):
                deep = ref[k + 2, top + 1 : top + 1 + SUB] - ref[k, top + 1 : top + 1 + SUB]
                down = ref[k + 1, top + 2 : top + 2 + SUB] - ref[k + 1, top : top + SUB]
                half = lax.rsqrt(deep * deep + down * down + cols * cols + 4.0)
                deep, down, cols = deep * half, down * half, cols * half
                for w in range(VIEWS):
                    a, b, c = towards[w]
                    dots[w, k, top : top + SUB] = deep * a + down * b + cols * c
        return carry

    tile = 32
    per_view = strip // tile
    base_row = y * rows + z * strip
    base_col = x * LANES
    lanes = lax.broadcasted_iota(jnp.int32, (tile, LANES), 1)
    rows_at = lax.broadcasted_iota(jnp.int32, (tile, LANES), 0)
    bias = [0.5 * palette[0, c] for c in range(3)]
    gain = [0.5 * palette[1, c] for c in range(3)]

    def march(w, top, brick, cells, start, colors, through):
        ambient = jnp.zeros((tile, LANES), jnp.float32)
        rate2 = rate[w] * (-math.log2(math.e))
        off_r, off_c = offset[brick, 0, w], offset[brick, 1, w]
        inside = jnp.logical_and(rows_at >= off_r - base_row - top, lanes >= off_c - base_col)
        fall = jnp.where(inside, rate2, 0.0)
        for j in range(bz):
            k = brick * bz + j
            sr = off_r + shear[w, 0, k]
            sc = off_c + shear[w, 1, k]
            at = HALO + top - sr
            wrap = lanes >= LANES - sc
            value = jnp.where(wrap, h_ref[k + 1, pl.ds(at, tile)], cells[start + j, pl.ds(at, tile)])
            dot = jnp.where(wrap, dh[w, k, pl.ds(at - 1, tile)], dm[w, k, pl.ds(at - 1, tile)])
            value = pltpu.roll(value, sc, 1)
            dot = pltpu.roll(dot, sc, 1)
            kept = jnp.exp2(fall * (1.0 + jnp.tanh(value)))
            weight = (0.125 + 0.375 * dot * dot) * ((1.0 - kept) * through)
            through = through * kept
            ambient = ambient + weight
            colors = [
                colors[c] + weight * jnp.tanh(bias[c] + gain[c] * value) for c in range(3)
            ]
        return [color + ambient for color in colors], through

    def views(act):
        def one(step, carry):
            act(step // per_view, (step % per_view) * tile)
            return carry

        lax.fori_loop(0, VIEWS * per_view, one, 0, unroll=VIEWS * per_view)

    def own_layer(w, top):
        at = pl.ds(top, tile)
        zero = jnp.zeros((tile, LANES), jnp.float32)
        colors, through = march(w, top, z, own_ref, 0, [zero] * 3, zero + 1.0)
        ahead = order[0, w] == z
        for c in range(3):
            out_ref[w, c, at] = jnp.where(ahead, colors[c], 0.0)
            back[w, c, at] = jnp.where(ahead, 0.0, colors[c])
        out_ref[w, 3, at] = jnp.where(ahead, through, 1.0)
        back[w, 3, at] = jnp.where(ahead, 1.0, through)

    def other_layer(w, top):
        at = pl.ds(top, tile)
        colors, through = march(
            w, top, 1 - z, m_ref, 1 + (1 - z) * bz, [out_ref[w, c, at] for c in range(3)],
            out_ref[w, 3, at],
        )
        for c in range(3):
            out_ref[w, c, at] = colors[c] + through * back[w, c, at]
        out_ref[w, 3, at] = 1.0 - through * back[w, 3, at]

    def each(start, stop):
        lax.fori_loop(start, stop, slopes, 0)

    each(z * (bz + 1), z * (bz + 1) + bz - 1)
    sided(middle)
    each(bz - 1, bz + 1)
    views(own_layer)
    sided(lambda mine: ending(mine, 1))
    each(bz + 1 - 3 * z, bz + 2 - 3 * z)
    sided(lambda mine: ending(mine, 2))
    each((1 - z) * (depth - 2), (1 - z) * (depth - 2) + 2)
    views(other_layer)
    sided(lambda mine: steps[mine][3]())


def two_bricks(mesh, pressure, light, palette, rate, shear, offset, order):
    bz, rows, cols = pressure.shape
    dims = (mesh.shape["gy"], mesh.shape["gx"], bz, rows)
    strip = rows // 2
    tall = HALO + strip + SUB
    depth = 2 * bz
    vmem = pl.BlockSpec(memory_space=pltpu.VMEM)
    hbm = pl.BlockSpec(memory_space=pltpu.HBM)
    f32 = jnp.float32
    _, sent, got = routes_of(dims)
    tables = (
        light,
        palette.T,
        rate,
        jnp.transpose(shear, (0, 2, 1)),
        jnp.transpose(offset, (1, 2, 0)),
        order.T,
    )
    image = pl.pallas_call(
        functools.partial(render, dims),
        out_shape=jax.ShapeDtypeStruct((VIEWS, 4, strip, LANES), f32),
        in_specs=[hbm] * 7,
        out_specs=vmem,
        scratch_shapes=[
            *[pltpu.SMEM(table.shape, table.dtype) for table in tables],
            pltpu.VMEM((bz, rows, LANES), f32),
            pltpu.VMEM((depth + 2, tall, LANES), f32),
            pltpu.VMEM((bz, tall, LANES), f32),
            pltpu.VMEM((2, got, LANES), f32),
            pltpu.VMEM((2, 2, SUB, LANES), f32),
            pltpu.VMEM((sent, LANES), f32),
            pltpu.VMEM((SUB, LANES), f32),
            pltpu.VMEM((depth + 2, tall, LANES), f32),
            pltpu.VMEM((2, tall, LANES), f32),
            pltpu.VMEM((VIEWS, depth, HALO + strip, LANES), f32),
            pltpu.VMEM((VIEWS, depth, HALO + strip, LANES), f32),
            pltpu.VMEM((VIEWS, 4, strip, LANES), f32),
            pltpu.SemaphoreType.DMA,
            pltpu.SemaphoreType.DMA((SLOTS,)),
            pltpu.SemaphoreType.REGULAR((3,)),
            pltpu.SemaphoreType.DMA((2,)),
            pltpu.SemaphoreType.DMA,
        ],
        compiler_params=pltpu.CompilerParams(collective_id=0, has_side_effects=True, vmem_limit_bytes=12 << 20),
        name="render",
    )(
        *[pltpu.with_memory_space_constraint(t, pltpu.HBM) for t in (*tables, pressure)]
    )
    return image[:, :, None]


def fits(mesh, shape):
    bz, rows, cols = shape
    return (
        mesh.shape["gz"] == 2
        and cols == LANES
        and rows % 64 == 0
        and 2 * HALO <= rows <= LANES
        and bz * (HALO - SUB) == LANES
        and bz * (rows // SUB) <= LANES
    )


def on_device(mesh, pressure, *rest):
    if fits(mesh, pressure.shape):
        return two_bricks(mesh, pressure, *rest)
    return many_bricks(pressure, *rest)


def solution(mesh):
    return jax.shard_map(
        functools.partial(on_device, mesh),
        mesh=mesh,
        in_specs=(P("gz", "gy", "gx"), P(), P(), P(), P(), P(), P()),
        out_specs=P(None, None, "gz", "gy", "gx"),
        check_vma=False,
    )
```

```python
import functools
import math

import jax
import jax.numpy as jnp
from jax import lax
from jax.experimental import pallas as pl
from jax.experimental.pallas import tpu as pltpu
from jax.sharding import PartitionSpec as P

VIEWS = 4
SHEAR = 8
REACH = 32
HALO = SHEAR + REACH
SUB = 8
LANES = 128
MESH = pl.DeviceIdType.MESH


def padded(cells, sides, width):
    for axis, dim in sides:
        count = lax.axis_size(axis)
        ends = count - 1
        head = lax.slice_in_dim(cells, 0, width, axis=dim)
        tail = lax.slice_in_dim(cells, cells.shape[dim] - width, cells.shape[dim], axis=dim)
        cells = jnp.concatenate(
            [
                lax.ppermute(tail, axis, [(i, (i + 1) % count) for i in range(ends)]),
                cells,
                lax.ppermute(head, axis, [((i + 1) % count, i) for i in range(ends)]),
            ],
            axis=dim,
        )
    return cells


def shifted(value, axis, steps):
    count = lax.axis_size(axis)
    first, last = (max(0, -steps), min(count, count - steps))
    return lax.ppermute(value, axis, [(source, source + steps) for source in range(first, last)])


def surface_terms(slab):
    inner = slab[1:-1, 1:-1, 1:-1]
    grad_depth = 0.5 * (slab[2:, 1:-1, 1:-1] - slab[:-2, 1:-1, 1:-1])
    grad_rows = 0.5 * (slab[1:-1, 2:, 1:-1] - slab[1:-1, :-2, 1:-1])
    grad_cols = 0.5 * (slab[1:-1, 1:-1, 2:] - slab[1:-1, 1:-1, :-2])
    factor = lax.rsqrt(
        grad_depth * grad_depth + grad_rows * grad_rows + grad_cols * grad_cols + 1.0
    )
    return (inner, (grad_depth * factor, grad_rows * factor, grad_cols * factor))


def render_layers(inner, normals, shifts, light, palette, rate, rows, cols):
    lengths = jnp.sqrt(jnp.sum(light * light, axis=1, keepdims=True) + 1.0)
    towards = light / lengths
    offsets = palette[:, 0][:, None, None]
    slopes = palette[:, 1][:, None, None]
    layers = []
    for view in range(light.shape[0]):

        def advance(carry, items):
            color, depth = carry
            value_slab, normal_depth, normal_rows, normal_cols, moved = items
            start = (SHEAR - moved[0], SHEAR - moved[1])
            value = lax.dynamic_slice(value_slab, start, (rows, cols))
            dot = (
                lax.dynamic_slice(normal_depth, start, (rows, cols)) * towards[view, 0]
                + lax.dynamic_slice(normal_rows, start, (rows, cols)) * towards[view, 1]
                + lax.dynamic_slice(normal_cols, start, (rows, cols)) * towards[view, 2]
            )
            shade = 0.25 + 0.75 * dot * dot
            density = rate[view] * (1.0 + jnp.tanh(value))
            alpha = 1.0 - jnp.exp(-density)
            weight = alpha * jnp.exp(-depth)
            hues = jax.nn.sigmoid(offsets + slopes * value[None]) * shade[None]
            return ((color + hues * weight[None], depth + density), None)

        start_carry = (
            jnp.zeros((3, rows, cols), jnp.float32),
            jnp.zeros((rows, cols), jnp.float32),
        )
        (color, depth), _ = lax.scan(
            advance, start_carry, (inner, normals[0], normals[1], normals[2], shifts[view])
        )
        layers.append(jnp.concatenate([color, depth[None]], axis=0))
    return jnp.stack(layers)


def precedence(order):
    bricks = order.shape[1]
    onehot = (order[:, :, None] == jnp.arange(bricks, dtype=jnp.int32)[None, None, :]).astype(
        jnp.float32
    )
    ranks = jnp.sum(onehot * jnp.arange(bricks, dtype=jnp.float32)[None, :, None], axis=1)
    return (ranks[:, None, :] < ranks[:, :, None]).astype(jnp.float32)


def many_bricks(pressure, light, palette, rate, shear, offset, order):
    depth_cells, rows, cols = pressure.shape
    brick = lax.axis_index("gz")
    zero = jnp.zeros((), jnp.int32)
    widened = padded(pressure, (("gy", 1), ("gx", 2)), SHEAR + 1)
    slab = padded(widened, (("gz", 0),), 1)
    inner, normals = surface_terms(slab)
    shifts = lax.dynamic_slice(shear, (zero, brick * depth_cells, zero), (VIEWS, depth_cells, 2))
    layers = render_layers(inner, normals, shifts, light, palette, rate, rows, cols)
    moved = lax.dynamic_index_in_dim(offset, brick, 1, keepdims=False)
    blank = jnp.zeros((4, rows + REACH, cols + REACH), jnp.float32)
    canvas = jnp.stack(
        [
            lax.dynamic_update_slice(blank, layers[view], (zero, moved[view, 0], moved[view, 1]))
            for view in range(VIEWS)
        ]
    )
    own_tile = canvas[:, :, :rows, :cols]
    from_above = shifted(canvas[:, :, rows:, :cols], "gy", 1)
    from_left = shifted(canvas[:, :, :rows, cols:], "gx", 1)
    from_diagonal = shifted(canvas[:, :, rows:, cols:], ("gy", "gx"), lax.axis_size("gx") + 1)
    from_diagonal = from_diagonal * (lax.axis_index("gx") > 0).astype(jnp.float32)
    own_tile = own_tile.at[:, :, :REACH, :].add(from_above)
    own_tile = own_tile.at[:, :, :, :REACH].add(from_left)
    own_tile = own_tile.at[:, :, :REACH, :REACH].add(from_diagonal)
    ranking = precedence(order)
    pieces = lax.all_to_all(own_tile[None], "gz", split_axis=3, concat_axis=0, tiled=True)
    depths = pieces[:, :, 3]
    cover = jnp.einsum("vbc,cvyx->bvyx", ranking, depths, precision=lax.Precision.HIGHEST)
    colors = jnp.sum(pieces[:, :, :3] * jnp.exp(-cover)[:, :, None], axis=0)
    opacity = 1.0 - jnp.exp(-jnp.sum(depths, axis=0))
    image = jnp.concatenate([colors, opacity[:, None]], axis=1)
    return image[:, :, None]


class Route:
    def __init__(self, dims, side, step, start, count, slab, half):
        bz = dims[2]
        self.side, self.step, self.half = side, step, half
        self.slab = pl.ds(slab, count)
        needed = count - SUB + 1 if start == 0 else count
        self.rows, self.lands = pl.ds(start, needed), pl.ds(slab, needed)
        self.groups = LANES // (SUB * bz)
        self.tiles = range(start // SUB, (start + count) // SUB)
        self.first = slab // SUB
        self.folds = range(
            self.tiles[0] // self.groups, self.tiles[-1] // self.groups + 1
        )
        self.size = (len(self.tiles) + len(self.folds)) * SUB
        self.base = self.sent = 0

    def there(self, y, ny):
        return y + self.step >= 0 if self.step < 0 else y + self.step < ny

    def comes(self, y, ny):
        return y - self.step < ny if self.step < 0 else y - self.step >= 0

    def wide(self, tile):
        return (tile - self.tiles[0]) * SUB

    def narrow(self, fold):
        return (len(self.tiles) + fold - self.folds[0]) * SUB


def routes_of(dims):
    rows = dims[3]
    strip = rows // 2
    routes = [
        Route(dims, 0, 0, 0, strip + SUB, HALO, 0),
        Route(dims, 0, 1, rows - HALO, HALO, 0, 1),
        Route(dims, 1, 0, strip - HALO, HALO + strip, 0, 0),
        Route(dims, 1, -1, 0, SUB, HALO + strip, 1),
    ]
    sent = 0
    for route in routes:
        route.sent = sent
        sent += route.size
    routes[1].base, routes[3].base = routes[0].size, routes[2].size
    return routes, sent, max(routes[0].size + routes[1].size, routes[2].size + routes[3].size)


MAIN, EDGE, BESIDE, COLS, ENDS, SLOTS = 0, 3, 6, 7, 11, 15
PARTS = 3
BELOW, RIGHT, ACROSS = range(3)


def exchange(
    dims, mine, here, p_ref, m_ref, cols_out, cols_in, ends_out, ends_in, sends, arrivals, ready
):
    ny, nx, bz, rows = dims
    z, y, x = here
    has_left, has_right = x > 0, x < nx - 1
    has_up, has_down = y > 0, y < ny - 1
    routes = routes_of(dims)[0]

    def remote(src, dst, arrival, who):
        return pltpu.make_async_remote_copy(
            src_ref=src,
            dst_ref=dst,
            send_sem=sends,
            recv_sem=arrivals.at[arrival],
            device_id=who,
            device_id_type=MESH,
        )

    def rows_of(brick, route, part):
        first = bz - PARTS + 1
        start = first + part - 1 if part else 0
        count = bz if part is None else 1 if part else first
        if part is not None and brick == 0:
            start = bz - start - count
        slot = BESIDE if part is None else (EDGE if route.half else MAIN) + part
        return remote(
            p_ref.at[pl.ds(start, count), route.rows],
            m_ref.at[pl.ds(1 + brick * bz + start, count), route.lands],
            slot, (route.side, y + route.step, x),
        )

    def cols_of(brick, route):
        return remote(
            cols_out.at[pl.ds(route.sent, route.size)],
            cols_in.at[brick, pl.ds(route.base, route.size)],
            COLS + 2 * brick + route.half,
            (route.side, y + route.step, x + 1),
        )

    def ends_of(brick, route):
        return remote(
            ends_out,
            ends_in.at[brick, route.half],
            ENDS + 2 * brick + route.half,
            (route.side, y + route.step, x - 1),
        )

    def rows_out(route, part=0):
        there = route.there(y, ny)
        if route.side != mine:
            return [(there, rows_of(mine, route, part))]
        return [(there, rows_of(mine, route, None))] if route.half else []

    def cols_sent(same):
        return [
            (jnp.logical_and(r.there(y, ny), has_right), cols_of(mine, r))
            for r in routes
            if (r.side == mine) == same
        ]

    def ends_sent():
        return [(jnp.logical_and(r.there(y, ny), has_left), ends_of(mine, r)) for r in routes]

    def apply(pairs, act):
        for there, copy in pairs:

            @pl.when(there)
            def _():
                act(copy)

    def start(pairs):
        apply(pairs, lambda copy: copy.start())

    def heard(kind, there, count):
        @pl.when(there)
        def _():
            pl.semaphore_wait(ready.at[kind], count)

    mains, own_halo, halos = (
        (routes[2], routes[1], routes[3]) if mine == 0 else (routes[0], routes[3], routes[1])
    )
    next_ones = [1 + there.astype(jnp.int32) for there in (has_down, has_up)]

    def send_first():
        if mine == 0:
            start(rows_out(halos))
            start(rows_out(mains))
        else:
            start(rows_out(mains))
            start(rows_out(own_halo))

    def send_rest():
        if mine == 0:
            start(ends_sent())
            heard(BELOW, has_down, 1)
            start(rows_out(own_halo))
        else:
            start(ends_sent())
        heard(RIGHT, has_right, next_ones[mine])
        start(cols_sent(True))
        if mine == 1:
            heard(BELOW, has_down, 1)
            start(rows_out(halos))
        start(rows_out(halos, 1) + rows_out(mains, 1))
        heard(ACROSS, has_right, next_ones[1 - mine])
        start(cols_sent(False))
        start(rows_out(halos, 2) + rows_out(mains, 2))

    def receive(brick, parts, sides):
        pairs = []
        for route in routes:
            if route.side != mine:
                continue
            comes = route.comes(y, ny)
            if brick != mine:
                pairs += [(comes, rows_of(brick, route, part)) for part in parts]
            elif route.half:
                pairs += [(comes, rows_of(brick, route, None))]
            if sides:
                pairs += [
                    (jnp.logical_and(comes, has_left), cols_of(brick, route)),
                    (jnp.logical_and(comes, has_right), ends_of(brick, route)),
                ]
        apply(pairs, lambda copy: copy.wait_recv())

    def close():
        for part in range(PARTS):
            apply(rows_out(mains, part) + rows_out(halos, part), lambda copy: copy.wait_send())
        apply(rows_out(own_halo), lambda copy: copy.wait_send())
        apply(ends_sent() + cols_sent(True) + cols_sent(False), lambda copy: copy.wait_send())

    return send_first, send_rest, receive, close


def partners_of(dims, here, over):
    ny, nx = dims[:2]
    z, y, x = here
    steps = [(z, over, 0), (1 - z, 0, 0)]
    diagonal = z == 1 if over > 0 else z == 0
    yield jnp.logical_and(diagonal, inside_of(dims, y + over, x)), (1 - z, y + over, x)
    steps += [
        (side, step, over)
        for side, step in ((z, -1), (z, 0), (z, 1), (1 - z, 0), (1 - z, 2 * z - 1))
    ]
    for side, step, across in steps:
        yield inside_of(dims, y + step, x + across), (side, y + step, x + across)


def inside_of(dims, y, x):
    ny, nx = dims[:2]
    return jnp.logical_and(
        jnp.logical_and(y >= 0, y < ny), jnp.logical_and(x >= 0, x < nx)
    )


def answers_of(dims, here):
    z, y, x = here
    own = z == 0
    yield jnp.logical_and(own, y > 0), (z, y - 1, x), BELOW
    yield jnp.logical_and(own, y > 0), (1 - z, y - 1, x), BELOW
    for side, kind in ((z, RIGHT), (1 - z, ACROSS)):
        for step in (0, 2 * z - 1):
            yield inside_of(dims, y + step, x - 1), (side, y + step, x - 1), kind


def render(
    dims, light_in, palette_in, rate_in, shear_in, offset_in, order_in, p_ref, out_ref,
    light, palette, rate, shear, offset, order, tile_ref, m_ref, own_ref, cols_in, ends_in,
    cols_out, ends_out, h_ref, r_ref, dm, dh, back, sends, arrivals, ready, local_sems, table_sem,
):
    ny, nx, bz, rows = dims
    strip = rows // 2
    tall = HALO + strip + SUB
    depth = 2 * bz
    blocks = (HALO + strip) // SUB
    wide_lanes = HALO - SUB
    z, y, x = lax.axis_index("gz"), lax.axis_index("gy"), lax.axis_index("gx")
    routes = routes_of(dims)[0]

    tables = [
        pltpu.make_async_copy(source, target, table_sem)
        for source, target in (
            (light_in, light), (palette_in, palette), (rate_in, rate),
            (shear_in, shear), (offset_in, offset), (order_in, order),
        )
    ]
    barrier = pltpu.get_barrier_semaphore()

    def sided(act):
        for mine in range(2):

            @pl.when(z == mine)
            def _():
                act(mine)

    for there, who in partners_of(dims, (z, y, x), 1):

        @pl.when(there)
        def _():
            pl.semaphore_signal(barrier, inc=1, device_id=who, device_id_type=MESH)

    count = 0
    for there, _ in partners_of(dims, (z, y, x), -1):
        count = count + there.astype(jnp.int32)

    steps = [
        exchange(
            dims, mine, (z, y, x), p_ref, m_ref, cols_out, cols_in, ends_out, ends_in,
            sends, arrivals, ready,
        )
        for mine in range(2)
    ]

    def local_slab(mine):
        route = routes[2 * mine]
        return pltpu.make_async_copy(
            p_ref.at[:, route.rows], m_ref.at[pl.ds(1 + mine * bz, bz), route.lands],
            local_sems.at[1],
        )

    local_tile = pltpu.make_async_copy(p_ref, tile_ref, local_sems.at[0])
    local_tile.start()
    sided(lambda mine: local_slab(mine).start())
    for copy in tables:
        copy.start()

    @pl.when(count > 0)
    def _():
        pl.semaphore_wait(barrier, count)

    for there, who, kind in answers_of(dims, (z, y, x)):

        @pl.when(there)
        def _():
            pl.semaphore_signal(ready.at[kind], inc=1, device_id=who, device_id_type=MESH)


    sided(lambda mine: steps[mine][0]())

    empty = jnp.zeros((tall, LANES), jnp.float32)
    for ref in (m_ref, h_ref):
        ref[0] = empty
        ref[depth + 1] = empty

    def blank(mine):
        route = routes[2 * mine + 1]

        @pl.when(jnp.logical_not(route.comes(y, ny)))
        def _():
            m_ref[:, route.slab] = jnp.zeros((depth + 2, len(route.tiles) * SUB, LANES), jnp.float32)
            cols_in[:, route.base : route.base + route.size] = jnp.zeros(
                (2, route.size, LANES), jnp.float32
            )
            ends_in[:, 1] = jnp.zeros((2, SUB, LANES), jnp.float32)

    sided(blank)

    @pl.when(x == 0)
    def _():
        cols_in[...] = jnp.zeros(cols_in.shape, jnp.float32)

    @pl.when(x == nx - 1)
    def _():
        ends_in[...] = jnp.zeros(ends_in.shape, jnp.float32)

    lane = lax.broadcasted_iota(jnp.int32, (SUB, LANES), 1)
    last = lane == LANES - 1
    first = lane == 0
    groups = routes[0].groups
    tiles = rows // SUB

    def cell(j, t):
        return tile_ref[j, t * SUB : (t + 1) * SUB]

    def put(t_or_fold, is_wide, value):
        for route in routes:
            if t_or_fold in (route.tiles if is_wide else route.folds):
                at = route.sent + (route.wide if is_wide else route.narrow)(t_or_fold)
                cols_out[at : at + SUB] = value

    def merged(pieces):
        while len(pieces) > 1:
            pieces = [
                (a[0], jnp.where(lane >= b[0], b[1], a[1]))
                for a, b in zip(pieces[::2], pieces[1::2])
            ] + (pieces[-1:] if len(pieces) % 2 else [])
        return pieces[0][1]

    def turned(value, by):
        return pltpu.roll(value, by % LANES, 1) if by % LANES else value

    local_tile.wait()
    for t in range(tiles):
        put(
            t, True,
            merged(
                [(wide_lanes * j, turned(cell(j, t), wide_lanes * (j + 1))) for j in range(bz)]
            ),
        )
    for fold in range(tiles // groups):
        put(
            fold, False,
            merged(
                [
                    (
                        SUB * (bz * g + j),
                        turned(cell(j, fold * groups + g), SUB * (bz * g + j) + HALO),
                    )
                    for g in range(groups)
                    for j in range(bz)
                ]
            ),
        )
    ends_out[...] = merged(
        [(t * bz + j, turned(cell(j, t), t * bz + j)) for t in range(tiles) for j in range(bz)]
    )

    def unpack(mine, brick):
        for route in routes[2 * mine : 2 * mine + 2]:
            for t in route.tiles:
                row = (route.first + t - route.tiles[0]) * SUB
                at = route.base + route.wide(t)
                wide = cols_in[brick, at : at + SUB]
                at = route.base + route.narrow(t // groups)
                narrow = cols_in[brick, at : at + SUB]
                for j in range(bz):
                    h_ref[1 + brick * bz + j, row : row + SUB] = jnp.where(
                        lane >= LANES - wide_lanes,
                        turned(wide, -wide_lanes * (j + 1)),
                        turned(narrow, -SUB * (bz * (t % groups) + j) - HALO),
                    )
                r_ref[brick, row : row + SUB] = turned(
                    ends_in[brick, route.half], LANES - 1 - t * bz
                )

    def opening(mine):
        _, send_rest, receive, _ = steps[mine]
        send_rest()
        local_slab(mine).wait()
        receive(mine, (), True)
        own_ref[...] = m_ref[1 + mine * bz : 1 + (mine + 1) * bz]
        unpack(mine, mine)

    def middle(mine):
        receive = steps[mine][2]
        receive(1 - mine, (0,), True)
        unpack(mine, 1 - mine)

    def ending(mine, part):
        receive = steps[mine][2]
        receive(1 - mine, (part,), False)

    sided(opening)
    for copy in tables:
        copy.wait()

    towards = []
    for w in range(VIEWS):
        a, b, c = light[w, 0], light[w, 1], light[w, 2]
        inverse = lax.rsqrt(jnp.full((SUB, LANES), a * a + b * b + c * c + 1.0, jnp.float32))
        towards.append((a * inverse, b * inverse, c * inverse))

    def slopes(k, carry):
        for i in range(blocks):
            top = i * SUB
            here = m_ref[k + 1, top + 1 : top + 1 + SUB]
            side = h_ref[k + 1, top + 1 : top + 1 + SUB]
            beyond = pltpu.roll(
                r_ref[k // bz, top + 1 : top + 1 + SUB], (LANES - k % bz) % LANES, 1
            )
            here_r, here_l = pltpu.roll(here, LANES - 1, 1), pltpu.roll(here, 1, 1)
            side_r, side_l = pltpu.roll(side, LANES - 1, 1), pltpu.roll(side, 1, 1)
            for ref, cols, dots in (
                (m_ref, jnp.where(last, beyond, here_r) - jnp.where(first, side_l, here_l), dm),
                (h_ref, jnp.where(last, here_r, side_r) - side_l, dh),
            ):
                deep = ref[k + 2, top + 1 : top + 1 + SUB] - ref[k, top + 1 : top + 1 + SUB]
                down = ref[k + 1, top + 2 : top + 2 + SUB] - ref[k + 1, top : top + SUB]
                half = lax.rsqrt(deep * deep + down * down + cols * cols + 4.0)
                deep, down, cols = deep * half, down * half, cols * half
                for w in range(VIEWS):
                    a, b, c = towards[w]
                    dots[w, k, top : top + SUB] = deep * a + down * b + cols * c
        return carry

    tile = 32
    per_view = strip // tile
    base_row = y * rows + z * strip
    base_col = x * LANES
    lanes = lax.broadcasted_iota(jnp.int32, (tile, LANES), 1)
    rows_at = lax.broadcasted_iota(jnp.int32, (tile, LANES), 0)
    bias = [0.5 * palette[0, c] for c in range(3)]
    gain = [0.5 * palette[1, c] for c in range(3)]

    def march(w, top, brick, cells, start, colors, through):
        ambient = jnp.zeros((tile, LANES), jnp.float32)
        rate2 = rate[w] * (-math.log2(math.e))
        off_r, off_c = offset[brick, 0, w], offset[brick, 1, w]
        inside = jnp.logical_and(rows_at >= off_r - base_row - top, lanes >= off_c - base_col)
        fall = jnp.where(inside, rate2, 0.0)
        for j in range(bz):
            k = brick * bz + j
            sr = off_r + shear[w, 0, k]
            sc = off_c + shear[w, 1, k]
            at = HALO + top - sr
            wrap = lanes >= LANES - sc
            value = jnp.where(wrap, h_ref[k + 1, pl.ds(at, tile)], cells[start + j, pl.ds(at, tile)])
            dot = jnp.where(wrap, dh[w, k, pl.ds(at - 1, tile)], dm[w, k, pl.ds(at - 1, tile)])
            value = pltpu.roll(value, sc, 1)
            dot = pltpu.roll(dot, sc, 1)
            kept = jnp.exp2(fall * (1.0 + jnp.tanh(value)))
            weight = (0.125 + 0.375 * dot * dot) * ((1.0 - kept) * through)
            through = through * kept
            ambient = ambient + weight
            colors = [
                colors[c] + weight * jnp.tanh(bias[c] + gain[c] * value) for c in range(3)
            ]
        return [color + ambient for color in colors], through

    def views(act):
        def one(step, carry):
            act(step // per_view, (step % per_view) * tile)
            return carry

        lax.fori_loop(0, VIEWS * per_view, one, 0, unroll=VIEWS * per_view)

    def own_layer(w, top):
        at = pl.ds(top, tile)
        zero = jnp.zeros((tile, LANES), jnp.float32)
        colors, through = march(w, top, z, own_ref, 0, [zero] * 3, zero + 1.0)
        ahead = order[0, w] == z
        for c in range(3):
            out_ref[w, c, at] = jnp.where(ahead, colors[c], 0.0)
            back[w, c, at] = jnp.where(ahead, 0.0, colors[c])
        out_ref[w, 3, at] = jnp.where(ahead, through, 1.0)
        back[w, 3, at] = jnp.where(ahead, 1.0, through)

    def other_layer(w, top):
        at = pl.ds(top, tile)
        colors, through = march(
            w, top, 1 - z, m_ref, 1 + (1 - z) * bz, [out_ref[w, c, at] for c in range(3)],
            out_ref[w, 3, at],
        )
        for c in range(3):
            out_ref[w, c, at] = colors[c] + through * back[w, c, at]
        out_ref[w, 3, at] = 1.0 - through * back[w, 3, at]

    def each(start, stop):
        lax.fori_loop(start, stop, slopes, 0)

    each(z * (bz + 1), z * (bz + 1) + bz - 1)
    sided(middle)
    for k in range(2):
        slopes(bz - 1 + k, 0)
    views(own_layer)
    sided(lambda mine: ending(mine, 1))
    each(bz + 1 - 3 * z, bz + 2 - 3 * z)
    sided(lambda mine: ending(mine, 2))
    for k in range(2):
        slopes((1 - z) * (depth - 2) + k, 0)
    views(other_layer)
    sided(lambda mine: steps[mine][3]())


def two_bricks(mesh, pressure, light, palette, rate, shear, offset, order):
    bz, rows, cols = pressure.shape
    dims = (mesh.shape["gy"], mesh.shape["gx"], bz, rows)
    strip = rows // 2
    tall = HALO + strip + SUB
    depth = 2 * bz
    vmem = pl.BlockSpec(memory_space=pltpu.VMEM)
    hbm = pl.BlockSpec(memory_space=pltpu.HBM)
    f32 = jnp.float32
    _, sent, got = routes_of(dims)
    tables = (
        light,
        palette.T,
        rate,
        jnp.transpose(shear, (0, 2, 1)),
        jnp.transpose(offset, (1, 2, 0)),
        order.T,
    )
    image = pl.pallas_call(
        functools.partial(render, dims),
        out_shape=jax.ShapeDtypeStruct((VIEWS, 4, strip, LANES), f32),
        in_specs=[hbm] * 7,
        out_specs=vmem,
        scratch_shapes=[
            *[pltpu.SMEM(table.shape, table.dtype) for table in tables],
            pltpu.VMEM((bz, rows, LANES), f32),
            pltpu.VMEM((depth + 2, tall, LANES), f32),
            pltpu.VMEM((bz, tall, LANES), f32),
            pltpu.VMEM((2, got, LANES), f32),
            pltpu.VMEM((2, 2, SUB, LANES), f32),
            pltpu.VMEM((sent, LANES), f32),
            pltpu.VMEM((SUB, LANES), f32),
            pltpu.VMEM((depth + 2, tall, LANES), f32),
            pltpu.VMEM((2, tall, LANES), f32),
            pltpu.VMEM((VIEWS, depth, HALO + strip, LANES), f32),
            pltpu.VMEM((VIEWS, depth, HALO + strip, LANES), f32),
            pltpu.VMEM((VIEWS, 4, strip, LANES), f32),
            pltpu.SemaphoreType.DMA,
            pltpu.SemaphoreType.DMA((SLOTS,)),
            pltpu.SemaphoreType.REGULAR((3,)),
            pltpu.SemaphoreType.DMA((2,)),
            pltpu.SemaphoreType.DMA,
        ],
        compiler_params=pltpu.CompilerParams(collective_id=0, has_side_effects=True, vmem_limit_bytes=12 << 20),
        name="render",
    )(
        *[pltpu.with_memory_space_constraint(t, pltpu.HBM) for t in (*tables, pressure)]
    )
    return image[:, :, None]


def fits(mesh, shape):
    bz, rows, cols = shape
    return (
        mesh.shape["gz"] == 2
        and cols == LANES
        and rows % 64 == 0
        and 2 * HALO <= rows <= LANES
        and bz * (HALO - SUB) == LANES
        and bz * (rows // SUB) <= LANES
    )


def on_device(mesh, pressure, *rest):
    if fits(mesh, pressure.shape):
        return two_bricks(mesh, pressure, *rest)
    return many_bricks(pressure, *rest)


def solution(mesh):
    return jax.shard_map(
        functools.partial(on_device, mesh),
        mesh=mesh,
        in_specs=(P("gz", "gy", "gx"), P(), P(), P(), P(), P(), P()),
        out_specs=P(None, None, "gz", "gy", "gx"),
        check_vma=False,
    )
```

```python
import functools
import math

import jax
import jax.numpy as jnp
from jax import lax
from jax.experimental import pallas as pl
from jax.experimental.pallas import tpu as pltpu
from jax.sharding import PartitionSpec as P

VIEWS = 4
SHEAR = 8
REACH = 32
HALO = SHEAR + REACH
SUB = 8
LANES = 128
MESH = pl.DeviceIdType.MESH


def padded(cells, sides, width):
    for axis, dim in sides:
        count = lax.axis_size(axis)
        ends = count - 1
        head = lax.slice_in_dim(cells, 0, width, axis=dim)
        tail = lax.slice_in_dim(cells, cells.shape[dim] - width, cells.shape[dim], axis=dim)
        cells = jnp.concatenate(
            [
                lax.ppermute(tail, axis, [(i, (i + 1) % count) for i in range(ends)]),
                cells,
                lax.ppermute(head, axis, [((i + 1) % count, i) for i in range(ends)]),
            ],
            axis=dim,
        )
    return cells


def shifted(value, axis, steps):
    count = lax.axis_size(axis)
    first, last = (max(0, -steps), min(count, count - steps))
    return lax.ppermute(value, axis, [(source, source + steps) for source in range(first, last)])


def surface_terms(slab):
    inner = slab[1:-1, 1:-1, 1:-1]
    grad_depth = 0.5 * (slab[2:, 1:-1, 1:-1] - slab[:-2, 1:-1, 1:-1])
    grad_rows = 0.5 * (slab[1:-1, 2:, 1:-1] - slab[1:-1, :-2, 1:-1])
    grad_cols = 0.5 * (slab[1:-1, 1:-1, 2:] - slab[1:-1, 1:-1, :-2])
    factor = lax.rsqrt(
        grad_depth * grad_depth + grad_rows * grad_rows + grad_cols * grad_cols + 1.0
    )
    return (inner, (grad_depth * factor, grad_rows * factor, grad_cols * factor))


def render_layers(inner, normals, shifts, light, palette, rate, rows, cols):
    lengths = jnp.sqrt(jnp.sum(light * light, axis=1, keepdims=True) + 1.0)
    towards = light / lengths
    offsets = palette[:, 0][:, None, None]
    slopes = palette[:, 1][:, None, None]
    layers = []
    for view in range(light.shape[0]):

        def advance(carry, items):
            color, depth = carry
            value_slab, normal_depth, normal_rows, normal_cols, moved = items
            start = (SHEAR - moved[0], SHEAR - moved[1])
            value = lax.dynamic_slice(value_slab, start, (rows, cols))
            dot = (
                lax.dynamic_slice(normal_depth, start, (rows, cols)) * towards[view, 0]
                + lax.dynamic_slice(normal_rows, start, (rows, cols)) * towards[view, 1]
                + lax.dynamic_slice(normal_cols, start, (rows, cols)) * towards[view, 2]
            )
            shade = 0.25 + 0.75 * dot * dot
            density = rate[view] * (1.0 + jnp.tanh(value))
            alpha = 1.0 - jnp.exp(-density)
            weight = alpha * jnp.exp(-depth)
            hues = jax.nn.sigmoid(offsets + slopes * value[None]) * shade[None]
            return ((color + hues * weight[None], depth + density), None)

        start_carry = (
            jnp.zeros((3, rows, cols), jnp.float32),
            jnp.zeros((rows, cols), jnp.float32),
        )
        (color, depth), _ = lax.scan(
            advance, start_carry, (inner, normals[0], normals[1], normals[2], shifts[view])
        )
        layers.append(jnp.concatenate([color, depth[None]], axis=0))
    return jnp.stack(layers)


def precedence(order):
    bricks = order.shape[1]
    onehot = (order[:, :, None] == jnp.arange(bricks, dtype=jnp.int32)[None, None, :]).astype(
        jnp.float32
    )
    ranks = jnp.sum(onehot * jnp.arange(bricks, dtype=jnp.float32)[None, :, None], axis=1)
    return (ranks[:, None, :] < ranks[:, :, None]).astype(jnp.float32)


def many_bricks(pressure, light, palette, rate, shear, offset, order):
    depth_cells, rows, cols = pressure.shape
    brick = lax.axis_index("gz")
    zero = jnp.zeros((), jnp.int32)
    widened = padded(pressure, (("gy", 1), ("gx", 2)), SHEAR + 1)
    slab = padded(widened, (("gz", 0),), 1)
    inner, normals = surface_terms(slab)
    shifts = lax.dynamic_slice(shear, (zero, brick * depth_cells, zero), (VIEWS, depth_cells, 2))
    layers = render_layers(inner, normals, shifts, light, palette, rate, rows, cols)
    moved = lax.dynamic_index_in_dim(offset, brick, 1, keepdims=False)
    blank = jnp.zeros((4, rows + REACH, cols + REACH), jnp.float32)
    canvas = jnp.stack(
        [
            lax.dynamic_update_slice(blank, layers[view], (zero, moved[view, 0], moved[view, 1]))
            for view in range(VIEWS)
        ]
    )
    own_tile = canvas[:, :, :rows, :cols]
    from_above = shifted(canvas[:, :, rows:, :cols], "gy", 1)
    from_left = shifted(canvas[:, :, :rows, cols:], "gx", 1)
    from_diagonal = shifted(canvas[:, :, rows:, cols:], ("gy", "gx"), lax.axis_size("gx") + 1)
    from_diagonal = from_diagonal * (lax.axis_index("gx") > 0).astype(jnp.float32)
    own_tile = own_tile.at[:, :, :REACH, :].add(from_above)
    own_tile = own_tile.at[:, :, :, :REACH].add(from_left)
    own_tile = own_tile.at[:, :, :REACH, :REACH].add(from_diagonal)
    ranking = precedence(order)
    pieces = lax.all_to_all(own_tile[None], "gz", split_axis=3, concat_axis=0, tiled=True)
    depths = pieces[:, :, 3]
    cover = jnp.einsum("vbc,cvyx->bvyx", ranking, depths, precision=lax.Precision.HIGHEST)
    colors = jnp.sum(pieces[:, :, :3] * jnp.exp(-cover)[:, :, None], axis=0)
    opacity = 1.0 - jnp.exp(-jnp.sum(depths, axis=0))
    image = jnp.concatenate([colors, opacity[:, None]], axis=1)
    return image[:, :, None]


class Route:
    def __init__(self, dims, side, step, start, count, slab, half):
        bz = dims[2]
        self.side, self.step, self.half = side, step, half
        self.slab = pl.ds(slab, count)
        needed = count - SUB + 1 if start == 0 else count
        self.rows, self.lands = pl.ds(start, needed), pl.ds(slab, needed)
        self.groups = LANES // (SUB * bz)
        self.tiles = range(start // SUB, (start + count) // SUB)
        self.first = slab // SUB
        self.folds = range(
            self.tiles[0] // self.groups, self.tiles[-1] // self.groups + 1
        )
        self.size = (len(self.tiles) + len(self.folds)) * SUB
        self.base = self.sent = 0

    def there(self, y, ny):
        return y + self.step >= 0 if self.step < 0 else y + self.step < ny

    def comes(self, y, ny):
        return y - self.step < ny if self.step < 0 else y - self.step >= 0

    def wide(self, tile):
        return (tile - self.tiles[0]) * SUB

    def narrow(self, fold):
        return (len(self.tiles) + fold - self.folds[0]) * SUB


def routes_of(dims):
    rows = dims[3]
    strip = rows // 2
    routes = [
        Route(dims, 0, 0, 0, strip + SUB, HALO, 0),
        Route(dims, 0, 1, rows - HALO, HALO, 0, 1),
        Route(dims, 1, 0, strip - HALO, HALO + strip, 0, 0),
        Route(dims, 1, -1, 0, SUB, HALO + strip, 1),
    ]
    sent = 0
    for route in routes:
        route.sent = sent
        sent += route.size
    routes[1].base, routes[3].base = routes[0].size, routes[2].size
    return routes, sent, max(routes[0].size + routes[1].size, routes[2].size + routes[3].size)


MAIN, EDGE, BESIDE, COLS, ENDS, SLOTS = 0, 3, 6, 7, 11, 15
PARTS = 3
BELOW, RIGHT, ACROSS = range(3)


def exchange(
    dims, mine, here, p_ref, m_ref, cols_out, cols_in, ends_out, ends_in, sends, arrivals, ready
):
    ny, nx, bz, rows = dims
    z, y, x = here
    has_left, has_right = x > 0, x < nx - 1
    has_up, has_down = y > 0, y < ny - 1
    routes = routes_of(dims)[0]

    def remote(src, dst, arrival, who):
        return pltpu.make_async_remote_copy(
            src_ref=src,
            dst_ref=dst,
            send_sem=sends,
            recv_sem=arrivals.at[arrival],
            device_id=who,
            device_id_type=MESH,
        )

    def rows_of(brick, route, part):
        first = bz - PARTS + 1
        start = first + part - 1 if part else 0
        count = bz if part is None else 1 if part else first
        if part is not None and brick == 0:
            start = bz - start - count
        slot = BESIDE if part is None else (EDGE if route.half else MAIN) + part
        return remote(
            p_ref.at[pl.ds(start, count), route.rows],
            m_ref.at[pl.ds(1 + brick * bz + start, count), route.lands],
            slot, (route.side, y + route.step, x),
        )

    def cols_of(brick, route):
        return remote(
            cols_out.at[pl.ds(route.sent, route.size)],
            cols_in.at[brick, pl.ds(route.base, route.size)],
            COLS + 2 * brick + route.half,
            (route.side, y + route.step, x + 1),
        )

    def ends_of(brick, route):
        return remote(
            ends_out,
            ends_in.at[brick, route.half],
            ENDS + 2 * brick + route.half,
            (route.side, y + route.step, x - 1),
        )

    def rows_out(route, part=0):
        there = route.there(y, ny)
        if route.side != mine:
            return [(there, rows_of(mine, route, part))]
        return [(there, rows_of(mine, route, None))] if route.half else []

    def cols_sent(same):
        return [
            (jnp.logical_and(r.there(y, ny), has_right), cols_of(mine, r))
            for r in routes
            if (r.side == mine) == same
        ]

    def ends_sent():
        return [(jnp.logical_and(r.there(y, ny), has_left), ends_of(mine, r)) for r in routes]

    def apply(pairs, act):
        for there, copy in pairs:

            @pl.when(there)
            def _():
                act(copy)

    def start(pairs):
        apply(pairs, lambda copy: copy.start())

    def heard(kind, there, count):
        @pl.when(there)
        def _():
            pl.semaphore_wait(ready.at[kind], count)

    mains, own_halo, halos = (
        (routes[2], routes[1], routes[3]) if mine == 0 else (routes[0], routes[3], routes[1])
    )
    next_ones = [1 + there.astype(jnp.int32) for there in (has_down, has_up)]

    def send_first():
        if mine == 0:
            start(rows_out(halos))
            start(rows_out(mains))
        else:
            start(rows_out(mains))
            start(rows_out(own_halo))

    def send_rest():
        if mine == 0:
            start(ends_sent())
            heard(BELOW, has_down, 1)
            start(rows_out(own_halo))
        else:
            start(ends_sent())
        heard(RIGHT, has_right, next_ones[mine])
        start(cols_sent(True))
        if mine == 1:
            heard(BELOW, has_down, 1)
            start(rows_out(halos))
        start(rows_out(halos, 1) + rows_out(mains, 1))
        heard(ACROSS, has_right, next_ones[1 - mine])
        start(cols_sent(False))
        start(rows_out(halos, 2) + rows_out(mains, 2))

    def receive(brick, parts, sides):
        pairs = []
        for route in routes:
            if route.side != mine:
                continue
            comes = route.comes(y, ny)
            if brick != mine:
                pairs += [(comes, rows_of(brick, route, part)) for part in parts]
            elif route.half:
                pairs += [(comes, rows_of(brick, route, None))]
            if sides:
                pairs += [
                    (jnp.logical_and(comes, has_left), cols_of(brick, route)),
                    (jnp.logical_and(comes, has_right), ends_of(brick, route)),
                ]
        apply(pairs, lambda copy: copy.wait_recv())

    def close():
        for part in range(PARTS):
            apply(rows_out(mains, part) + rows_out(halos, part), lambda copy: copy.wait_send())
        apply(rows_out(own_halo), lambda copy: copy.wait_send())
        apply(ends_sent() + cols_sent(True) + cols_sent(False), lambda copy: copy.wait_send())

    return send_first, send_rest, receive, close


def partners_of(dims, here, over):
    ny, nx = dims[:2]
    z, y, x = here
    steps = [(z, over, 0), (1 - z, 0, 0)]
    diagonal = z == 1 if over > 0 else z == 0
    yield jnp.logical_and(diagonal, inside_of(dims, y + over, x)), (1 - z, y + over, x)
    steps += [
        (side, step, over)
        for side, step in ((z, -1), (z, 0), (z, 1), (1 - z, 0), (1 - z, 2 * z - 1))
    ]
    for side, step, across in steps:
        yield inside_of(dims, y + step, x + across), (side, y + step, x + across)


def inside_of(dims, y, x):
    ny, nx = dims[:2]
    return jnp.logical_and(
        jnp.logical_and(y >= 0, y < ny), jnp.logical_and(x >= 0, x < nx)
    )


def answers_of(dims, here):
    z, y, x = here
    own = z == 0
    yield jnp.logical_and(own, y > 0), (z, y - 1, x), BELOW
    yield jnp.logical_and(own, y > 0), (1 - z, y - 1, x), BELOW
    for side, kind in ((z, RIGHT), (1 - z, ACROSS)):
        for step in (0, 2 * z - 1):
            yield inside_of(dims, y + step, x - 1), (side, y + step, x - 1), kind


def render(
    dims, light_in, palette_in, rate_in, shear_in, offset_in, order_in, p_ref, out_ref,
    light, palette, rate, shear, offset, order, tile_ref, m_ref, own_ref, near_ref, cols_in, ends_in,
    cols_out, ends_out, h_ref, r_ref, dm, dh, back, sends, arrivals, ready, local_sems, table_sem,
):
    ny, nx, bz, rows = dims
    strip = rows // 2
    tall = HALO + strip + SUB
    depth = 2 * bz
    blocks = (HALO + strip) // SUB
    wide_lanes = HALO - SUB
    z, y, x = lax.axis_index("gz"), lax.axis_index("gy"), lax.axis_index("gx")
    routes = routes_of(dims)[0]

    tables = [
        pltpu.make_async_copy(source, target, table_sem)
        for source, target in (
            (light_in, light), (palette_in, palette), (rate_in, rate),
            (shear_in, shear), (offset_in, offset), (order_in, order),
        )
    ]
    barrier = pltpu.get_barrier_semaphore()

    def sided(act):
        for mine in range(2):

            @pl.when(z == mine)
            def _():
                act(mine)

    for there, who in partners_of(dims, (z, y, x), 1):

        @pl.when(there)
        def _():
            pl.semaphore_signal(barrier, inc=1, device_id=who, device_id_type=MESH)

    count = 0
    for there, _ in partners_of(dims, (z, y, x), -1):
        count = count + there.astype(jnp.int32)

    steps = [
        exchange(
            dims, mine, (z, y, x), p_ref, m_ref, cols_out, cols_in, ends_out, ends_in,
            sends, arrivals, ready,
        )
        for mine in range(2)
    ]

    def local_slab(mine):
        route = routes[2 * mine]
        return pltpu.make_async_copy(
            p_ref.at[:, route.rows], m_ref.at[pl.ds(1 + mine * bz, bz), route.lands],
            local_sems.at[1],
        )

    local_tile = pltpu.make_async_copy(p_ref, tile_ref, local_sems.at[0])
    local_tile.start()
    sided(lambda mine: local_slab(mine).start())
    for copy in tables:
        copy.start()

    @pl.when(count > 0)
    def _():
        pl.semaphore_wait(barrier, count)

    for there, who, kind in answers_of(dims, (z, y, x)):

        @pl.when(there)
        def _():
            pl.semaphore_signal(ready.at[kind], inc=1, device_id=who, device_id_type=MESH)


    sided(lambda mine: steps[mine][0]())

    empty = jnp.zeros((tall, LANES), jnp.float32)
    for ref in (m_ref, h_ref):
        ref[0] = empty
        ref[depth + 1] = empty

    def blank(mine):
        route = routes[2 * mine + 1]

        @pl.when(jnp.logical_not(route.comes(y, ny)))
        def _():
            m_ref[:, route.slab] = jnp.zeros((depth + 2, len(route.tiles) * SUB, LANES), jnp.float32)
            cols_in[:, route.base : route.base + route.size] = jnp.zeros(
                (2, route.size, LANES), jnp.float32
            )
            ends_in[:, 1] = jnp.zeros((2, SUB, LANES), jnp.float32)

    sided(blank)

    @pl.when(x == 0)
    def _():
        cols_in[...] = jnp.zeros(cols_in.shape, jnp.float32)

    @pl.when(x == nx - 1)
    def _():
        ends_in[...] = jnp.zeros(ends_in.shape, jnp.float32)

    lane = lax.broadcasted_iota(jnp.int32, (SUB, LANES), 1)
    last = lane == LANES - 1
    first = lane == 0
    groups = routes[0].groups
    tiles = rows // SUB

    def cell(j, t):
        return tile_ref[j, t * SUB : (t + 1) * SUB]

    def put(t_or_fold, is_wide, value):
        for route in routes:
            if t_or_fold in (route.tiles if is_wide else route.folds):
                at = route.sent + (route.wide if is_wide else route.narrow)(t_or_fold)
                cols_out[at : at + SUB] = value

    def merged(pieces):
        while len(pieces) > 1:
            pieces = [
                (a[0], jnp.where(lane >= b[0], b[1], a[1]))
                for a, b in zip(pieces[::2], pieces[1::2])
            ] + (pieces[-1:] if len(pieces) % 2 else [])
        return pieces[0][1]

    def turned(value, by):
        return pltpu.roll(value, by % LANES, 1) if by % LANES else value

    local_tile.wait()
    for t in range(tiles):
        put(
            t, True,
            merged(
                [(wide_lanes * j, turned(cell(j, t), wide_lanes * (j + 1))) for j in range(bz)]
            ),
        )
    for fold in range(tiles // groups):
        put(
            fold, False,
            merged(
                [
                    (
                        SUB * (bz * g + j),
                        turned(cell(j, fold * groups + g), SUB * (bz * g + j) + HALO),
                    )
                    for g in range(groups)
                    for j in range(bz)
                ]
            ),
        )
    ends_out[...] = merged(
        [(t * bz + j, turned(cell(j, t), t * bz + j)) for t in range(tiles) for j in range(bz)]
    )

    def unpack(mine, brick):
        for route in routes[2 * mine : 2 * mine + 2]:
            for t in route.tiles:
                row = (route.first + t - route.tiles[0]) * SUB
                at = route.base + route.wide(t)
                wide = cols_in[brick, at : at + SUB]
                at = route.base + route.narrow(t // groups)
                narrow = cols_in[brick, at : at + SUB]
                for j in range(bz):
                    h_ref[1 + brick * bz + j, row : row + SUB] = jnp.where(
                        lane >= LANES - wide_lanes,
                        turned(wide, -wide_lanes * (j + 1)),
                        turned(narrow, -SUB * (bz * (t % groups) + j) - HALO),
                    )
                r_ref[brick, row : row + SUB] = turned(
                    ends_in[brick, route.half], LANES - 1 - t * bz
                )

    def opening(mine):
        _, send_rest, receive, _ = steps[mine]
        send_rest()
        local_slab(mine).wait()
        receive(mine, (), True)
        own_ref[...] = m_ref[1 + mine * bz : 1 + (mine + 1) * bz]
        unpack(mine, mine)

    def middle(mine):
        receive = steps[mine][2]
        receive(1 - mine, (0,), True)
        near_ref[...] = m_ref[(bz if mine == 0 else 2) + 1 : (depth - 2 if mine == 0 else bz) + 1]
        unpack(mine, 1 - mine)

    def ending(mine, part):
        receive = steps[mine][2]
        receive(1 - mine, (part,), False)

    sided(opening)
    for copy in tables:
        copy.wait()

    towards = []
    for w in range(VIEWS):
        a, b, c = light[w, 0], light[w, 1], light[w, 2]
        inverse = lax.rsqrt(jnp.full((SUB, LANES), a * a + b * b + c * c + 1.0, jnp.float32))
        towards.append((a * inverse, b * inverse, c * inverse))

    def slopes(k, carry):
        for i in range(blocks):
            top = i * SUB
            here = m_ref[k + 1, top + 1 : top + 1 + SUB]
            side = h_ref[k + 1, top + 1 : top + 1 + SUB]
            beyond = pltpu.roll(
                r_ref[k // bz, top + 1 : top + 1 + SUB], (LANES - k % bz) % LANES, 1
            )
            here_r, here_l = pltpu.roll(here, LANES - 1, 1), pltpu.roll(here, 1, 1)
            side_r, side_l = pltpu.roll(side, LANES - 1, 1), pltpu.roll(side, 1, 1)
            for ref, cols, dots in (
                (m_ref, jnp.where(last, beyond, here_r) - jnp.where(first, side_l, here_l), dm),
                (h_ref, jnp.where(last, here_r, side_r) - side_l, dh),
            ):
                deep = ref[k + 2, top + 1 : top + 1 + SUB] - ref[k, top + 1 : top + 1 + SUB]
                down = ref[k + 1, top + 2 : top + 2 + SUB] - ref[k + 1, top : top + SUB]
                half = lax.rsqrt(deep * deep + down * down + cols * cols + 4.0)
                deep, down, cols = deep * half, down * half, cols * half
                for w in range(VIEWS):
                    a, b, c = towards[w]
                    dots[w, k, top : top + SUB] = deep * a + down * b + cols * c
        return carry

    tile = 32
    per_view = strip // tile
    base_row = y * rows + z * strip
    base_col = x * LANES
    lanes = lax.broadcasted_iota(jnp.int32, (tile, LANES), 1)
    rows_at = lax.broadcasted_iota(jnp.int32, (tile, LANES), 0)
    bias = [0.5 * palette[0, c] for c in range(3)]
    gain = [0.5 * palette[1, c] for c in range(3)]

    def march(w, top, brick, first_k, count, cells, start, colors, through):
        ambient = jnp.zeros((tile, LANES), jnp.float32)
        rate2 = rate[w] * (-math.log2(math.e))
        off_r, off_c = offset[brick, 0, w], offset[brick, 1, w]
        inside = jnp.logical_and(rows_at >= off_r - base_row - top, lanes >= off_c - base_col)
        fall = jnp.where(inside, rate2, 0.0)
        for j in range(count):
            k = first_k + j
            sr = off_r + shear[w, 0, k]
            sc = off_c + shear[w, 1, k]
            at = HALO + top - sr
            wrap = lanes >= LANES - sc
            value = jnp.where(wrap, h_ref[k + 1, pl.ds(at, tile)], cells[start + j, pl.ds(at, tile)])
            dot = jnp.where(wrap, dh[w, k, pl.ds(at - 1, tile)], dm[w, k, pl.ds(at - 1, tile)])
            value = pltpu.roll(value, sc, 1)
            dot = pltpu.roll(dot, sc, 1)
            kept = jnp.exp2(fall * (1.0 + jnp.tanh(value)))
            weight = (0.125 + 0.375 * dot * dot) * ((1.0 - kept) * through)
            through = through * kept
            ambient = ambient + weight
            colors = [
                colors[c] + weight * jnp.tanh(bias[c] + gain[c] * value) for c in range(3)
            ]
        return [color + ambient for color in colors], through

    def views(act):
        def one(step, carry):
            act(step // per_view, (step % per_view) * tile)
            return carry

        lax.fori_loop(0, VIEWS * per_view, one, 0, unroll=VIEWS * per_view)

    zero = jnp.zeros((tile, LANES), jnp.float32)
    early = bz - 2
    near, far = bz - early * z, (depth - 2) * (1 - z)

    def own_layer(w, top):
        at = pl.ds(top, tile)
        colors, through = march(w, top, z, z * bz, bz, own_ref, 0, [zero] * 3, zero + 1.0)
        for c in range(3):
            back[w, c, at] = colors[c]
        back[w, 3, at] = through

    def near_layer(w, top):
        at = pl.ds(top, tile)
        colors, through = march(
            w, top, 1 - z, near, early, near_ref, 0, [zero] * 3, zero + 1.0
        )
        own_first, near_first = order[0, w] == z, z == 0
        own_through = back[w, 3, at]
        ahead = jnp.where(own_first, own_through, 1.0)
        after = jnp.where(near_first, 1.0, through)
        for c in range(3):
            own_color = back[w, c, at]
            out_ref[w, c, at] = jnp.where(own_first, own_color, 0.0) + jnp.where(
                near_first, ahead * colors[c], 0.0
            )
            back[w, c, at] = jnp.where(near_first, 0.0, colors[c]) + jnp.where(
                own_first, 0.0, after * own_color
            )
        out_ref[w, 3, at] = ahead * jnp.where(near_first, through, 1.0)
        back[w, 3, at] = after * jnp.where(own_first, 1.0, own_through)

    def far_layer(w, top):
        at = pl.ds(top, tile)
        colors, through = march(
            w, top, 1 - z, far, 2, m_ref, 1 + far, [out_ref[w, c, at] for c in range(3)],
            out_ref[w, 3, at],
        )
        for c in range(3):
            out_ref[w, c, at] = colors[c] + through * back[w, c, at]
        out_ref[w, 3, at] = 1.0 - through * back[w, 3, at]

    def each(start, stop):
        lax.fori_loop(start, stop, slopes, 0)

    each(z * (bz + 1), z * (bz + 1) + bz - 1)
    sided(middle)
    for k in range(2):
        slopes(bz - 1 + k, 0)
    views(own_layer)
    sided(lambda mine: ending(mine, 1))
    each(bz + 1 - 3 * z, bz + 2 - 3 * z)
    views(near_layer)
    sided(lambda mine: ending(mine, 2))
    for k in range(2):
        slopes((1 - z) * (depth - 2) + k, 0)
    views(far_layer)
    sided(lambda mine: steps[mine][3]())


def two_bricks(mesh, pressure, light, palette, rate, shear, offset, order):
    bz, rows, cols = pressure.shape
    dims = (mesh.shape["gy"], mesh.shape["gx"], bz, rows)
    strip = rows // 2
    tall = HALO + strip + SUB
    depth = 2 * bz
    vmem = pl.BlockSpec(memory_space=pltpu.VMEM)
    hbm = pl.BlockSpec(memory_space=pltpu.HBM)
    f32 = jnp.float32
    _, sent, got = routes_of(dims)
    tables = (
        light,
        palette.T,
        rate,
        jnp.transpose(shear, (0, 2, 1)),
        jnp.transpose(offset, (1, 2, 0)),
        order.T,
    )
    image = pl.pallas_call(
        functools.partial(render, dims),
        out_shape=jax.ShapeDtypeStruct((VIEWS, 4, strip, LANES), f32),
        in_specs=[hbm] * 7,
        out_specs=vmem,
        scratch_shapes=[
            *[pltpu.SMEM(table.shape, table.dtype) for table in tables],
            pltpu.VMEM((bz, rows, LANES), f32),
            pltpu.VMEM((depth + 2, tall, LANES), f32),
            pltpu.VMEM((bz, tall, LANES), f32),
            pltpu.VMEM((bz - 2, tall, LANES), f32),
            pltpu.VMEM((2, got, LANES), f32),
            pltpu.VMEM((2, 2, SUB, LANES), f32),
            pltpu.VMEM((sent, LANES), f32),
            pltpu.VMEM((SUB, LANES), f32),
            pltpu.VMEM((depth + 2, tall, LANES), f32),
            pltpu.VMEM((2, tall, LANES), f32),
            pltpu.VMEM((VIEWS, depth, HALO + strip, LANES), f32),
            pltpu.VMEM((VIEWS, depth, HALO + strip, LANES), f32),
            pltpu.VMEM((VIEWS, 4, strip, LANES), f32),
            pltpu.SemaphoreType.DMA,
            pltpu.SemaphoreType.DMA((SLOTS,)),
            pltpu.SemaphoreType.REGULAR((3,)),
            pltpu.SemaphoreType.DMA((2,)),
            pltpu.SemaphoreType.DMA,
        ],
        compiler_params=pltpu.CompilerParams(collective_id=0, has_side_effects=True, vmem_limit_bytes=12 << 20),
        name="render",
    )(
        *[pltpu.with_memory_space_constraint(t, pltpu.HBM) for t in (*tables, pressure)]
    )
    return image[:, :, None]


def fits(mesh, shape):
    bz, rows, cols = shape
    return (
        mesh.shape["gz"] == 2
        and cols == LANES
        and rows % 64 == 0
        and 2 * HALO <= rows <= LANES
        and bz * (HALO - SUB) == LANES
        and bz * (rows // SUB) <= LANES
    )


def on_device(mesh, pressure, *rest):
    if fits(mesh, pressure.shape):
        return two_bricks(mesh, pressure, *rest)
    return many_bricks(pressure, *rest)


def solution(mesh):
    return jax.shard_map(
        functools.partial(on_device, mesh),
        mesh=mesh,
        in_specs=(P("gz", "gy", "gx"), P(), P(), P(), P(), P(), P()),
        out_specs=P(None, None, "gz", "gy", "gx"),
        check_vma=False,
    )
```

```python
import functools
import math

import jax
import jax.numpy as jnp
from jax import lax
from jax.experimental import pallas as pl
from jax.experimental.pallas import tpu as pltpu
from jax.sharding import PartitionSpec as P

VIEWS = 4
SHEAR = 8
REACH = 32
HALO = SHEAR + REACH
SUB = 8
LANES = 128
MESH = pl.DeviceIdType.MESH


def padded(cells, sides, width):
    for axis, dim in sides:
        count = lax.axis_size(axis)
        ends = count - 1
        head = lax.slice_in_dim(cells, 0, width, axis=dim)
        tail = lax.slice_in_dim(cells, cells.shape[dim] - width, cells.shape[dim], axis=dim)
        cells = jnp.concatenate(
            [
                lax.ppermute(tail, axis, [(i, (i + 1) % count) for i in range(ends)]),
                cells,
                lax.ppermute(head, axis, [((i + 1) % count, i) for i in range(ends)]),
            ],
            axis=dim,
        )
    return cells


def shifted(value, axis, steps):
    count = lax.axis_size(axis)
    first, last = (max(0, -steps), min(count, count - steps))
    return lax.ppermute(value, axis, [(source, source + steps) for source in range(first, last)])


def surface_terms(slab):
    inner = slab[1:-1, 1:-1, 1:-1]
    grad_depth = 0.5 * (slab[2:, 1:-1, 1:-1] - slab[:-2, 1:-1, 1:-1])
    grad_rows = 0.5 * (slab[1:-1, 2:, 1:-1] - slab[1:-1, :-2, 1:-1])
    grad_cols = 0.5 * (slab[1:-1, 1:-1, 2:] - slab[1:-1, 1:-1, :-2])
    factor = lax.rsqrt(
        grad_depth * grad_depth + grad_rows * grad_rows + grad_cols * grad_cols + 1.0
    )
    return (inner, (grad_depth * factor, grad_rows * factor, grad_cols * factor))


def render_layers(inner, normals, shifts, light, palette, rate, rows, cols):
    lengths = jnp.sqrt(jnp.sum(light * light, axis=1, keepdims=True) + 1.0)
    towards = light / lengths
    offsets = palette[:, 0][:, None, None]
    slopes = palette[:, 1][:, None, None]
    layers = []
    for view in range(light.shape[0]):

        def advance(carry, items):
            color, depth = carry
            value_slab, normal_depth, normal_rows, normal_cols, moved = items
            start = (SHEAR - moved[0], SHEAR - moved[1])
            value = lax.dynamic_slice(value_slab, start, (rows, cols))
            dot = (
                lax.dynamic_slice(normal_depth, start, (rows, cols)) * towards[view, 0]
                + lax.dynamic_slice(normal_rows, start, (rows, cols)) * towards[view, 1]
                + lax.dynamic_slice(normal_cols, start, (rows, cols)) * towards[view, 2]
            )
            shade = 0.25 + 0.75 * dot * dot
            density = rate[view] * (1.0 + jnp.tanh(value))
            alpha = 1.0 - jnp.exp(-density)
            weight = alpha * jnp.exp(-depth)
            hues = jax.nn.sigmoid(offsets + slopes * value[None]) * shade[None]
            return ((color + hues * weight[None], depth + density), None)

        start_carry = (
            jnp.zeros((3, rows, cols), jnp.float32),
            jnp.zeros((rows, cols), jnp.float32),
        )
        (color, depth), _ = lax.scan(
            advance, start_carry, (inner, normals[0], normals[1], normals[2], shifts[view])
        )
        layers.append(jnp.concatenate([color, depth[None]], axis=0))
    return jnp.stack(layers)


def precedence(order):
    bricks = order.shape[1]
    onehot = (order[:, :, None] == jnp.arange(bricks, dtype=jnp.int32)[None, None, :]).astype(
        jnp.float32
    )
    ranks = jnp.sum(onehot * jnp.arange(bricks, dtype=jnp.float32)[None, :, None], axis=1)
    return (ranks[:, None, :] < ranks[:, :, None]).astype(jnp.float32)


def many_bricks(pressure, light, palette, rate, shear, offset, order):
    depth_cells, rows, cols = pressure.shape
    brick = lax.axis_index("gz")
    zero = jnp.zeros((), jnp.int32)
    widened = padded(pressure, (("gy", 1), ("gx", 2)), SHEAR + 1)
    slab = padded(widened, (("gz", 0),), 1)
    inner, normals = surface_terms(slab)
    shifts = lax.dynamic_slice(shear, (zero, brick * depth_cells, zero), (VIEWS, depth_cells, 2))
    layers = render_layers(inner, normals, shifts, light, palette, rate, rows, cols)
    moved = lax.dynamic_index_in_dim(offset, brick, 1, keepdims=False)
    blank = jnp.zeros((4, rows + REACH, cols + REACH), jnp.float32)
    canvas = jnp.stack(
        [
            lax.dynamic_update_slice(blank, layers[view], (zero, moved[view, 0], moved[view, 1]))
            for view in range(VIEWS)
        ]
    )
    own_tile = canvas[:, :, :rows, :cols]
    from_above = shifted(canvas[:, :, rows:, :cols], "gy", 1)
    from_left = shifted(canvas[:, :, :rows, cols:], "gx", 1)
    from_diagonal = shifted(canvas[:, :, rows:, cols:], ("gy", "gx"), lax.axis_size("gx") + 1)
    from_diagonal = from_diagonal * (lax.axis_index("gx") > 0).astype(jnp.float32)
    own_tile = own_tile.at[:, :, :REACH, :].add(from_above)
    own_tile = own_tile.at[:, :, :, :REACH].add(from_left)
    own_tile = own_tile.at[:, :, :REACH, :REACH].add(from_diagonal)
    ranking = precedence(order)
    pieces = lax.all_to_all(own_tile[None], "gz", split_axis=3, concat_axis=0, tiled=True)
    depths = pieces[:, :, 3]
    cover = jnp.einsum("vbc,cvyx->bvyx", ranking, depths, precision=lax.Precision.HIGHEST)
    colors = jnp.sum(pieces[:, :, :3] * jnp.exp(-cover)[:, :, None], axis=0)
    opacity = 1.0 - jnp.exp(-jnp.sum(depths, axis=0))
    image = jnp.concatenate([colors, opacity[:, None]], axis=1)
    return image[:, :, None]


class Route:
    def __init__(self, dims, side, step, start, count, slab, half):
        bz = dims[2]
        self.side, self.step, self.half = side, step, half
        self.slab = pl.ds(slab, count)
        needed = count - SUB + 1 if start == 0 else count
        self.rows, self.lands = pl.ds(start, needed), pl.ds(slab, needed)
        self.groups = LANES // (SUB * bz)
        self.tiles = range(start // SUB, (start + count) // SUB)
        self.first = slab // SUB
        self.folds = range(
            self.tiles[0] // self.groups, self.tiles[-1] // self.groups + 1
        )
        self.size = (len(self.tiles) + len(self.folds)) * SUB
        self.base = self.sent = 0

    def there(self, y, ny):
        return y + self.step >= 0 if self.step < 0 else y + self.step < ny

    def comes(self, y, ny):
        return y - self.step < ny if self.step < 0 else y - self.step >= 0

    def wide(self, tile):
        return (tile - self.tiles[0]) * SUB

    def narrow(self, fold):
        return (len(self.tiles) + fold - self.folds[0]) * SUB


def routes_of(dims):
    rows = dims[3]
    strip = rows // 2
    routes = [
        Route(dims, 0, 0, 0, strip + SUB, HALO, 0),
        Route(dims, 0, 1, rows - HALO, HALO, 0, 1),
        Route(dims, 1, 0, strip - HALO, HALO + strip, 0, 0),
        Route(dims, 1, -1, 0, SUB, HALO + strip, 1),
    ]
    sent = 0
    for route in routes:
        route.sent = sent
        sent += route.size
    routes[1].base, routes[3].base = routes[0].size, routes[2].size
    return routes, sent, max(routes[0].size + routes[1].size, routes[2].size + routes[3].size)


MAIN, EDGE, BESIDE, COLS, ENDS, SLOTS = 0, 3, 6, 7, 11, 15
PARTS = 3
BELOW, RIGHT, ACROSS = range(3)


def exchange(
    dims, mine, here, p_ref, m_ref, cols_out, cols_in, ends_out, ends_in, sends, arrivals, ready
):
    ny, nx, bz, rows = dims
    z, y, x = here
    has_left, has_right = x > 0, x < nx - 1
    has_up, has_down = y > 0, y < ny - 1
    routes = routes_of(dims)[0]

    def remote(src, dst, arrival, who):
        return pltpu.make_async_remote_copy(
            src_ref=src,
            dst_ref=dst,
            send_sem=sends,
            recv_sem=arrivals.at[arrival],
            device_id=who,
            device_id_type=MESH,
        )

    def rows_of(brick, route, part):
        first = bz - PARTS + 1
        start = first + part - 1 if part else 0
        count = bz if part is None else 1 if part else first
        if part is not None and brick == 0:
            start = bz - start - count
        slot = BESIDE if part is None else (EDGE if route.half else MAIN) + part
        return remote(
            p_ref.at[pl.ds(start, count), route.rows],
            m_ref.at[pl.ds(1 + brick * bz + start, count), route.lands],
            slot, (route.side, y + route.step, x),
        )

    def cols_of(brick, route):
        return remote(
            cols_out.at[pl.ds(route.sent, route.size)],
            cols_in.at[brick, pl.ds(route.base, route.size)],
            COLS + 2 * brick + route.half,
            (route.side, y + route.step, x + 1),
        )

    def ends_of(brick, route):
        return remote(
            ends_out,
            ends_in.at[brick, route.half],
            ENDS + 2 * brick + route.half,
            (route.side, y + route.step, x - 1),
        )

    def rows_out(route, part=0):
        there = route.there(y, ny)
        if route.side != mine:
            return [(there, rows_of(mine, route, part))]
        return [(there, rows_of(mine, route, None))] if route.half else []

    def cols_sent(same):
        return [
            (jnp.logical_and(r.there(y, ny), has_right), cols_of(mine, r))
            for r in routes
            if (r.side == mine) == same
        ]

    def ends_sent():
        return [(jnp.logical_and(r.there(y, ny), has_left), ends_of(mine, r)) for r in routes]

    def apply(pairs, act):
        for there, copy in pairs:

            @pl.when(there)
            def _():
                act(copy)

    def start(pairs):
        apply(pairs, lambda copy: copy.start())

    def heard(kind, there, count):
        @pl.when(there)
        def _():
            pl.semaphore_wait(ready.at[kind], count)

    mains, own_halo, halos = (
        (routes[2], routes[1], routes[3]) if mine == 0 else (routes[0], routes[3], routes[1])
    )
    next_ones = [1 + there.astype(jnp.int32) for there in (has_down, has_up)]

    def send_first():
        if mine == 0:
            start(rows_out(halos))
            start(rows_out(mains))
        else:
            start(rows_out(mains))
            start(rows_out(own_halo))

    def send_rest():
        if mine == 0:
            start(ends_sent())
            heard(BELOW, has_down, 1)
            start(rows_out(own_halo))
        else:
            start(ends_sent())
        heard(RIGHT, has_right, next_ones[mine])
        start(cols_sent(True))
        if mine == 1:
            heard(BELOW, has_down, 1)
            start(rows_out(halos))
        start(rows_out(halos, 1) + rows_out(mains, 1))
        heard(ACROSS, has_right, next_ones[1 - mine])
        start(cols_sent(False))
        start(rows_out(halos, 2) + rows_out(mains, 2))

    def receive(brick, parts, sides):
        pairs = []
        for route in routes:
            if route.side != mine:
                continue
            comes = route.comes(y, ny)
            if brick != mine:
                pairs += [(comes, rows_of(brick, route, part)) for part in parts]
            elif route.half:
                pairs += [(comes, rows_of(brick, route, None))]
            if sides:
                pairs += [
                    (jnp.logical_and(comes, has_left), cols_of(brick, route)),
                    (jnp.logical_and(comes, has_right), ends_of(brick, route)),
                ]
        apply(pairs, lambda copy: copy.wait_recv())

    def close():
        for part in range(PARTS):
            apply(rows_out(mains, part) + rows_out(halos, part), lambda copy: copy.wait_send())
        apply(rows_out(own_halo), lambda copy: copy.wait_send())
        apply(ends_sent() + cols_sent(True) + cols_sent(False), lambda copy: copy.wait_send())

    return send_first, send_rest, receive, close


def partners_of(dims, here, over):
    ny, nx = dims[:2]
    z, y, x = here
    steps = [(z, over, 0), (1 - z, 0, 0)]
    diagonal = z == 1 if over > 0 else z == 0
    yield jnp.logical_and(diagonal, inside_of(dims, y + over, x)), (1 - z, y + over, x)
    steps += [
        (side, step, over)
        for side, step in ((z, -1), (z, 0), (z, 1), (1 - z, 0), (1 - z, 2 * z - 1))
    ]
    for side, step, across in steps:
        yield inside_of(dims, y + step, x + across), (side, y + step, x + across)


def inside_of(dims, y, x):
    ny, nx = dims[:2]
    return jnp.logical_and(
        jnp.logical_and(y >= 0, y < ny), jnp.logical_and(x >= 0, x < nx)
    )


def answers_of(dims, here):
    z, y, x = here
    own = z == 0
    yield jnp.logical_and(own, y > 0), (z, y - 1, x), BELOW
    yield jnp.logical_and(own, y > 0), (1 - z, y - 1, x), BELOW
    for side, kind in ((z, RIGHT), (1 - z, ACROSS)):
        for step in (0, 2 * z - 1):
            yield inside_of(dims, y + step, x - 1), (side, y + step, x - 1), kind


def render(
    dims, light_in, palette_in, rate_in, shear_in, offset_in, order_in, p_ref, out_ref,
    light, palette, rate, shear, offset, order, tile_ref, m_ref, own_ref, near_ref, cols_in, ends_in,
    cols_out, ends_out, h_ref, r_ref, dm, dh, back, sends, arrivals, ready, local_sems, table_sem,
):
    ny, nx, bz, rows = dims
    strip = rows // 2
    tall = HALO + strip + SUB
    depth = 2 * bz
    blocks = (HALO + strip) // SUB
    wide_lanes = HALO - SUB
    z, y, x = lax.axis_index("gz"), lax.axis_index("gy"), lax.axis_index("gx")
    routes = routes_of(dims)[0]

    tables = [
        pltpu.make_async_copy(source, target, table_sem)
        for source, target in (
            (light_in, light), (palette_in, palette), (rate_in, rate),
            (shear_in, shear), (offset_in, offset), (order_in, order),
        )
    ]
    barrier = pltpu.get_barrier_semaphore()

    def sided(act):
        for mine in range(2):

            @pl.when(z == mine)
            def _():
                act(mine)

    for there, who in partners_of(dims, (z, y, x), 1):

        @pl.when(there)
        def _():
            pl.semaphore_signal(barrier, inc=1, device_id=who, device_id_type=MESH)

    count = 0
    for there, _ in partners_of(dims, (z, y, x), -1):
        count = count + there.astype(jnp.int32)

    steps = [
        exchange(
            dims, mine, (z, y, x), p_ref, m_ref, cols_out, cols_in, ends_out, ends_in,
            sends, arrivals, ready,
        )
        for mine in range(2)
    ]

    def local_slab(mine):
        route = routes[2 * mine]
        return pltpu.make_async_copy(
            p_ref.at[:, route.rows], m_ref.at[pl.ds(1 + mine * bz, bz), route.lands],
            local_sems.at[1],
        )

    local_tile = pltpu.make_async_copy(p_ref, tile_ref, local_sems.at[0])
    local_tile.start()
    sided(lambda mine: local_slab(mine).start())
    for copy in tables:
        copy.start()

    @pl.when(count > 0)
    def _():
        pl.semaphore_wait(barrier, count)

    for there, who, kind in answers_of(dims, (z, y, x)):

        @pl.when(there)
        def _():
            pl.semaphore_signal(ready.at[kind], inc=1, device_id=who, device_id_type=MESH)


    sided(lambda mine: steps[mine][0]())

    empty = jnp.zeros((tall, LANES), jnp.float32)
    for ref in (m_ref, h_ref):
        ref[0] = empty
        ref[depth + 1] = empty

    def blank(mine):
        route = routes[2 * mine + 1]

        @pl.when(jnp.logical_not(route.comes(y, ny)))
        def _():
            m_ref[:, route.slab] = jnp.zeros((depth + 2, len(route.tiles) * SUB, LANES), jnp.float32)
            cols_in[:, route.base : route.base + route.size] = jnp.zeros(
                (2, route.size, LANES), jnp.float32
            )
            ends_in[:, 1] = jnp.zeros((2, SUB, LANES), jnp.float32)

    sided(blank)

    @pl.when(x == 0)
    def _():
        cols_in[...] = jnp.zeros(cols_in.shape, jnp.float32)

    @pl.when(x == nx - 1)
    def _():
        ends_in[...] = jnp.zeros(ends_in.shape, jnp.float32)

    lane = lax.broadcasted_iota(jnp.int32, (SUB, LANES), 1)
    last = lane == LANES - 1
    first = lane == 0
    groups = routes[0].groups
    tiles = rows // SUB

    def cell(j, t):
        return tile_ref[j, t * SUB : (t + 1) * SUB]

    def put(t_or_fold, is_wide, value):
        for route in routes:
            if t_or_fold in (route.tiles if is_wide else route.folds):
                at = route.sent + (route.wide if is_wide else route.narrow)(t_or_fold)
                cols_out[at : at + SUB] = value

    def merged(pieces):
        while len(pieces) > 1:
            pieces = [
                (a[0], jnp.where(lane >= b[0], b[1], a[1]))
                for a, b in zip(pieces[::2], pieces[1::2])
            ] + (pieces[-1:] if len(pieces) % 2 else [])
        return pieces[0][1]

    def turned(value, by):
        return pltpu.roll(value, by % LANES, 1) if by % LANES else value

    local_tile.wait()
    for t in range(tiles):
        put(
            t, True,
            merged(
                [(wide_lanes * j, turned(cell(j, t), wide_lanes * (j + 1))) for j in range(bz)]
            ),
        )
    for fold in range(tiles // groups):
        put(
            fold, False,
            merged(
                [
                    (
                        SUB * (bz * g + j),
                        turned(cell(j, fold * groups + g), SUB * (bz * g + j) + HALO),
                    )
                    for g in range(groups)
                    for j in range(bz)
                ]
            ),
        )
    ends_out[...] = merged(
        [(t * bz + j, turned(cell(j, t), t * bz + j)) for t in range(tiles) for j in range(bz)]
    )

    def unpack(mine, brick):
        for route in routes[2 * mine : 2 * mine + 2]:
            for t in route.tiles:
                row = (route.first + t - route.tiles[0]) * SUB
                at = route.base + route.wide(t)
                wide = cols_in[brick, at : at + SUB]
                at = route.base + route.narrow(t // groups)
                narrow = cols_in[brick, at : at + SUB]
                for j in range(bz):
                    h_ref[1 + brick * bz + j, row : row + SUB] = jnp.where(
                        lane >= LANES - wide_lanes,
                        turned(wide, -wide_lanes * (j + 1)),
                        turned(narrow, -SUB * (bz * (t % groups) + j) - HALO),
                    )
                r_ref[brick, row : row + SUB] = turned(
                    ends_in[brick, route.half], LANES - 1 - t * bz
                )

    def opening(mine):
        _, send_rest, receive, _ = steps[mine]
        send_rest()
        local_slab(mine).wait()
        receive(mine, (), True)
        own_ref[...] = m_ref[1 + mine * bz : 1 + (mine + 1) * bz]
        unpack(mine, mine)

    def middle(mine):
        receive = steps[mine][2]
        receive(1 - mine, (0,), True)
        near_ref[...] = m_ref[(bz if mine == 0 else 2) + 1 : (depth - 2 if mine == 0 else bz) + 1]
        unpack(mine, 1 - mine)

    def ending(mine, part):
        receive = steps[mine][2]
        receive(1 - mine, (part,), False)

    sided(opening)
    for copy in tables:
        copy.wait()

    towards = []
    for w in range(VIEWS):
        a, b, c = light[w, 0], light[w, 1], light[w, 2]
        inverse = lax.rsqrt(jnp.full((SUB, LANES), a * a + b * b + c * c + 1.0, jnp.float32))
        towards.append((a * inverse, b * inverse, c * inverse))

    def slopes(k, carry):
        for i in range(blocks):
            top = i * SUB
            here = m_ref[k + 1, top + 1 : top + 1 + SUB]
            side = h_ref[k + 1, top + 1 : top + 1 + SUB]
            beyond = pltpu.roll(
                r_ref[k // bz, top + 1 : top + 1 + SUB], (LANES - k % bz) % LANES, 1
            )
            here_r, here_l = pltpu.roll(here, LANES - 1, 1), pltpu.roll(here, 1, 1)
            side_r, side_l = pltpu.roll(side, LANES - 1, 1), pltpu.roll(side, 1, 1)
            for ref, cols, dots in (
                (m_ref, jnp.where(last, beyond, here_r) - jnp.where(first, side_l, here_l), dm),
                (h_ref, jnp.where(last, here_r, side_r) - side_l, dh),
            ):
                deep = ref[k + 2, top + 1 : top + 1 + SUB] - ref[k, top + 1 : top + 1 + SUB]
                down = ref[k + 1, top + 2 : top + 2 + SUB] - ref[k + 1, top : top + SUB]
                half = lax.rsqrt(deep * deep + down * down + cols * cols + 4.0)
                deep, down, cols = deep * half, down * half, cols * half
                for w in range(VIEWS):
                    a, b, c = towards[w]
                    dots[w, k, top : top + SUB] = deep * a + down * b + cols * c
        return carry

    tile = 32
    per_view = strip // tile
    base_row = y * rows + z * strip
    base_col = x * LANES
    lanes = lax.broadcasted_iota(jnp.int32, (tile, LANES), 1)
    rows_at = lax.broadcasted_iota(jnp.int32, (tile, LANES), 0)
    bias = [0.5 * palette[0, c] for c in range(3)]
    gain = [0.5 * palette[1, c] for c in range(3)]

    def march(w, top, brick, first_k, count, cells, start, colors, through):
        ambient = jnp.zeros((tile, LANES), jnp.float32)
        rate2 = rate[w] * (-math.log2(math.e))
        off_r, off_c = offset[brick, 0, w], offset[brick, 1, w]
        inside = jnp.logical_and(rows_at >= off_r - base_row - top, lanes >= off_c - base_col)
        fall = jnp.where(inside, rate2, 0.0)
        for j in range(count):
            k = first_k + j
            sr = off_r + shear[w, 0, k]
            sc = off_c + shear[w, 1, k]
            at = HALO + top - sr
            wrap = lanes >= LANES - sc
            value = jnp.where(wrap, h_ref[k + 1, pl.ds(at, tile)], cells[start + j, pl.ds(at, tile)])
            dot = jnp.where(wrap, dh[w, k, pl.ds(at - 1, tile)], dm[w, k, pl.ds(at - 1, tile)])
            value = pltpu.roll(value, sc, 1)
            dot = pltpu.roll(dot, sc, 1)
            kept = jnp.exp2(fall * (1.0 + jnp.tanh(value)))
            weight = (0.125 + 0.375 * dot * dot) * ((1.0 - kept) * through)
            through = through * kept
            ambient = ambient + weight
            colors = [
                colors[c] + weight * jnp.tanh(bias[c] + gain[c] * value) for c in range(3)
            ]
        return [color + ambient for color in colors], through

    def views(act):
        def one(step, carry):
            act(step // per_view, (step % per_view) * tile)
            return carry

        lax.fori_loop(0, VIEWS * per_view, one, 0, unroll=VIEWS * per_view)

    zero = jnp.zeros((tile, LANES), jnp.float32)
    early = bz - 2
    near, far = bz - early * z, (depth - 2) * (1 - z)

    def own_layer(w, top):
        at = pl.ds(top, tile)
        colors, through = march(
            w, top, z, z * (bz + 1), bz - 1, own_ref, z, [zero] * 3, zero + 1.0
        )
        for c in range(3):
            back[w, c, at] = colors[c]
        back[w, 3, at] = through

    def near_layer(w, top):
        at = pl.ds(top, tile)
        colors, through = march(
            w, top, 1 - z, near, early, near_ref, 0, [zero] * 3, zero + 1.0
        )
        own_first, near_first = order[0, w] == z, z == 0
        edge_colors, edge_through = march(
            w, top, z, bz - 1 + z, 1, own_ref, (1 - z) * (bz - 1), [zero] * 3, zero + 1.0
        )
        inner_through = back[w, 3, at]
        own_through = inner_through * edge_through
        of_inner = jnp.where(near_first, 1.0, edge_through)
        of_edge = jnp.where(near_first, inner_through, 1.0)
        ahead = jnp.where(own_first, own_through, 1.0)
        after = jnp.where(near_first, 1.0, through)
        for c in range(3):
            own_color = of_inner * back[w, c, at] + of_edge * edge_colors[c]
            out_ref[w, c, at] = jnp.where(own_first, own_color, 0.0) + jnp.where(
                near_first, ahead * colors[c], 0.0
            )
            back[w, c, at] = jnp.where(near_first, 0.0, colors[c]) + jnp.where(
                own_first, 0.0, after * own_color
            )
        out_ref[w, 3, at] = ahead * jnp.where(near_first, through, 1.0)
        back[w, 3, at] = after * jnp.where(own_first, 1.0, own_through)

    def far_layer(w, top):
        at = pl.ds(top, tile)
        colors, through = march(
            w, top, 1 - z, far, 2, m_ref, 1 + far, [out_ref[w, c, at] for c in range(3)],
            out_ref[w, 3, at],
        )
        for c in range(3):
            out_ref[w, c, at] = colors[c] + through * back[w, c, at]
        out_ref[w, 3, at] = 1.0 - through * back[w, 3, at]

    def each(start, stop):
        lax.fori_loop(start, stop, slopes, 0)

    each(z * (bz + 1), z * (bz + 1) + bz - 1)
    views(own_layer)
    sided(middle)
    for k in range(2):
        slopes(bz - 1 + k, 0)
    sided(lambda mine: ending(mine, 1))
    each(bz + 1 - 3 * z, bz + 2 - 3 * z)
    views(near_layer)
    sided(lambda mine: ending(mine, 2))
    for k in range(2):
        slopes((1 - z) * (depth - 2) + k, 0)
    views(far_layer)
    sided(lambda mine: steps[mine][3]())


def two_bricks(mesh, pressure, light, palette, rate, shear, offset, order):
    bz, rows, cols = pressure.shape
    dims = (mesh.shape["gy"], mesh.shape["gx"], bz, rows)
    strip = rows // 2
    tall = HALO + strip + SUB
    depth = 2 * bz
    vmem = pl.BlockSpec(memory_space=pltpu.VMEM)
    hbm = pl.BlockSpec(memory_space=pltpu.HBM)
    f32 = jnp.float32
    _, sent, got = routes_of(dims)
    tables = (
        light,
        palette.T,
        rate,
        jnp.transpose(shear, (0, 2, 1)),
        jnp.transpose(offset, (1, 2, 0)),
        order.T,
    )
    image = pl.pallas_call(
        functools.partial(render, dims),
        out_shape=jax.ShapeDtypeStruct((VIEWS, 4, strip, LANES), f32),
        in_specs=[hbm] * 7,
        out_specs=vmem,
        scratch_shapes=[
            *[pltpu.SMEM(table.shape, table.dtype) for table in tables],
            pltpu.VMEM((bz, rows, LANES), f32),
            pltpu.VMEM((depth + 2, tall, LANES), f32),
            pltpu.VMEM((bz, tall, LANES), f32),
            pltpu.VMEM((bz - 2, tall, LANES), f32),
            pltpu.VMEM((2, got, LANES), f32),
            pltpu.VMEM((2, 2, SUB, LANES), f32),
            pltpu.VMEM((sent, LANES), f32),
            pltpu.VMEM((SUB, LANES), f32),
            pltpu.VMEM((depth + 2, tall, LANES), f32),
            pltpu.VMEM((2, tall, LANES), f32),
            pltpu.VMEM((VIEWS, depth, HALO + strip, LANES), f32),
            pltpu.VMEM((VIEWS, depth, HALO + strip, LANES), f32),
            pltpu.VMEM((VIEWS, 4, strip, LANES), f32),
            pltpu.SemaphoreType.DMA,
            pltpu.SemaphoreType.DMA((SLOTS,)),
            pltpu.SemaphoreType.REGULAR((3,)),
            pltpu.SemaphoreType.DMA((2,)),
            pltpu.SemaphoreType.DMA,
        ],
        compiler_params=pltpu.CompilerParams(collective_id=0, has_side_effects=True, vmem_limit_bytes=12 << 20),
        name="render",
    )(
        *[pltpu.with_memory_space_constraint(t, pltpu.HBM) for t in (*tables, pressure)]
    )
    return image[:, :, None]


def fits(mesh, shape):
    bz, rows, cols = shape
    return (
        mesh.shape["gz"] == 2
        and cols == LANES
        and rows % 64 == 0
        and 2 * HALO <= rows <= LANES
        and bz * (HALO - SUB) == LANES
        and bz * (rows // SUB) <= LANES
    )


def on_device(mesh, pressure, *rest):
    if fits(mesh, pressure.shape):
        return two_bricks(mesh, pressure, *rest)
    return many_bricks(pressure, *rest)


def solution(mesh):
    return jax.shard_map(
        functools.partial(on_device, mesh),
        mesh=mesh,
        in_specs=(P("gz", "gy", "gx"), P(), P(), P(), P(), P(), P()),
        out_specs=P(None, None, "gz", "gy", "gx"),
        check_vma=False,
    )
```

```python
import functools
import math

import jax
import jax.numpy as jnp
from jax import lax
from jax.experimental import pallas as pl
from jax.experimental.pallas import tpu as pltpu
from jax.sharding import PartitionSpec as P

VIEWS = 4
SHEAR = 8
REACH = 32
HALO = SHEAR + REACH
SUB = 8
LANES = 128
MESH = pl.DeviceIdType.MESH


def padded(cells, sides, width):
    for axis, dim in sides:
        count = lax.axis_size(axis)
        ends = count - 1
        head = lax.slice_in_dim(cells, 0, width, axis=dim)
        tail = lax.slice_in_dim(cells, cells.shape[dim] - width, cells.shape[dim], axis=dim)
        cells = jnp.concatenate(
            [
                lax.ppermute(tail, axis, [(i, (i + 1) % count) for i in range(ends)]),
                cells,
                lax.ppermute(head, axis, [((i + 1) % count, i) for i in range(ends)]),
            ],
            axis=dim,
        )
    return cells


def shifted(value, axis, steps):
    count = lax.axis_size(axis)
    first, last = (max(0, -steps), min(count, count - steps))
    return lax.ppermute(value, axis, [(source, source + steps) for source in range(first, last)])


def surface_terms(slab):
    inner = slab[1:-1, 1:-1, 1:-1]
    grad_depth = 0.5 * (slab[2:, 1:-1, 1:-1] - slab[:-2, 1:-1, 1:-1])
    grad_rows = 0.5 * (slab[1:-1, 2:, 1:-1] - slab[1:-1, :-2, 1:-1])
    grad_cols = 0.5 * (slab[1:-1, 1:-1, 2:] - slab[1:-1, 1:-1, :-2])
    factor = lax.rsqrt(
        grad_depth * grad_depth + grad_rows * grad_rows + grad_cols * grad_cols + 1.0
    )
    return (inner, (grad_depth * factor, grad_rows * factor, grad_cols * factor))


def render_layers(inner, normals, shifts, light, palette, rate, rows, cols):
    lengths = jnp.sqrt(jnp.sum(light * light, axis=1, keepdims=True) + 1.0)
    towards = light / lengths
    offsets = palette[:, 0][:, None, None]
    slopes = palette[:, 1][:, None, None]
    layers = []
    for view in range(light.shape[0]):

        def advance(carry, items):
            color, depth = carry
            value_slab, normal_depth, normal_rows, normal_cols, moved = items
            start = (SHEAR - moved[0], SHEAR - moved[1])
            value = lax.dynamic_slice(value_slab, start, (rows, cols))
            dot = (
                lax.dynamic_slice(normal_depth, start, (rows, cols)) * towards[view, 0]
                + lax.dynamic_slice(normal_rows, start, (rows, cols)) * towards[view, 1]
                + lax.dynamic_slice(normal_cols, start, (rows, cols)) * towards[view, 2]
            )
            shade = 0.25 + 0.75 * dot * dot
            density = rate[view] * (1.0 + jnp.tanh(value))
            alpha = 1.0 - jnp.exp(-density)
            weight = alpha * jnp.exp(-depth)
            hues = jax.nn.sigmoid(offsets + slopes * value[None]) * shade[None]
            return ((color + hues * weight[None], depth + density), None)

        start_carry = (
            jnp.zeros((3, rows, cols), jnp.float32),
            jnp.zeros((rows, cols), jnp.float32),
        )
        (color, depth), _ = lax.scan(
            advance, start_carry, (inner, normals[0], normals[1], normals[2], shifts[view])
        )
        layers.append(jnp.concatenate([color, depth[None]], axis=0))
    return jnp.stack(layers)


def precedence(order):
    bricks = order.shape[1]
    onehot = (order[:, :, None] == jnp.arange(bricks, dtype=jnp.int32)[None, None, :]).astype(
        jnp.float32
    )
    ranks = jnp.sum(onehot * jnp.arange(bricks, dtype=jnp.float32)[None, :, None], axis=1)
    return (ranks[:, None, :] < ranks[:, :, None]).astype(jnp.float32)


def many_bricks(pressure, light, palette, rate, shear, offset, order):
    depth_cells, rows, cols = pressure.shape
    brick = lax.axis_index("gz")
    zero = jnp.zeros((), jnp.int32)
    widened = padded(pressure, (("gy", 1), ("gx", 2)), SHEAR + 1)
    slab = padded(widened, (("gz", 0),), 1)
    inner, normals = surface_terms(slab)
    shifts = lax.dynamic_slice(shear, (zero, brick * depth_cells, zero), (VIEWS, depth_cells, 2))
    layers = render_layers(inner, normals, shifts, light, palette, rate, rows, cols)
    moved = lax.dynamic_index_in_dim(offset, brick, 1, keepdims=False)
    blank = jnp.zeros((4, rows + REACH, cols + REACH), jnp.float32)
    canvas = jnp.stack(
        [
            lax.dynamic_update_slice(blank, layers[view], (zero, moved[view, 0], moved[view, 1]))
            for view in range(VIEWS)
        ]
    )
    own_tile = canvas[:, :, :rows, :cols]
    from_above = shifted(canvas[:, :, rows:, :cols], "gy", 1)
    from_left = shifted(canvas[:, :, :rows, cols:], "gx", 1)
    from_diagonal = shifted(canvas[:, :, rows:, cols:], ("gy", "gx"), lax.axis_size("gx") + 1)
    from_diagonal = from_diagonal * (lax.axis_index("gx") > 0).astype(jnp.float32)
    own_tile = own_tile.at[:, :, :REACH, :].add(from_above)
    own_tile = own_tile.at[:, :, :, :REACH].add(from_left)
    own_tile = own_tile.at[:, :, :REACH, :REACH].add(from_diagonal)
    ranking = precedence(order)
    pieces = lax.all_to_all(own_tile[None], "gz", split_axis=3, concat_axis=0, tiled=True)
    depths = pieces[:, :, 3]
    cover = jnp.einsum("vbc,cvyx->bvyx", ranking, depths, precision=lax.Precision.HIGHEST)
    colors = jnp.sum(pieces[:, :, :3] * jnp.exp(-cover)[:, :, None], axis=0)
    opacity = 1.0 - jnp.exp(-jnp.sum(depths, axis=0))
    image = jnp.concatenate([colors, opacity[:, None]], axis=1)
    return image[:, :, None]


class Route:
    def __init__(self, dims, side, step, start, count, slab, half):
        bz = dims[2]
        self.side, self.step, self.half = side, step, half
        self.slab = pl.ds(slab, count)
        needed = count - SUB + 1 if start == 0 else count
        self.rows, self.lands = pl.ds(start, needed), pl.ds(slab, needed)
        self.groups = LANES // (SUB * bz)
        self.tiles = range(start // SUB, (start + count) // SUB)
        self.first = slab // SUB
        self.folds = range(
            self.tiles[0] // self.groups, self.tiles[-1] // self.groups + 1
        )
        self.size = (len(self.tiles) + len(self.folds)) * SUB
        self.base = self.sent = 0

    def there(self, y, ny):
        return y + self.step >= 0 if self.step < 0 else y + self.step < ny

    def comes(self, y, ny):
        return y - self.step < ny if self.step < 0 else y - self.step >= 0

    def wide(self, tile):
        return (tile - self.tiles[0]) * SUB

    def narrow(self, fold):
        return (len(self.tiles) + fold - self.folds[0]) * SUB


def routes_of(dims):
    rows = dims[3]
    strip = rows // 2
    routes = [
        Route(dims, 0, 0, 0, strip + SUB, HALO, 0),
        Route(dims, 0, 1, rows - HALO, HALO, 0, 1),
        Route(dims, 1, 0, strip - HALO, HALO + strip, 0, 0),
        Route(dims, 1, -1, 0, SUB, HALO + strip, 1),
    ]
    sent = 0
    for route in routes:
        route.sent = sent
        sent += route.size
    routes[1].base, routes[3].base = routes[0].size, routes[2].size
    return routes, sent, max(routes[0].size + routes[1].size, routes[2].size + routes[3].size)


MAIN, EDGE, BESIDE, COLS, ENDS, SLOTS = 0, 3, 6, 7, 11, 15
PARTS = 3
BELOW, RIGHT, ACROSS = range(3)


def exchange(
    dims, mine, here, p_ref, m_ref, cols_out, cols_in, ends_out, ends_in, sends, arrivals, ready
):
    ny, nx, bz, rows = dims
    z, y, x = here
    has_left, has_right = x > 0, x < nx - 1
    has_up, has_down = y > 0, y < ny - 1
    routes = routes_of(dims)[0]

    def remote(src, dst, arrival, who):
        return pltpu.make_async_remote_copy(
            src_ref=src,
            dst_ref=dst,
            send_sem=sends,
            recv_sem=arrivals.at[arrival],
            device_id=who,
            device_id_type=MESH,
        )

    def rows_of(brick, route, part):
        first = bz - PARTS + 1
        start = first + part - 1 if part else 0
        count = bz if part is None else 1 if part else first
        if part is not None and brick == 0:
            start = bz - start - count
        slot = BESIDE if part is None else (EDGE if route.half else MAIN) + part
        return remote(
            p_ref.at[pl.ds(start, count), route.rows],
            m_ref.at[pl.ds(1 + brick * bz + start, count), route.lands],
            slot, (route.side, y + route.step, x),
        )

    def cols_of(brick, route):
        return remote(
            cols_out.at[pl.ds(route.sent, route.size)],
            cols_in.at[brick, pl.ds(route.base, route.size)],
            COLS + 2 * brick + route.half,
            (route.side, y + route.step, x + 1),
        )

    def ends_of(brick, route):
        return remote(
            ends_out,
            ends_in.at[brick, route.half],
            ENDS + 2 * brick + route.half,
            (route.side, y + route.step, x - 1),
        )

    def rows_out(route, part=0):
        there = route.there(y, ny)
        if route.side != mine:
            return [(there, rows_of(mine, route, part))]
        return [(there, rows_of(mine, route, None))] if route.half else []

    def cols_sent(same):
        return [
            (jnp.logical_and(r.there(y, ny), has_right), cols_of(mine, r))
            for r in routes
            if (r.side == mine) == same
        ]

    def ends_sent():
        return [(jnp.logical_and(r.there(y, ny), has_left), ends_of(mine, r)) for r in routes]

    def apply(pairs, act):
        for there, copy in pairs:

            @pl.when(there)
            def _():
                act(copy)

    def start(pairs):
        apply(pairs, lambda copy: copy.start())

    def heard(kind, there, count):
        @pl.when(there)
        def _():
            pl.semaphore_wait(ready.at[kind], count)

    mains, own_halo, halos = (
        (routes[2], routes[1], routes[3]) if mine == 0 else (routes[0], routes[3], routes[1])
    )
    first, second = (halos, mains) if mine == 0 else (mains, halos)
    next_ones = [1 + there.astype(jnp.int32) for there in (has_down, has_up)]

    def send_first():
        if mine == 0:
            start(rows_out(halos))
            start(rows_out(mains))
        else:
            start(rows_out(mains))
            start(rows_out(own_halo))

    def send_rest():
        if mine == 0:
            start(ends_sent())
            heard(BELOW, has_down, 1)
            start(rows_out(own_halo))
        else:
            start(ends_sent())
        heard(RIGHT, has_right, next_ones[mine])
        start(cols_sent(True))
        if mine == 1:
            heard(BELOW, has_down, 1)
            start(rows_out(halos))
        start(rows_out(first, 1) + rows_out(second, 1))
        heard(ACROSS, has_right, next_ones[1 - mine])
        start(cols_sent(False))
        start(rows_out(first, 2) + rows_out(second, 2))

    def receive(brick, parts, sides):
        pairs = []
        for route in routes:
            if route.side != mine:
                continue
            comes = route.comes(y, ny)
            if brick != mine:
                pairs += [(comes, rows_of(brick, route, part)) for part in parts]
            elif route.half:
                pairs += [(comes, rows_of(brick, route, None))]
            if sides:
                pairs += [
                    (jnp.logical_and(comes, has_left), cols_of(brick, route)),
                    (jnp.logical_and(comes, has_right), ends_of(brick, route)),
                ]
        apply(pairs, lambda copy: copy.wait_recv())

    def close():
        for part in range(PARTS):
            apply(rows_out(mains, part) + rows_out(halos, part), lambda copy: copy.wait_send())
        apply(rows_out(own_halo), lambda copy: copy.wait_send())
        apply(ends_sent() + cols_sent(True) + cols_sent(False), lambda copy: copy.wait_send())

    return send_first, send_rest, receive, close


def partners_of(dims, here, over):
    ny, nx = dims[:2]
    z, y, x = here
    steps = [(z, over, 0), (1 - z, 0, 0)]
    diagonal = z == 1 if over > 0 else z == 0
    yield jnp.logical_and(diagonal, inside_of(dims, y + over, x)), (1 - z, y + over, x)
    steps += [
        (side, step, over)
        for side, step in ((z, -1), (z, 0), (z, 1), (1 - z, 0), (1 - z, 2 * z - 1))
    ]
    for side, step, across in steps:
        yield inside_of(dims, y + step, x + across), (side, y + step, x + across)


def inside_of(dims, y, x):
    ny, nx = dims[:2]
    return jnp.logical_and(
        jnp.logical_and(y >= 0, y < ny), jnp.logical_and(x >= 0, x < nx)
    )


def answers_of(dims, here):
    z, y, x = here
    own = z == 0
    yield jnp.logical_and(own, y > 0), (z, y - 1, x), BELOW
    yield jnp.logical_and(own, y > 0), (1 - z, y - 1, x), BELOW
    for side, kind in ((z, RIGHT), (1 - z, ACROSS)):
        for step in (0, 2 * z - 1):
            yield inside_of(dims, y + step, x - 1), (side, y + step, x - 1), kind


def render(
    dims, light_in, palette_in, rate_in, shear_in, offset_in, order_in, p_ref, out_ref,
    light, palette, rate, shear, offset, order, tile_ref, m_ref, own_ref, near_ref, cols_in, ends_in,
    cols_out, ends_out, h_ref, r_ref, dm, dh, back, sends, arrivals, ready, local_sems, table_sem,
):
    ny, nx, bz, rows = dims
    strip = rows // 2
    tall = HALO + strip + SUB
    depth = 2 * bz
    blocks = (HALO + strip) // SUB
    wide_lanes = HALO - SUB
    z, y, x = lax.axis_index("gz"), lax.axis_index("gy"), lax.axis_index("gx")
    routes = routes_of(dims)[0]

    tables = [
        pltpu.make_async_copy(source, target, table_sem)
        for source, target in (
            (light_in, light), (palette_in, palette), (rate_in, rate),
            (shear_in, shear), (offset_in, offset), (order_in, order),
        )
    ]
    barrier = pltpu.get_barrier_semaphore()

    def sided(act):
        for mine in range(2):

            @pl.when(z == mine)
            def _():
                act(mine)

    for there, who in partners_of(dims, (z, y, x), 1):

        @pl.when(there)
        def _():
            pl.semaphore_signal(barrier, inc=1, device_id=who, device_id_type=MESH)

    count = 0
    for there, _ in partners_of(dims, (z, y, x), -1):
        count = count + there.astype(jnp.int32)

    steps = [
        exchange(
            dims, mine, (z, y, x), p_ref, m_ref, cols_out, cols_in, ends_out, ends_in,
            sends, arrivals, ready,
        )
        for mine in range(2)
    ]

    def local_slab(mine):
        route = routes[2 * mine]
        return pltpu.make_async_copy(
            p_ref.at[:, route.rows], m_ref.at[pl.ds(1 + mine * bz, bz), route.lands],
            local_sems.at[1],
        )

    local_tile = pltpu.make_async_copy(p_ref, tile_ref, local_sems.at[0])
    local_tile.start()
    sided(lambda mine: local_slab(mine).start())
    for copy in tables:
        copy.start()

    @pl.when(count > 0)
    def _():
        pl.semaphore_wait(barrier, count)

    for there, who, kind in answers_of(dims, (z, y, x)):

        @pl.when(there)
        def _():
            pl.semaphore_signal(ready.at[kind], inc=1, device_id=who, device_id_type=MESH)


    sided(lambda mine: steps[mine][0]())

    empty = jnp.zeros((tall, LANES), jnp.float32)
    for ref in (m_ref, h_ref):
        ref[0] = empty
        ref[depth + 1] = empty

    def blank(mine):
        route = routes[2 * mine + 1]

        @pl.when(jnp.logical_not(route.comes(y, ny)))
        def _():
            m_ref[:, route.slab] = jnp.zeros((depth + 2, len(route.tiles) * SUB, LANES), jnp.float32)
            cols_in[:, route.base : route.base + route.size] = jnp.zeros(
                (2, route.size, LANES), jnp.float32
            )
            ends_in[:, 1] = jnp.zeros((2, SUB, LANES), jnp.float32)

    sided(blank)

    @pl.when(x == 0)
    def _():
        cols_in[...] = jnp.zeros(cols_in.shape, jnp.float32)

    @pl.when(x == nx - 1)
    def _():
        ends_in[...] = jnp.zeros(ends_in.shape, jnp.float32)

    lane = lax.broadcasted_iota(jnp.int32, (SUB, LANES), 1)
    last = lane == LANES - 1
    first = lane == 0
    groups = routes[0].groups
    tiles = rows // SUB

    def cell(j, t):
        return tile_ref[j, t * SUB : (t + 1) * SUB]

    def put(t_or_fold, is_wide, value):
        for route in routes:
            if t_or_fold in (route.tiles if is_wide else route.folds):
                at = route.sent + (route.wide if is_wide else route.narrow)(t_or_fold)
                cols_out[at : at + SUB] = value

    def merged(pieces):
        while len(pieces) > 1:
            pieces = [
                (a[0], jnp.where(lane >= b[0], b[1], a[1]))
                for a, b in zip(pieces[::2], pieces[1::2])
            ] + (pieces[-1:] if len(pieces) % 2 else [])
        return pieces[0][1]

    def turned(value, by):
        return pltpu.roll(value, by % LANES, 1) if by % LANES else value

    local_tile.wait()
    for t in range(tiles):
        put(
            t, True,
            merged(
                [(wide_lanes * j, turned(cell(j, t), wide_lanes * (j + 1))) for j in range(bz)]
            ),
        )
    for fold in range(tiles // groups):
        put(
            fold, False,
            merged(
                [
                    (
                        SUB * (bz * g + j),
                        turned(cell(j, fold * groups + g), SUB * (bz * g + j) + HALO),
                    )
                    for g in range(groups)
                    for j in range(bz)
                ]
            ),
        )
    ends_out[...] = merged(
        [(t * bz + j, turned(cell(j, t), t * bz + j)) for t in range(tiles) for j in range(bz)]
    )

    def unpack(mine, brick):
        for route in routes[2 * mine : 2 * mine + 2]:
            for t in route.tiles:
                row = (route.first + t - route.tiles[0]) * SUB
                at = route.base + route.wide(t)
                wide = cols_in[brick, at : at + SUB]
                at = route.base + route.narrow(t // groups)
                narrow = cols_in[brick, at : at + SUB]
                for j in range(bz):
                    h_ref[1 + brick * bz + j, row : row + SUB] = jnp.where(
                        lane >= LANES - wide_lanes,
                        turned(wide, -wide_lanes * (j + 1)),
                        turned(narrow, -SUB * (bz * (t % groups) + j) - HALO),
                    )
                r_ref[brick, row : row + SUB] = turned(
                    ends_in[brick, route.half], LANES - 1 - t * bz
                )

    def opening(mine):
        _, send_rest, receive, _ = steps[mine]
        send_rest()
        local_slab(mine).wait()
        receive(mine, (), True)
        own_ref[...] = m_ref[1 + mine * bz : 1 + (mine + 1) * bz]
        unpack(mine, mine)

    def middle(mine):
        receive = steps[mine][2]
        receive(1 - mine, (0,), True)
        near_ref[...] = m_ref[(bz if mine == 0 else 2) + 1 : (depth - 2 if mine == 0 else bz) + 1]
        unpack(mine, 1 - mine)

    def ending(mine, part):
        receive = steps[mine][2]
        receive(1 - mine, (part,), False)

    sided(opening)
    for copy in tables:
        copy.wait()

    towards = []
    for w in range(VIEWS):
        a, b, c = light[w, 0], light[w, 1], light[w, 2]
        inverse = lax.rsqrt(jnp.full((SUB, LANES), a * a + b * b + c * c + 1.0, jnp.float32))
        towards.append((a * inverse, b * inverse, c * inverse))

    def slopes(k, carry):
        for i in range(blocks):
            top = i * SUB
            here = m_ref[k + 1, top + 1 : top + 1 + SUB]
            side = h_ref[k + 1, top + 1 : top + 1 + SUB]
            beyond = pltpu.roll(
                r_ref[k // bz, top + 1 : top + 1 + SUB], (LANES - k % bz) % LANES, 1
            )
            here_r, here_l = pltpu.roll(here, LANES - 1, 1), pltpu.roll(here, 1, 1)
            side_r, side_l = pltpu.roll(side, LANES - 1, 1), pltpu.roll(side, 1, 1)
            for ref, cols, dots in (
                (m_ref, jnp.where(last, beyond, here_r) - jnp.where(first, side_l, here_l), dm),
                (h_ref, jnp.where(last, here_r, side_r) - side_l, dh),
            ):
                deep = ref[k + 2, top + 1 : top + 1 + SUB] - ref[k, top + 1 : top + 1 + SUB]
                down = ref[k + 1, top + 2 : top + 2 + SUB] - ref[k + 1, top : top + SUB]
                half = lax.rsqrt(deep * deep + down * down + cols * cols + 4.0)
                deep, down, cols = deep * half, down * half, cols * half
                for w in range(VIEWS):
                    a, b, c = towards[w]
                    dots[w, k, top : top + SUB] = deep * a + down * b + cols * c
        return carry

    tile = 32
    per_view = strip // tile
    base_row = y * rows + z * strip
    base_col = x * LANES
    lanes = lax.broadcasted_iota(jnp.int32, (tile, LANES), 1)
    rows_at = lax.broadcasted_iota(jnp.int32, (tile, LANES), 0)
    bias = [0.5 * palette[0, c] for c in range(3)]
    gain = [0.5 * palette[1, c] for c in range(3)]

    def march(w, top, brick, first_k, count, cells, start, colors, through):
        ambient = jnp.zeros((tile, LANES), jnp.float32)
        rate2 = rate[w] * (-math.log2(math.e))
        off_r, off_c = offset[brick, 0, w], offset[brick, 1, w]
        inside = jnp.logical_and(rows_at >= off_r - base_row - top, lanes >= off_c - base_col)
        fall = jnp.where(inside, rate2, 0.0)
        for j in range(count):
            k = first_k + j
            sr = off_r + shear[w, 0, k]
            sc = off_c + shear[w, 1, k]
            at = HALO + top - sr
            wrap = lanes >= LANES - sc
            value = jnp.where(wrap, h_ref[k + 1, pl.ds(at, tile)], cells[start + j, pl.ds(at, tile)])
            dot = jnp.where(wrap, dh[w, k, pl.ds(at - 1, tile)], dm[w, k, pl.ds(at - 1, tile)])
            value = pltpu.roll(value, sc, 1)
            dot = pltpu.roll(dot, sc, 1)
            kept = jnp.exp2(fall * (1.0 + jnp.tanh(value)))
            weight = (0.125 + 0.375 * dot * dot) * ((1.0 - kept) * through)
            through = through * kept
            ambient = ambient + weight
            colors = [
                colors[c] + weight * jnp.tanh(bias[c] + gain[c] * value) for c in range(3)
            ]
        return [color + ambient for color in colors], through

    def views(act):
        def one(step, carry):
            act(step // per_view, (step % per_view) * tile)
            return carry

        lax.fori_loop(0, VIEWS * per_view, one, 0, unroll=VIEWS * per_view)

    zero = jnp.zeros((tile, LANES), jnp.float32)
    early = bz - 2
    near, far = bz - early * z, (depth - 2) * (1 - z)

    def own_layer(w, top):
        at = pl.ds(top, tile)
        colors, through = march(
            w, top, z, z * (bz + 1), bz - 1, own_ref, z, [zero] * 3, zero + 1.0
        )
        for c in range(3):
            back[w, c, at] = colors[c]
        back[w, 3, at] = through

    def near_layer(w, top):
        at = pl.ds(top, tile)
        colors, through = march(
            w, top, 1 - z, near, early, near_ref, 0, [zero] * 3, zero + 1.0
        )
        own_first, near_first = order[0, w] == z, z == 0
        edge_colors, edge_through = march(
            w, top, z, bz - 1 + z, 1, own_ref, (1 - z) * (bz - 1), [zero] * 3, zero + 1.0
        )
        inner_through = back[w, 3, at]
        own_through = inner_through * edge_through
        of_inner = jnp.where(near_first, 1.0, edge_through)
        of_edge = jnp.where(near_first, inner_through, 1.0)
        ahead = jnp.where(own_first, own_through, 1.0)
        after = jnp.where(near_first, 1.0, through)
        for c in range(3):
            own_color = of_inner * back[w, c, at] + of_edge * edge_colors[c]
            out_ref[w, c, at] = jnp.where(own_first, own_color, 0.0) + jnp.where(
                near_first, ahead * colors[c], 0.0
            )
            back[w, c, at] = jnp.where(near_first, 0.0, colors[c]) + jnp.where(
                own_first, 0.0, after * own_color
            )
        out_ref[w, 3, at] = ahead * jnp.where(near_first, through, 1.0)
        back[w, 3, at] = after * jnp.where(own_first, 1.0, own_through)

    def far_layer(w, top):
        at = pl.ds(top, tile)
        colors, through = march(
            w, top, 1 - z, far, 2, m_ref, 1 + far, [out_ref[w, c, at] for c in range(3)],
            out_ref[w, 3, at],
        )
        for c in range(3):
            out_ref[w, c, at] = colors[c] + through * back[w, c, at]
        out_ref[w, 3, at] = 1.0 - through * back[w, 3, at]

    def each(start, stop):
        lax.fori_loop(start, stop, slopes, 0)

    each(z * (bz + 1), z * (bz + 1) + bz - 1)
    views(own_layer)
    sided(middle)
    for k in range(2):
        slopes(bz - 1 + k, 0)
    sided(lambda mine: ending(mine, 1))
    each(bz + 1 - 3 * z, bz + 2 - 3 * z)
    views(near_layer)
    sided(lambda mine: ending(mine, 2))
    for k in range(2):
        slopes((1 - z) * (depth - 2) + k, 0)
    views(far_layer)
    sided(lambda mine: steps[mine][3]())


def two_bricks(mesh, pressure, light, palette, rate, shear, offset, order):
    bz, rows, cols = pressure.shape
    dims = (mesh.shape["gy"], mesh.shape["gx"], bz, rows)
    strip = rows // 2
    tall = HALO + strip + SUB
    depth = 2 * bz
    vmem = pl.BlockSpec(memory_space=pltpu.VMEM)
    hbm = pl.BlockSpec(memory_space=pltpu.HBM)
    f32 = jnp.float32
    _, sent, got = routes_of(dims)
    tables = (
        light,
        palette.T,
        rate,
        jnp.transpose(shear, (0, 2, 1)),
        jnp.transpose(offset, (1, 2, 0)),
        order.T,
    )
    image = pl.pallas_call(
        functools.partial(render, dims),
        out_shape=jax.ShapeDtypeStruct((VIEWS, 4, strip, LANES), f32),
        in_specs=[hbm] * 7,
        out_specs=vmem,
        scratch_shapes=[
            *[pltpu.SMEM(table.shape, table.dtype) for table in tables],
            pltpu.VMEM((bz, rows, LANES), f32),
            pltpu.VMEM((depth + 2, tall, LANES), f32),
            pltpu.VMEM((bz, tall, LANES), f32),
            pltpu.VMEM((bz - 2, tall, LANES), f32),
            pltpu.VMEM((2, got, LANES), f32),
            pltpu.VMEM((2, 2, SUB, LANES), f32),
            pltpu.VMEM((sent, LANES), f32),
            pltpu.VMEM((SUB, LANES), f32),
            pltpu.VMEM((depth + 2, tall, LANES), f32),
            pltpu.VMEM((2, tall, LANES), f32),
            pltpu.VMEM((VIEWS, depth, HALO + strip, LANES), f32),
            pltpu.VMEM((VIEWS, depth, HALO + strip, LANES), f32),
            pltpu.VMEM((VIEWS, 4, strip, LANES), f32),
            pltpu.SemaphoreType.DMA,
            pltpu.SemaphoreType.DMA((SLOTS,)),
            pltpu.SemaphoreType.REGULAR((3,)),
            pltpu.SemaphoreType.DMA((2,)),
            pltpu.SemaphoreType.DMA,
        ],
        compiler_params=pltpu.CompilerParams(collective_id=0, has_side_effects=True, vmem_limit_bytes=12 << 20),
        name="render",
    )(
        *[pltpu.with_memory_space_constraint(t, pltpu.HBM) for t in (*tables, pressure)]
    )
    return image[:, :, None]


def fits(mesh, shape):
    bz, rows, cols = shape
    return (
        mesh.shape["gz"] == 2
        and cols == LANES
        and rows % 64 == 0
        and 2 * HALO <= rows <= LANES
        and bz * (HALO - SUB) == LANES
        and bz * (rows // SUB) <= LANES
    )


def on_device(mesh, pressure, *rest):
    if fits(mesh, pressure.shape):
        return two_bricks(mesh, pressure, *rest)
    return many_bricks(pressure, *rest)


def solution(mesh):
    return jax.shard_map(
        functools.partial(on_device, mesh),
        mesh=mesh,
        in_specs=(P("gz", "gy", "gx"), P(), P(), P(), P(), P(), P()),
        out_specs=P(None, None, "gz", "gy", "gx"),
        check_vma=False,
    )
```

```python
import functools
import math

import jax
import jax.numpy as jnp
from jax import lax
from jax.experimental import pallas as pl
from jax.experimental.pallas import tpu as pltpu
from jax.sharding import PartitionSpec as P

VIEWS = 4
SHEAR = 8
REACH = 32
HALO = SHEAR + REACH
SUB = 8
LANES = 128
MESH = pl.DeviceIdType.MESH


def padded(cells, sides, width):
    for axis, dim in sides:
        count = lax.axis_size(axis)
        ends = count - 1
        head = lax.slice_in_dim(cells, 0, width, axis=dim)
        tail = lax.slice_in_dim(cells, cells.shape[dim] - width, cells.shape[dim], axis=dim)
        cells = jnp.concatenate(
            [
                lax.ppermute(tail, axis, [(i, (i + 1) % count) for i in range(ends)]),
                cells,
                lax.ppermute(head, axis, [((i + 1) % count, i) for i in range(ends)]),
            ],
            axis=dim,
        )
    return cells


def shifted(value, axis, steps):
    count = lax.axis_size(axis)
    first, last = (max(0, -steps), min(count, count - steps))
    return lax.ppermute(value, axis, [(source, source + steps) for source in range(first, last)])


def surface_terms(slab):
    inner = slab[1:-1, 1:-1, 1:-1]
    grad_depth = 0.5 * (slab[2:, 1:-1, 1:-1] - slab[:-2, 1:-1, 1:-1])
    grad_rows = 0.5 * (slab[1:-1, 2:, 1:-1] - slab[1:-1, :-2, 1:-1])
    grad_cols = 0.5 * (slab[1:-1, 1:-1, 2:] - slab[1:-1, 1:-1, :-2])
    factor = lax.rsqrt(
        grad_depth * grad_depth + grad_rows * grad_rows + grad_cols * grad_cols + 1.0
    )
    return (inner, (grad_depth * factor, grad_rows * factor, grad_cols * factor))


def render_layers(inner, normals, shifts, light, palette, rate, rows, cols):
    lengths = jnp.sqrt(jnp.sum(light * light, axis=1, keepdims=True) + 1.0)
    towards = light / lengths
    offsets = palette[:, 0][:, None, None]
    slopes = palette[:, 1][:, None, None]
    layers = []
    for view in range(light.shape[0]):

        def advance(carry, items):
            color, depth = carry
            value_slab, normal_depth, normal_rows, normal_cols, moved = items
            start = (SHEAR - moved[0], SHEAR - moved[1])
            value = lax.dynamic_slice(value_slab, start, (rows, cols))
            dot = (
                lax.dynamic_slice(normal_depth, start, (rows, cols)) * towards[view, 0]
                + lax.dynamic_slice(normal_rows, start, (rows, cols)) * towards[view, 1]
                + lax.dynamic_slice(normal_cols, start, (rows, cols)) * towards[view, 2]
            )
            shade = 0.25 + 0.75 * dot * dot
            density = rate[view] * (1.0 + jnp.tanh(value))
            alpha = 1.0 - jnp.exp(-density)
            weight = alpha * jnp.exp(-depth)
            hues = jax.nn.sigmoid(offsets + slopes * value[None]) * shade[None]
            return ((color + hues * weight[None], depth + density), None)

        start_carry = (
            jnp.zeros((3, rows, cols), jnp.float32),
            jnp.zeros((rows, cols), jnp.float32),
        )
        (color, depth), _ = lax.scan(
            advance, start_carry, (inner, normals[0], normals[1], normals[2], shifts[view])
        )
        layers.append(jnp.concatenate([color, depth[None]], axis=0))
    return jnp.stack(layers)


def precedence(order):
    bricks = order.shape[1]
    onehot = (order[:, :, None] == jnp.arange(bricks, dtype=jnp.int32)[None, None, :]).astype(
        jnp.float32
    )
    ranks = jnp.sum(onehot * jnp.arange(bricks, dtype=jnp.float32)[None, :, None], axis=1)
    return (ranks[:, None, :] < ranks[:, :, None]).astype(jnp.float32)


def many_bricks(pressure, light, palette, rate, shear, offset, order):
    depth_cells, rows, cols = pressure.shape
    brick = lax.axis_index("gz")
    zero = jnp.zeros((), jnp.int32)
    widened = padded(pressure, (("gy", 1), ("gx", 2)), SHEAR + 1)
    slab = padded(widened, (("gz", 0),), 1)
    inner, normals = surface_terms(slab)
    shifts = lax.dynamic_slice(shear, (zero, brick * depth_cells, zero), (VIEWS, depth_cells, 2))
    layers = render_layers(inner, normals, shifts, light, palette, rate, rows, cols)
    moved = lax.dynamic_index_in_dim(offset, brick, 1, keepdims=False)
    blank = jnp.zeros((4, rows + REACH, cols + REACH), jnp.float32)
    canvas = jnp.stack(
        [
            lax.dynamic_update_slice(blank, layers[view], (zero, moved[view, 0], moved[view, 1]))
            for view in range(VIEWS)
        ]
    )
    own_tile = canvas[:, :, :rows, :cols]
    from_above = shifted(canvas[:, :, rows:, :cols], "gy", 1)
    from_left = shifted(canvas[:, :, :rows, cols:], "gx", 1)
    from_diagonal = shifted(canvas[:, :, rows:, cols:], ("gy", "gx"), lax.axis_size("gx") + 1)
    from_diagonal = from_diagonal * (lax.axis_index("gx") > 0).astype(jnp.float32)
    own_tile = own_tile.at[:, :, :REACH, :].add(from_above)
    own_tile = own_tile.at[:, :, :, :REACH].add(from_left)
    own_tile = own_tile.at[:, :, :REACH, :REACH].add(from_diagonal)
    ranking = precedence(order)
    pieces = lax.all_to_all(own_tile[None], "gz", split_axis=3, concat_axis=0, tiled=True)
    depths = pieces[:, :, 3]
    cover = jnp.einsum("vbc,cvyx->bvyx", ranking, depths, precision=lax.Precision.HIGHEST)
    colors = jnp.sum(pieces[:, :, :3] * jnp.exp(-cover)[:, :, None], axis=0)
    opacity = 1.0 - jnp.exp(-jnp.sum(depths, axis=0))
    image = jnp.concatenate([colors, opacity[:, None]], axis=1)
    return image[:, :, None]


class Route:
    def __init__(self, dims, side, step, start, count, slab, half):
        bz = dims[2]
        self.side, self.step, self.half = side, step, half
        self.slab = pl.ds(slab, count)
        needed = count - SUB + 1 if start == 0 else count
        self.rows, self.lands = pl.ds(start, needed), pl.ds(slab, needed)
        self.groups = LANES // (SUB * bz)
        self.tiles = range(start // SUB, (start + count) // SUB)
        self.first = slab // SUB
        self.folds = range(
            self.tiles[0] // self.groups, self.tiles[-1] // self.groups + 1
        )
        self.size = (len(self.tiles) + len(self.folds)) * SUB
        self.base = self.sent = 0

    def there(self, y, ny):
        return y + self.step >= 0 if self.step < 0 else y + self.step < ny

    def comes(self, y, ny):
        return y - self.step < ny if self.step < 0 else y - self.step >= 0

    def wide(self, tile):
        return (tile - self.tiles[0]) * SUB

    def narrow(self, fold):
        return (len(self.tiles) + fold - self.folds[0]) * SUB


def routes_of(dims):
    rows = dims[3]
    strip = rows // 2
    routes = [
        Route(dims, 0, 0, 0, strip + SUB, HALO, 0),
        Route(dims, 0, 1, rows - HALO, HALO, 0, 1),
        Route(dims, 1, 0, strip - HALO, HALO + strip, 0, 0),
        Route(dims, 1, -1, 0, SUB, HALO + strip, 1),
    ]
    sent = 0
    for route in routes:
        route.sent = sent
        sent += route.size
    routes[1].base, routes[3].base = routes[0].size, routes[2].size
    return routes, sent, max(routes[0].size + routes[1].size, routes[2].size + routes[3].size)


MAIN, EDGE, BESIDE, COLS, ENDS, SLOTS = 0, 3, 6, 7, 11, 15
PARTS = 3
BELOW, RIGHT, ACROSS = range(3)


def exchange(
    dims, mine, here, p_ref, m_ref, cols_out, cols_in, ends_out, ends_in, sends, arrivals, ready
):
    ny, nx, bz, rows = dims
    z, y, x = here
    has_left, has_right = x > 0, x < nx - 1
    has_up, has_down = y > 0, y < ny - 1
    routes = routes_of(dims)[0]

    def remote(src, dst, arrival, who):
        return pltpu.make_async_remote_copy(
            src_ref=src,
            dst_ref=dst,
            send_sem=sends,
            recv_sem=arrivals.at[arrival],
            device_id=who,
            device_id_type=MESH,
        )

    def rows_of(brick, route, part):
        first = bz - PARTS + 1
        start = first + part - 1 if part else 0
        count = bz if part is None else 1 if part else first
        if part is not None and brick == 0:
            start = bz - start - count
        slot = BESIDE if part is None else (EDGE if route.half else MAIN) + part
        return remote(
            p_ref.at[pl.ds(start, count), route.rows],
            m_ref.at[pl.ds(1 + brick * bz + start, count), route.lands],
            slot, (route.side, y + route.step, x),
        )

    def cols_of(brick, route):
        return remote(
            cols_out.at[pl.ds(route.sent, route.size)],
            cols_in.at[brick, pl.ds(route.base, route.size)],
            COLS + 2 * brick + route.half,
            (route.side, y + route.step, x + 1),
        )

    def ends_of(brick, route):
        return remote(
            ends_out,
            ends_in.at[brick, route.half],
            ENDS + 2 * brick + route.half,
            (route.side, y + route.step, x - 1),
        )

    def rows_out(route, part=0):
        there = route.there(y, ny)
        if route.side != mine:
            return [(there, rows_of(mine, route, part))]
        return [(there, rows_of(mine, route, None))] if route.half else []

    def cols_sent(same):
        return [
            (jnp.logical_and(r.there(y, ny), has_right), cols_of(mine, r))
            for r in routes
            if (r.side == mine) == same
        ]

    def ends_sent():
        return [(jnp.logical_and(r.there(y, ny), has_left), ends_of(mine, r)) for r in routes]

    def apply(pairs, act):
        for there, copy in pairs:

            @pl.when(there)
            def _():
                act(copy)

    def start(pairs):
        apply(pairs, lambda copy: copy.start())

    def heard(kind, there, count):
        @pl.when(there)
        def _():
            pl.semaphore_wait(ready.at[kind], count)

    mains, own_halo, halos = (
        (routes[2], routes[1], routes[3]) if mine == 0 else (routes[0], routes[3], routes[1])
    )
    first, second = (halos, mains) if mine == 0 else (mains, halos)
    next_ones = [1 + there.astype(jnp.int32) for there in (has_down, has_up)]

    def send_first():
        if mine == 0:
            start(rows_out(halos))
            start(rows_out(mains))
        else:
            start(rows_out(mains))
            start(rows_out(own_halo))

    def send_rest():
        if mine == 0:
            start(ends_sent())
            heard(BELOW, has_down, 1)
            start(rows_out(own_halo))
        else:
            start(ends_sent())
        heard(RIGHT, has_right, next_ones[mine])
        start(cols_sent(True))
        if mine == 1:
            heard(BELOW, has_down, 1)
            start(rows_out(halos))
        start(rows_out(first, 1) + rows_out(second, 1))
        heard(ACROSS, has_right, next_ones[1 - mine])
        start(cols_sent(False))
        start(rows_out(first, 2) + rows_out(second, 2))

    def receive(brick, parts, sides):
        pairs = []
        for route in routes:
            if route.side != mine:
                continue
            comes = route.comes(y, ny)
            if brick != mine:
                pairs += [(comes, rows_of(brick, route, part)) for part in parts]
            elif route.half:
                pairs += [(comes, rows_of(brick, route, None))]
            if sides:
                pairs += [
                    (jnp.logical_and(comes, has_left), cols_of(brick, route)),
                    (jnp.logical_and(comes, has_right), ends_of(brick, route)),
                ]
        apply(pairs, lambda copy: copy.wait_recv())

    def close():
        for part in range(PARTS):
            apply(rows_out(mains, part) + rows_out(halos, part), lambda copy: copy.wait_send())
        apply(rows_out(own_halo), lambda copy: copy.wait_send())
        apply(ends_sent() + cols_sent(True) + cols_sent(False), lambda copy: copy.wait_send())

    return send_first, send_rest, receive, close


def partners_of(dims, here, over):
    ny, nx = dims[:2]
    z, y, x = here
    steps = [(z, over, 0), (1 - z, 0, 0)]
    diagonal = z == 1 if over > 0 else z == 0
    yield jnp.logical_and(diagonal, inside_of(dims, y + over, x)), (1 - z, y + over, x)
    steps += [
        (side, step, over)
        for side, step in ((z, -1), (z, 0), (z, 1), (1 - z, 0), (1 - z, 2 * z - 1))
    ]
    for side, step, across in steps:
        yield inside_of(dims, y + step, x + across), (side, y + step, x + across)


def inside_of(dims, y, x):
    ny, nx = dims[:2]
    return jnp.logical_and(
        jnp.logical_and(y >= 0, y < ny), jnp.logical_and(x >= 0, x < nx)
    )


def answers_of(dims, here):
    z, y, x = here
    own = z == 0
    yield jnp.logical_and(own, y > 0), (z, y - 1, x), BELOW
    yield jnp.logical_and(own, y > 0), (1 - z, y - 1, x), BELOW
    for side, kind in ((z, RIGHT), (1 - z, ACROSS)):
        for step in (0, 2 * z - 1):
            yield inside_of(dims, y + step, x - 1), (side, y + step, x - 1), kind


def render(
    dims, light_in, palette_in, rate_in, shear_in, offset_in, order_in, p_ref, out_ref,
    light, palette, rate, shear, offset, order, tile_ref, m_ref, own_ref, near_ref, cols_in, ends_in,
    cols_out, ends_out, h_ref, r_ref, dm, dh, back, sends, arrivals, ready, local_sems, table_sem,
):
    ny, nx, bz, rows = dims
    strip = rows // 2
    tall = HALO + strip + SUB
    depth = 2 * bz
    blocks = (HALO + strip) // SUB
    wide_lanes = HALO - SUB
    z, y, x = lax.axis_index("gz"), lax.axis_index("gy"), lax.axis_index("gx")
    routes = routes_of(dims)[0]

    tables = [
        pltpu.make_async_copy(source, target, table_sem)
        for source, target in (
            (light_in, light), (palette_in, palette), (rate_in, rate),
            (shear_in, shear), (offset_in, offset), (order_in, order),
        )
    ]
    barrier = pltpu.get_barrier_semaphore()

    def sided(act):
        for mine in range(2):

            @pl.when(z == mine)
            def _():
                act(mine)

    for there, who in partners_of(dims, (z, y, x), 1):

        @pl.when(there)
        def _():
            pl.semaphore_signal(barrier, inc=1, device_id=who, device_id_type=MESH)

    count = 0
    for there, _ in partners_of(dims, (z, y, x), -1):
        count = count + there.astype(jnp.int32)

    steps = [
        exchange(
            dims, mine, (z, y, x), p_ref, m_ref, cols_out, cols_in, ends_out, ends_in,
            sends, arrivals, ready,
        )
        for mine in range(2)
    ]

    def local_slab(mine):
        route = routes[2 * mine]
        return pltpu.make_async_copy(
            p_ref.at[:, route.rows], m_ref.at[pl.ds(1 + mine * bz, bz), route.lands],
            local_sems.at[1],
        )

    local_tile = pltpu.make_async_copy(p_ref, tile_ref, local_sems.at[0])
    local_tile.start()
    sided(lambda mine: local_slab(mine).start())
    for copy in tables:
        copy.start()

    @pl.when(count > 0)
    def _():
        pl.semaphore_wait(barrier, count)

    for there, who, kind in answers_of(dims, (z, y, x)):

        @pl.when(there)
        def _():
            pl.semaphore_signal(ready.at[kind], inc=1, device_id=who, device_id_type=MESH)


    sided(lambda mine: steps[mine][0]())

    empty = jnp.zeros((tall, LANES), jnp.float32)
    for ref in (m_ref, h_ref):
        ref[0] = empty
        ref[depth + 1] = empty

    def blank(mine):
        route = routes[2 * mine + 1]

        @pl.when(jnp.logical_not(route.comes(y, ny)))
        def _():
            m_ref[:, route.slab] = jnp.zeros((depth + 2, len(route.tiles) * SUB, LANES), jnp.float32)
            cols_in[:, route.base : route.base + route.size] = jnp.zeros(
                (2, route.size, LANES), jnp.float32
            )
            ends_in[:, 1] = jnp.zeros((2, SUB, LANES), jnp.float32)

    sided(blank)

    @pl.when(x == 0)
    def _():
        cols_in[...] = jnp.zeros(cols_in.shape, jnp.float32)

    @pl.when(x == nx - 1)
    def _():
        ends_in[...] = jnp.zeros(ends_in.shape, jnp.float32)

    lane = lax.broadcasted_iota(jnp.int32, (SUB, LANES), 1)
    last = lane == LANES - 1
    first = lane == 0
    groups = routes[0].groups
    tiles = rows // SUB

    def cell(j, t):
        return tile_ref[j, t * SUB : (t + 1) * SUB]

    def put(t_or_fold, is_wide, value):
        for route in routes:
            if t_or_fold in (route.tiles if is_wide else route.folds):
                at = route.sent + (route.wide if is_wide else route.narrow)(t_or_fold)
                cols_out[at : at + SUB] = value

    def merged(pieces):
        while len(pieces) > 1:
            pieces = [
                (a[0], jnp.where(lane >= b[0], b[1], a[1]))
                for a, b in zip(pieces[::2], pieces[1::2])
            ] + (pieces[-1:] if len(pieces) % 2 else [])
        return pieces[0][1]

    def turned(value, by):
        return pltpu.roll(value, by % LANES, 1) if by % LANES else value

    local_tile.wait()
    for t in range(tiles):
        put(
            t, True,
            merged(
                [(wide_lanes * j, turned(cell(j, t), wide_lanes * (j + 1))) for j in range(bz)]
            ),
        )
    for fold in range(tiles // groups):
        put(
            fold, False,
            merged(
                [
                    (
                        SUB * (bz * g + j),
                        turned(cell(j, fold * groups + g), SUB * (bz * g + j) + HALO),
                    )
                    for g in range(groups)
                    for j in range(bz)
                ]
            ),
        )
    ends_out[...] = merged(
        [(t * bz + j, turned(cell(j, t), t * bz + j)) for t in range(tiles) for j in range(bz)]
    )

    def unpack(mine, brick):
        for route in routes[2 * mine : 2 * mine + 2]:
            for t in route.tiles:
                row = (route.first + t - route.tiles[0]) * SUB
                at = route.base + route.wide(t)
                wide = cols_in[brick, at : at + SUB]
                at = route.base + route.narrow(t // groups)
                narrow = cols_in[brick, at : at + SUB]
                for j in range(bz):
                    h_ref[1 + brick * bz + j, row : row + SUB] = jnp.where(
                        lane >= LANES - wide_lanes,
                        turned(wide, -wide_lanes * (j + 1)),
                        turned(narrow, -SUB * (bz * (t % groups) + j) - HALO),
                    )
                r_ref[brick, row : row + SUB] = turned(
                    ends_in[brick, route.half], LANES - 1 - t * bz
                )

    def opening(mine):
        _, send_rest, receive, _ = steps[mine]
        send_rest()
        local_slab(mine).wait()
        receive(mine, (), True)
        own_ref[...] = m_ref[1 + mine * bz : 1 + (mine + 1) * bz]
        unpack(mine, mine)

    def middle(mine):
        receive = steps[mine][2]
        receive(1 - mine, (0,), True)
        near_ref[...] = m_ref[(bz if mine == 0 else 2) + 1 : (depth - 2 if mine == 0 else bz) + 1]
        unpack(mine, 1 - mine)

    def ending(mine, part):
        receive = steps[mine][2]
        receive(1 - mine, (part,), False)

    sided(opening)
    for copy in tables:
        copy.wait()

    towards = []
    for w in range(VIEWS):
        a, b, c = light[w, 0], light[w, 1], light[w, 2]
        inverse = lax.rsqrt(jnp.full((SUB, LANES), a * a + b * b + c * c + 1.0, jnp.float32))
        towards.append((a * inverse, b * inverse, c * inverse))

    def slopes(k, carry):
        for i in range(blocks):
            top = i * SUB
            here = m_ref[k + 1, top + 1 : top + 1 + SUB]
            side = h_ref[k + 1, top + 1 : top + 1 + SUB]
            beyond = pltpu.roll(
                r_ref[k // bz, top + 1 : top + 1 + SUB], (LANES - k % bz) % LANES, 1
            )
            here_r, here_l = pltpu.roll(here, LANES - 1, 1), pltpu.roll(here, 1, 1)
            side_r, side_l = pltpu.roll(side, LANES - 1, 1), pltpu.roll(side, 1, 1)
            for ref, cols, dots in (
                (m_ref, jnp.where(last, beyond, here_r) - jnp.where(first, side_l, here_l), dm),
                (h_ref, jnp.where(last, here_r, side_r) - side_l, dh),
            ):
                deep = ref[k + 2, top + 1 : top + 1 + SUB] - ref[k, top + 1 : top + 1 + SUB]
                down = ref[k + 1, top + 2 : top + 2 + SUB] - ref[k + 1, top : top + SUB]
                half = lax.rsqrt(deep * deep + down * down + cols * cols + 4.0)
                deep, down, cols = deep * half, down * half, cols * half
                for w in range(VIEWS):
                    a, b, c = towards[w]
                    dots[w, k, top : top + SUB] = deep * a + down * b + cols * c
        return carry

    tile = 32
    per_view = strip // tile
    base_row = y * rows + z * strip
    base_col = x * LANES
    lanes = lax.broadcasted_iota(jnp.int32, (tile, LANES), 1)
    rows_at = lax.broadcasted_iota(jnp.int32, (tile, LANES), 0)
    bias = [0.5 * palette[0, c] for c in range(3)]
    gain = [0.5 * palette[1, c] for c in range(3)]

    def march(w, top, brick, first_k, count, cells, start, colors, through):
        ambient = jnp.zeros((tile, LANES), jnp.float32)
        rate2 = rate[w] * (-math.log2(math.e))
        off_r, off_c = offset[brick, 0, w], offset[brick, 1, w]
        inside = jnp.logical_and(rows_at >= off_r - base_row - top, lanes >= off_c - base_col)
        fall = jnp.where(inside, rate2, 0.0)
        for j in range(count):
            k = first_k + j
            sr = off_r + shear[w, 0, k]
            sc = off_c + shear[w, 1, k]
            at = HALO + top - sr
            wrap = lanes >= LANES - sc
            value = jnp.where(wrap, h_ref[k + 1, pl.ds(at, tile)], cells[start + j, pl.ds(at, tile)])
            dot = jnp.where(wrap, dh[w, k, pl.ds(at - 1, tile)], dm[w, k, pl.ds(at - 1, tile)])
            value = pltpu.roll(value, sc, 1)
            dot = pltpu.roll(dot, sc, 1)
            kept = jnp.exp2(fall * (1.0 + jnp.tanh(value)))
            weight = (0.125 + 0.375 * dot * dot) * ((1.0 - kept) * through)
            through = through * kept
            ambient = ambient + weight
            colors = [
                colors[c] + weight * jnp.tanh(bias[c] + gain[c] * value) for c in range(3)
            ]
        return [color + ambient for color in colors], through

    def views(act):
        def one(step, carry):
            act(step // per_view, (step % per_view) * tile)
            return carry

        lax.fori_loop(0, VIEWS * per_view, one, 0, unroll=VIEWS * per_view)

    zero = jnp.zeros((tile, LANES), jnp.float32)
    early = bz - 2
    near, far = bz - early * z, (depth - 2) * (1 - z)

    def own_layer(w, top):
        at = pl.ds(top, tile)
        colors, through = march(
            w, top, z, z * (bz + 1), bz - 1, own_ref, z, [zero] * 3, zero + 1.0
        )
        for c in range(3):
            back[w, c, at] = colors[c]
        back[w, 3, at] = through

    def near_layer(w, top):
        at = pl.ds(top, tile)
        colors, through = march(
            w, top, 1 - z, near, early, near_ref, 0, [zero] * 3, zero + 1.0
        )
        own_first, near_first = order[0, w] == z, z == 0
        edge_colors, edge_through = march(
            w, top, z, bz - 1 + z, 1, own_ref, (1 - z) * (bz - 1), [zero] * 3, zero + 1.0
        )
        inner_through = back[w, 3, at]
        own_through = inner_through * edge_through
        of_inner = jnp.where(near_first, 1.0, edge_through)
        of_edge = jnp.where(near_first, inner_through, 1.0)
        ahead = jnp.where(own_first, own_through, 1.0)
        after = jnp.where(near_first, 1.0, through)
        for c in range(3):
            own_color = of_inner * back[w, c, at] + of_edge * edge_colors[c]
            out_ref[w, c, at] = jnp.where(own_first, own_color, 0.0) + jnp.where(
                near_first, ahead * colors[c], 0.0
            )
            back[w, c, at] = jnp.where(near_first, 0.0, colors[c]) + jnp.where(
                own_first, 0.0, after * own_color
            )
        out_ref[w, 3, at] = ahead * jnp.where(near_first, through, 1.0)
        back[w, 3, at] = after * jnp.where(own_first, 1.0, own_through)

    def far_layer(w, top):
        at = pl.ds(top, tile)
        colors, through = march(
            w, top, 1 - z, far, 2, m_ref, 1 + far, [out_ref[w, c, at] for c in range(3)],
            out_ref[w, 3, at],
        )
        for c in range(3):
            out_ref[w, c, at] = colors[c] + through * back[w, c, at]
        out_ref[w, 3, at] = 1.0 - through * back[w, 3, at]

    def each(start, stop):
        lax.fori_loop(start, stop, slopes, 0)

    each(z * (bz + 1), z * (bz + 1) + bz - 1)
    views(own_layer)
    sided(middle)
    for k in range(2):
        slopes(bz - 1 + k, 0)
    sided(lambda mine: ending(mine, 1))
    slopes(bz + 1 - 3 * z, 0)
    views(near_layer)
    sided(lambda mine: ending(mine, 2))
    for k in range(2):
        slopes((1 - z) * (depth - 2) + k, 0)
    views(far_layer)
    sided(lambda mine: steps[mine][3]())


def two_bricks(mesh, pressure, light, palette, rate, shear, offset, order):
    bz, rows, cols = pressure.shape
    dims = (mesh.shape["gy"], mesh.shape["gx"], bz, rows)
    strip = rows // 2
    tall = HALO + strip + SUB
    depth = 2 * bz
    vmem = pl.BlockSpec(memory_space=pltpu.VMEM)
    hbm = pl.BlockSpec(memory_space=pltpu.HBM)
    f32 = jnp.float32
    _, sent, got = routes_of(dims)
    tables = (
        light,
        palette.T,
        rate,
        jnp.transpose(shear, (0, 2, 1)),
        jnp.transpose(offset, (1, 2, 0)),
        order.T,
    )
    image = pl.pallas_call(
        functools.partial(render, dims),
        out_shape=jax.ShapeDtypeStruct((VIEWS, 4, strip, LANES), f32),
        in_specs=[hbm] * 7,
        out_specs=vmem,
        scratch_shapes=[
            *[pltpu.SMEM(table.shape, table.dtype) for table in tables],
            pltpu.VMEM((bz, rows, LANES), f32),
            pltpu.VMEM((depth + 2, tall, LANES), f32),
            pltpu.VMEM((bz, tall, LANES), f32),
            pltpu.VMEM((bz - 2, tall, LANES), f32),
            pltpu.VMEM((2, got, LANES), f32),
            pltpu.VMEM((2, 2, SUB, LANES), f32),
            pltpu.VMEM((sent, LANES), f32),
            pltpu.VMEM((SUB, LANES), f32),
            pltpu.VMEM((depth + 2, tall, LANES), f32),
            pltpu.VMEM((2, tall, LANES), f32),
            pltpu.VMEM((VIEWS, depth, HALO + strip, LANES), f32),
            pltpu.VMEM((VIEWS, depth, HALO + strip, LANES), f32),
            pltpu.VMEM((VIEWS, 4, strip, LANES), f32),
            pltpu.SemaphoreType.DMA,
            pltpu.SemaphoreType.DMA((SLOTS,)),
            pltpu.SemaphoreType.REGULAR((3,)),
            pltpu.SemaphoreType.DMA((2,)),
            pltpu.SemaphoreType.DMA,
        ],
        compiler_params=pltpu.CompilerParams(collective_id=0, has_side_effects=True, vmem_limit_bytes=12 << 20),
        name="render",
    )(
        *[pltpu.with_memory_space_constraint(t, pltpu.HBM) for t in (*tables, pressure)]
    )
    return image[:, :, None]


def fits(mesh, shape):
    bz, rows, cols = shape
    return (
        mesh.shape["gz"] == 2
        and cols == LANES
        and rows % 64 == 0
        and 2 * HALO <= rows <= LANES
        and bz * (HALO - SUB) == LANES
        and bz * (rows // SUB) <= LANES
    )


def on_device(mesh, pressure, *rest):
    if fits(mesh, pressure.shape):
        return two_bricks(mesh, pressure, *rest)
    return many_bricks(pressure, *rest)


def solution(mesh):
    return jax.shard_map(
        functools.partial(on_device, mesh),
        mesh=mesh,
        in_specs=(P("gz", "gy", "gx"), P(), P(), P(), P(), P(), P()),
        out_specs=P(None, None, "gz", "gy", "gx"),
        check_vma=False,
    )
```

```python
import functools
import math

import jax
import jax.numpy as jnp
from jax import lax
from jax.experimental import pallas as pl
from jax.experimental.pallas import tpu as pltpu
from jax.sharding import PartitionSpec as P

VIEWS = 4
SHEAR = 8
REACH = 32
HALO = SHEAR + REACH
SUB = 8
LANES = 128
MESH = pl.DeviceIdType.MESH


def padded(cells, sides, width):
    for axis, dim in sides:
        count = lax.axis_size(axis)
        ends = count - 1
        head = lax.slice_in_dim(cells, 0, width, axis=dim)
        tail = lax.slice_in_dim(cells, cells.shape[dim] - width, cells.shape[dim], axis=dim)
        cells = jnp.concatenate(
            [
                lax.ppermute(tail, axis, [(i, (i + 1) % count) for i in range(ends)]),
                cells,
                lax.ppermute(head, axis, [((i + 1) % count, i) for i in range(ends)]),
            ],
            axis=dim,
        )
    return cells


def shifted(value, axis, steps):
    count = lax.axis_size(axis)
    first, last = (max(0, -steps), min(count, count - steps))
    return lax.ppermute(value, axis, [(source, source + steps) for source in range(first, last)])


def surface_terms(slab):
    inner = slab[1:-1, 1:-1, 1:-1]
    grad_depth = 0.5 * (slab[2:, 1:-1, 1:-1] - slab[:-2, 1:-1, 1:-1])
    grad_rows = 0.5 * (slab[1:-1, 2:, 1:-1] - slab[1:-1, :-2, 1:-1])
    grad_cols = 0.5 * (slab[1:-1, 1:-1, 2:] - slab[1:-1, 1:-1, :-2])
    factor = lax.rsqrt(
        grad_depth * grad_depth + grad_rows * grad_rows + grad_cols * grad_cols + 1.0
    )
    return (inner, (grad_depth * factor, grad_rows * factor, grad_cols * factor))


def render_layers(inner, normals, shifts, light, palette, rate, rows, cols):
    lengths = jnp.sqrt(jnp.sum(light * light, axis=1, keepdims=True) + 1.0)
    towards = light / lengths
    offsets = palette[:, 0][:, None, None]
    slopes = palette[:, 1][:, None, None]
    layers = []
    for view in range(light.shape[0]):

        def advance(carry, items):
            color, depth = carry
            value_slab, normal_depth, normal_rows, normal_cols, moved = items
            start = (SHEAR - moved[0], SHEAR - moved[1])
            value = lax.dynamic_slice(value_slab, start, (rows, cols))
            dot = (
                lax.dynamic_slice(normal_depth, start, (rows, cols)) * towards[view, 0]
                + lax.dynamic_slice(normal_rows, start, (rows, cols)) * towards[view, 1]
                + lax.dynamic_slice(normal_cols, start, (rows, cols)) * towards[view, 2]
            )
            shade = 0.25 + 0.75 * dot * dot
            density = rate[view] * (1.0 + jnp.tanh(value))
            alpha = 1.0 - jnp.exp(-density)
            weight = alpha * jnp.exp(-depth)
            hues = jax.nn.sigmoid(offsets + slopes * value[None]) * shade[None]
            return ((color + hues * weight[None], depth + density), None)

        start_carry = (
            jnp.zeros((3, rows, cols), jnp.float32),
            jnp.zeros((rows, cols), jnp.float32),
        )
        (color, depth), _ = lax.scan(
            advance, start_carry, (inner, normals[0], normals[1], normals[2], shifts[view])
        )
        layers.append(jnp.concatenate([color, depth[None]], axis=0))
    return jnp.stack(layers)


def precedence(order):
    bricks = order.shape[1]
    onehot = (order[:, :, None] == jnp.arange(bricks, dtype=jnp.int32)[None, None, :]).astype(
        jnp.float32
    )
    ranks = jnp.sum(onehot * jnp.arange(bricks, dtype=jnp.float32)[None, :, None], axis=1)
    return (ranks[:, None, :] < ranks[:, :, None]).astype(jnp.float32)


def many_bricks(pressure, light, palette, rate, shear, offset, order):
    depth_cells, rows, cols = pressure.shape
    brick = lax.axis_index("gz")
    zero = jnp.zeros((), jnp.int32)
    widened = padded(pressure, (("gy", 1), ("gx", 2)), SHEAR + 1)
    slab = padded(widened, (("gz", 0),), 1)
    inner, normals = surface_terms(slab)
    shifts = lax.dynamic_slice(shear, (zero, brick * depth_cells, zero), (VIEWS, depth_cells, 2))
    layers = render_layers(inner, normals, shifts, light, palette, rate, rows, cols)
    moved = lax.dynamic_index_in_dim(offset, brick, 1, keepdims=False)
    blank = jnp.zeros((4, rows + REACH, cols + REACH), jnp.float32)
    canvas = jnp.stack(
        [
            lax.dynamic_update_slice(blank, layers[view], (zero, moved[view, 0], moved[view, 1]))
            for view in range(VIEWS)
        ]
    )
    own_tile = canvas[:, :, :rows, :cols]
    from_above = shifted(canvas[:, :, rows:, :cols], "gy", 1)
    from_left = shifted(canvas[:, :, :rows, cols:], "gx", 1)
    from_diagonal = shifted(canvas[:, :, rows:, cols:], ("gy", "gx"), lax.axis_size("gx") + 1)
    from_diagonal = from_diagonal * (lax.axis_index("gx") > 0).astype(jnp.float32)
    own_tile = own_tile.at[:, :, :REACH, :].add(from_above)
    own_tile = own_tile.at[:, :, :, :REACH].add(from_left)
    own_tile = own_tile.at[:, :, :REACH, :REACH].add(from_diagonal)
    ranking = precedence(order)
    pieces = lax.all_to_all(own_tile[None], "gz", split_axis=3, concat_axis=0, tiled=True)
    depths = pieces[:, :, 3]
    cover = jnp.einsum("vbc,cvyx->bvyx", ranking, depths, precision=lax.Precision.HIGHEST)
    colors = jnp.sum(pieces[:, :, :3] * jnp.exp(-cover)[:, :, None], axis=0)
    opacity = 1.0 - jnp.exp(-jnp.sum(depths, axis=0))
    image = jnp.concatenate([colors, opacity[:, None]], axis=1)
    return image[:, :, None]


class Route:
    def __init__(self, dims, side, step, start, count, slab, half):
        bz = dims[2]
        self.side, self.step, self.half = side, step, half
        self.slab = pl.ds(slab, count)
        needed = count - SUB + 1 if start == 0 else count
        self.rows, self.lands = pl.ds(start, needed), pl.ds(slab, needed)
        self.groups = LANES // (SUB * bz)
        self.tiles = range(start // SUB, (start + count) // SUB)
        self.first = slab // SUB
        self.folds = range(
            self.tiles[0] // self.groups, self.tiles[-1] // self.groups + 1
        )
        self.size = (len(self.tiles) + len(self.folds)) * SUB
        self.base = self.sent = 0

    def there(self, y, ny):
        return y + self.step >= 0 if self.step < 0 else y + self.step < ny

    def comes(self, y, ny):
        return y - self.step < ny if self.step < 0 else y - self.step >= 0

    def wide(self, tile):
        return (tile - self.tiles[0]) * SUB

    def narrow(self, fold):
        return (len(self.tiles) + fold - self.folds[0]) * SUB


def routes_of(dims):
    rows = dims[3]
    strip = rows // 2
    routes = [
        Route(dims, 0, 0, 0, strip + SUB, HALO, 0),
        Route(dims, 0, 1, rows - HALO, HALO, 0, 1),
        Route(dims, 1, 0, strip - HALO, HALO + strip, 0, 0),
        Route(dims, 1, -1, 0, SUB, HALO + strip, 1),
    ]
    sent = 0
    for route in routes:
        route.sent = sent
        sent += route.size
    routes[1].base, routes[3].base = routes[0].size, routes[2].size
    return routes, sent, max(routes[0].size + routes[1].size, routes[2].size + routes[3].size)


MAIN, EDGE, BESIDE, COLS, ENDS, SLOTS = 0, 3, 6, 7, 11, 15
PARTS = 3
BELOW, RIGHT, ACROSS = range(3)


def exchange(
    dims, mine, here, p_ref, m_ref, cols_out, cols_in, ends_out, ends_in, sends, arrivals, ready
):
    ny, nx, bz, rows = dims
    z, y, x = here
    has_left, has_right = x > 0, x < nx - 1
    has_up, has_down = y > 0, y < ny - 1
    routes = routes_of(dims)[0]

    def remote(src, dst, arrival, who):
        return pltpu.make_async_remote_copy(
            src_ref=src,
            dst_ref=dst,
            send_sem=sends,
            recv_sem=arrivals.at[arrival],
            device_id=who,
            device_id_type=MESH,
        )

    def rows_of(brick, route, part):
        first = bz - PARTS + 1
        start = first + part - 1 if part else 0
        count = bz if part is None else 1 if part else first
        if part is not None and brick == 0:
            start = bz - start - count
        slot = BESIDE if part is None else (EDGE if route.half else MAIN) + part
        return remote(
            p_ref.at[pl.ds(start, count), route.rows],
            m_ref.at[pl.ds(1 + brick * bz + start, count), route.lands],
            slot, (route.side, y + route.step, x),
        )

    def cols_of(brick, route):
        return remote(
            cols_out.at[pl.ds(route.sent, route.size)],
            cols_in.at[brick, pl.ds(route.base, route.size)],
            COLS + 2 * brick + route.half,
            (route.side, y + route.step, x + 1),
        )

    def ends_of(brick, route):
        return remote(
            ends_out,
            ends_in.at[brick, route.half],
            ENDS + 2 * brick + route.half,
            (route.side, y + route.step, x - 1),
        )

    def rows_out(route, part=0):
        there = route.there(y, ny)
        if route.side != mine:
            return [(there, rows_of(mine, route, part))]
        return [(there, rows_of(mine, route, None))] if route.half else []

    def cols_sent(same):
        return [
            (jnp.logical_and(r.there(y, ny), has_right), cols_of(mine, r))
            for r in routes
            if (r.side == mine) == same
        ]

    def ends_sent():
        return [(jnp.logical_and(r.there(y, ny), has_left), ends_of(mine, r)) for r in routes]

    def apply(pairs, act):
        for there, copy in pairs:

            @pl.when(there)
            def _():
                act(copy)

    def start(pairs):
        apply(pairs, lambda copy: copy.start())

    def heard(kind, there, count):
        @pl.when(there)
        def _():
            pl.semaphore_wait(ready.at[kind], count)

    mains, own_halo, halos = (
        (routes[2], routes[1], routes[3]) if mine == 0 else (routes[0], routes[3], routes[1])
    )
    first, second = (halos, mains) if mine == 0 else (mains, halos)
    next_ones = [1 + there.astype(jnp.int32) for there in (has_down, has_up)]

    def send_first():
        if mine == 0:
            start(rows_out(halos))
            start(rows_out(mains))
        else:
            start(rows_out(mains))
            start(rows_out(own_halo))

    def send_rest():
        if mine == 0:
            start(ends_sent())
            heard(BELOW, has_down, 1)
            start(rows_out(own_halo))
        else:
            start(ends_sent())
        heard(RIGHT, has_right, next_ones[mine])
        start(cols_sent(True))
        if mine == 1:
            heard(BELOW, has_down, 1)
            start(rows_out(halos))
        start(rows_out(first, 1) + rows_out(second, 1))
        heard(ACROSS, has_right, next_ones[1 - mine])
        start(cols_sent(False))
        start(rows_out(halos, 2) + rows_out(mains, 2))

    def receive(brick, parts, sides):
        pairs = []
        for route in routes:
            if route.side != mine:
                continue
            comes = route.comes(y, ny)
            if brick != mine:
                pairs += [(comes, rows_of(brick, route, part)) for part in parts]
            elif route.half:
                pairs += [(comes, rows_of(brick, route, None))]
            if sides:
                pairs += [
                    (jnp.logical_and(comes, has_left), cols_of(brick, route)),
                    (jnp.logical_and(comes, has_right), ends_of(brick, route)),
                ]
        apply(pairs, lambda copy: copy.wait_recv())

    def close():
        for part in range(PARTS):
            apply(rows_out(mains, part) + rows_out(halos, part), lambda copy: copy.wait_send())
        apply(rows_out(own_halo), lambda copy: copy.wait_send())
        apply(ends_sent() + cols_sent(True) + cols_sent(False), lambda copy: copy.wait_send())

    return send_first, send_rest, receive, close


def partners_of(dims, here, over):
    ny, nx = dims[:2]
    z, y, x = here
    steps = [(z, over, 0), (1 - z, 0, 0)]
    diagonal = z == 1 if over > 0 else z == 0
    yield jnp.logical_and(diagonal, inside_of(dims, y + over, x)), (1 - z, y + over, x)
    steps += [
        (side, step, over)
        for side, step in ((z, -1), (z, 0), (z, 1), (1 - z, 0), (1 - z, 2 * z - 1))
    ]
    for side, step, across in steps:
        yield inside_of(dims, y + step, x + across), (side, y + step, x + across)


def inside_of(dims, y, x):
    ny, nx = dims[:2]
    return jnp.logical_and(
        jnp.logical_and(y >= 0, y < ny), jnp.logical_and(x >= 0, x < nx)
    )


def answers_of(dims, here):
    z, y, x = here
    own = z == 0
    yield jnp.logical_and(own, y > 0), (z, y - 1, x), BELOW
    yield jnp.logical_and(own, y > 0), (1 - z, y - 1, x), BELOW
    for side, kind in ((z, RIGHT), (1 - z, ACROSS)):
        for step in (0, 2 * z - 1):
            yield inside_of(dims, y + step, x - 1), (side, y + step, x - 1), kind


def render(
    dims, light_in, palette_in, rate_in, shear_in, offset_in, order_in, p_ref, out_ref,
    light, palette, rate, shear, offset, order, tile_ref, m_ref, own_ref, near_ref, cols_in, ends_in,
    cols_out, ends_out, h_ref, r_ref, dm, dh, back, sends, arrivals, ready, local_sems, table_sem,
):
    ny, nx, bz, rows = dims
    strip = rows // 2
    tall = HALO + strip + SUB
    depth = 2 * bz
    blocks = (HALO + strip) // SUB
    wide_lanes = HALO - SUB
    z, y, x = lax.axis_index("gz"), lax.axis_index("gy"), lax.axis_index("gx")
    routes = routes_of(dims)[0]

    tables = [
        pltpu.make_async_copy(source, target, table_sem)
        for source, target in (
            (light_in, light), (palette_in, palette), (rate_in, rate),
            (shear_in, shear), (offset_in, offset), (order_in, order),
        )
    ]
    barrier = pltpu.get_barrier_semaphore()

    def sided(act):
        for mine in range(2):

            @pl.when(z == mine)
            def _():
                act(mine)

    for there, who in partners_of(dims, (z, y, x), 1):

        @pl.when(there)
        def _():
            pl.semaphore_signal(barrier, inc=1, device_id=who, device_id_type=MESH)

    count = 0
    for there, _ in partners_of(dims, (z, y, x), -1):
        count = count + there.astype(jnp.int32)

    steps = [
        exchange(
            dims, mine, (z, y, x), p_ref, m_ref, cols_out, cols_in, ends_out, ends_in,
            sends, arrivals, ready,
        )
        for mine in range(2)
    ]

    def local_slab(mine):
        route = routes[2 * mine]
        return pltpu.make_async_copy(
            p_ref.at[:, route.rows], m_ref.at[pl.ds(1 + mine * bz, bz), route.lands],
            local_sems.at[1],
        )

    local_tile = pltpu.make_async_copy(p_ref, tile_ref, local_sems.at[0])
    local_tile.start()
    sided(lambda mine: local_slab(mine).start())
    for copy in tables:
        copy.start()

    @pl.when(count > 0)
    def _():
        pl.semaphore_wait(barrier, count)

    for there, who, kind in answers_of(dims, (z, y, x)):

        @pl.when(there)
        def _():
            pl.semaphore_signal(ready.at[kind], inc=1, device_id=who, device_id_type=MESH)


    sided(lambda mine: steps[mine][0]())

    empty = jnp.zeros((tall, LANES), jnp.float32)
    for ref in (m_ref, h_ref):
        ref[0] = empty
        ref[depth + 1] = empty

    def blank(mine):
        route = routes[2 * mine + 1]

        @pl.when(jnp.logical_not(route.comes(y, ny)))
        def _():
            m_ref[:, route.slab] = jnp.zeros((depth + 2, len(route.tiles) * SUB, LANES), jnp.float32)
            cols_in[:, route.base : route.base + route.size] = jnp.zeros(
                (2, route.size, LANES), jnp.float32
            )
            ends_in[:, 1] = jnp.zeros((2, SUB, LANES), jnp.float32)

    sided(blank)

    @pl.when(x == 0)
    def _():
        cols_in[...] = jnp.zeros(cols_in.shape, jnp.float32)

    @pl.when(x == nx - 1)
    def _():
        ends_in[...] = jnp.zeros(ends_in.shape, jnp.float32)

    lane = lax.broadcasted_iota(jnp.int32, (SUB, LANES), 1)
    last = lane == LANES - 1
    first = lane == 0
    groups = routes[0].groups
    tiles = rows // SUB

    def cell(j, t):
        return tile_ref[j, t * SUB : (t + 1) * SUB]

    def put(t_or_fold, is_wide, value):
        for route in routes:
            if t_or_fold in (route.tiles if is_wide else route.folds):
                at = route.sent + (route.wide if is_wide else route.narrow)(t_or_fold)
                cols_out[at : at + SUB] = value

    def merged(pieces):
        while len(pieces) > 1:
            pieces = [
                (a[0], jnp.where(lane >= b[0], b[1], a[1]))
                for a, b in zip(pieces[::2], pieces[1::2])
            ] + (pieces[-1:] if len(pieces) % 2 else [])
        return pieces[0][1]

    def turned(value, by):
        return pltpu.roll(value, by % LANES, 1) if by % LANES else value

    local_tile.wait()
    for t in range(tiles):
        put(
            t, True,
            merged(
                [(wide_lanes * j, turned(cell(j, t), wide_lanes * (j + 1))) for j in range(bz)]
            ),
        )
    for fold in range(tiles // groups):
        put(
            fold, False,
            merged(
                [
                    (
                        SUB * (bz * g + j),
                        turned(cell(j, fold * groups + g), SUB * (bz * g + j) + HALO),
                    )
                    for g in range(groups)
                    for j in range(bz)
                ]
            ),
        )
    ends_out[...] = merged(
        [(t * bz + j, turned(cell(j, t), t * bz + j)) for t in range(tiles) for j in range(bz)]
    )

    def unpack(mine, brick):
        for route in routes[2 * mine : 2 * mine + 2]:
            for t in route.tiles:
                row = (route.first + t - route.tiles[0]) * SUB
                at = route.base + route.wide(t)
                wide = cols_in[brick, at : at + SUB]
                at = route.base + route.narrow(t // groups)
                narrow = cols_in[brick, at : at + SUB]
                for j in range(bz):
                    h_ref[1 + brick * bz + j, row : row + SUB] = jnp.where(
                        lane >= LANES - wide_lanes,
                        turned(wide, -wide_lanes * (j + 1)),
                        turned(narrow, -SUB * (bz * (t % groups) + j) - HALO),
                    )
                r_ref[brick, row : row + SUB] = turned(
                    ends_in[brick, route.half], LANES - 1 - t * bz
                )

    def opening(mine):
        _, send_rest, receive, _ = steps[mine]
        send_rest()
        local_slab(mine).wait()
        receive(mine, (), True)
        own_ref[...] = m_ref[1 + mine * bz : 1 + (mine + 1) * bz]
        unpack(mine, mine)

    def middle(mine):
        receive = steps[mine][2]
        receive(1 - mine, (0,), True)
        near_ref[...] = m_ref[(bz if mine == 0 else 2) + 1 : (depth - 2 if mine == 0 else bz) + 1]
        unpack(mine, 1 - mine)

    def ending(mine, part):
        receive = steps[mine][2]
        receive(1 - mine, (part,), False)

    sided(opening)
    for copy in tables:
        copy.wait()

    towards = []
    for w in range(VIEWS):
        a, b, c = light[w, 0], light[w, 1], light[w, 2]
        inverse = lax.rsqrt(jnp.full((SUB, LANES), a * a + b * b + c * c + 1.0, jnp.float32))
        towards.append((a * inverse, b * inverse, c * inverse))

    def slopes(k, carry):
        for i in range(blocks):
            top = i * SUB
            here = m_ref[k + 1, top + 1 : top + 1 + SUB]
            side = h_ref[k + 1, top + 1 : top + 1 + SUB]
            beyond = pltpu.roll(
                r_ref[k // bz, top + 1 : top + 1 + SUB], (LANES - k % bz) % LANES, 1
            )
            here_r, here_l = pltpu.roll(here, LANES - 1, 1), pltpu.roll(here, 1, 1)
            side_r, side_l = pltpu.roll(side, LANES - 1, 1), pltpu.roll(side, 1, 1)
            for ref, cols, dots in (
                (m_ref, jnp.where(last, beyond, here_r) - jnp.where(first, side_l, here_l), dm),
                (h_ref, jnp.where(last, here_r, side_r) - side_l, dh),
            ):
                deep = ref[k + 2, top + 1 : top + 1 + SUB] - ref[k, top + 1 : top + 1 + SUB]
                down = ref[k + 1, top + 2 : top + 2 + SUB] - ref[k + 1, top : top + SUB]
                half = lax.rsqrt(deep * deep + down * down + cols * cols + 4.0)
                deep, down, cols = deep * half, down * half, cols * half
                for w in range(VIEWS):
                    a, b, c = towards[w]
                    dots[w, k, top : top + SUB] = deep * a + down * b + cols * c
        return carry

    tile = 32
    per_view = strip // tile
    base_row = y * rows + z * strip
    base_col = x * LANES
    lanes = lax.broadcasted_iota(jnp.int32, (tile, LANES), 1)
    rows_at = lax.broadcasted_iota(jnp.int32, (tile, LANES), 0)
    bias = [0.5 * palette[0, c] for c in range(3)]
    gain = [0.5 * palette[1, c] for c in range(3)]

    def march(w, top, brick, first_k, count, cells, start, colors, through):
        ambient = jnp.zeros((tile, LANES), jnp.float32)
        rate2 = rate[w] * (-math.log2(math.e))
        off_r, off_c = offset[brick, 0, w], offset[brick, 1, w]
        inside = jnp.logical_and(rows_at >= off_r - base_row - top, lanes >= off_c - base_col)
        fall = jnp.where(inside, rate2, 0.0)
        for j in range(count):
            k = first_k + j
            sr = off_r + shear[w, 0, k]
            sc = off_c + shear[w, 1, k]
            at = HALO + top - sr
            wrap = lanes >= LANES - sc
            value = jnp.where(wrap, h_ref[k + 1, pl.ds(at, tile)], cells[start + j, pl.ds(at, tile)])
            dot = jnp.where(wrap, dh[w, k, pl.ds(at - 1, tile)], dm[w, k, pl.ds(at - 1, tile)])
            value = pltpu.roll(value, sc, 1)
            dot = pltpu.roll(dot, sc, 1)
            kept = jnp.exp2(fall * (1.0 + jnp.tanh(value)))
            weight = (0.125 + 0.375 * dot * dot) * ((1.0 - kept) * through)
            through = through * kept
            ambient = ambient + weight
            colors = [
                colors[c] + weight * jnp.tanh(bias[c] + gain[c] * value) for c in range(3)
            ]
        return [color + ambient for color in colors], through

    def views(act):
        def one(step, carry):
            act(step // per_view, (step % per_view) * tile)
            return carry

        lax.fori_loop(0, VIEWS * per_view, one, 0, unroll=VIEWS * per_view)

    zero = jnp.zeros((tile, LANES), jnp.float32)
    early = bz - 2
    near, far = bz - early * z, (depth - 2) * (1 - z)

    def own_layer(w, top):
        at = pl.ds(top, tile)
        colors, through = march(
            w, top, z, z * (bz + 1), bz - 1, own_ref, z, [zero] * 3, zero + 1.0
        )
        for c in range(3):
            back[w, c, at] = colors[c]
        back[w, 3, at] = through

    def near_layer(w, top):
        at = pl.ds(top, tile)
        colors, through = march(
            w, top, 1 - z, near, early, near_ref, 0, [zero] * 3, zero + 1.0
        )
        own_first, near_first = order[0, w] == z, z == 0
        edge_colors, edge_through = march(
            w, top, z, bz - 1 + z, 1, own_ref, (1 - z) * (bz - 1), [zero] * 3, zero + 1.0
        )
        inner_through = back[w, 3, at]
        own_through = inner_through * edge_through
        of_inner = jnp.where(near_first, 1.0, edge_through)
        of_edge = jnp.where(near_first, inner_through, 1.0)
        ahead = jnp.where(own_first, own_through, 1.0)
        after = jnp.where(near_first, 1.0, through)
        for c in range(3):
            own_color = of_inner * back[w, c, at] + of_edge * edge_colors[c]
            out_ref[w, c, at] = jnp.where(own_first, own_color, 0.0) + jnp.where(
                near_first, ahead * colors[c], 0.0
            )
            back[w, c, at] = jnp.where(near_first, 0.0, colors[c]) + jnp.where(
                own_first, 0.0, after * own_color
            )
        out_ref[w, 3, at] = ahead * jnp.where(near_first, through, 1.0)
        back[w, 3, at] = after * jnp.where(own_first, 1.0, own_through)

    def far_layer(w, top):
        at = pl.ds(top, tile)
        colors, through = march(
            w, top, 1 - z, far, 2, m_ref, 1 + far, [out_ref[w, c, at] for c in range(3)],
            out_ref[w, 3, at],
        )
        for c in range(3):
            out_ref[w, c, at] = colors[c] + through * back[w, c, at]
        out_ref[w, 3, at] = 1.0 - through * back[w, 3, at]

    def each(start, stop):
        lax.fori_loop(start, stop, slopes, 0)

    each(z * (bz + 1), z * (bz + 1) + bz - 1)
    views(own_layer)
    sided(middle)
    for k in range(2):
        slopes(bz - 1 + k, 0)
    sided(lambda mine: ending(mine, 1))
    slopes(bz + 1 - 3 * z, 0)
    views(near_layer)
    sided(lambda mine: ending(mine, 2))
    for k in range(2):
        slopes((1 - z) * (depth - 2) + k, 0)
    views(far_layer)
    sided(lambda mine: steps[mine][3]())


def two_bricks(mesh, pressure, light, palette, rate, shear, offset, order):
    bz, rows, cols = pressure.shape
    dims = (mesh.shape["gy"], mesh.shape["gx"], bz, rows)
    strip = rows // 2
    tall = HALO + strip + SUB
    depth = 2 * bz
    vmem = pl.BlockSpec(memory_space=pltpu.VMEM)
    hbm = pl.BlockSpec(memory_space=pltpu.HBM)
    f32 = jnp.float32
    _, sent, got = routes_of(dims)
    tables = (
        light,
        palette.T,
        rate,
        jnp.transpose(shear, (0, 2, 1)),
        jnp.transpose(offset, (1, 2, 0)),
        order.T,
    )
    image = pl.pallas_call(
        functools.partial(render, dims),
        out_shape=jax.ShapeDtypeStruct((VIEWS, 4, strip, LANES), f32),
        in_specs=[hbm] * 7,
        out_specs=vmem,
        scratch_shapes=[
            *[pltpu.SMEM(table.shape, table.dtype) for table in tables],
            pltpu.VMEM((bz, rows, LANES), f32),
            pltpu.VMEM((depth + 2, tall, LANES), f32),
            pltpu.VMEM((bz, tall, LANES), f32),
            pltpu.VMEM((bz - 2, tall, LANES), f32),
            pltpu.VMEM((2, got, LANES), f32),
            pltpu.VMEM((2, 2, SUB, LANES), f32),
            pltpu.VMEM((sent, LANES), f32),
            pltpu.VMEM((SUB, LANES), f32),
            pltpu.VMEM((depth + 2, tall, LANES), f32),
            pltpu.VMEM((2, tall, LANES), f32),
            pltpu.VMEM((VIEWS, depth, HALO + strip, LANES), f32),
            pltpu.VMEM((VIEWS, depth, HALO + strip, LANES), f32),
            pltpu.VMEM((VIEWS, 4, strip, LANES), f32),
            pltpu.SemaphoreType.DMA,
            pltpu.SemaphoreType.DMA((SLOTS,)),
            pltpu.SemaphoreType.REGULAR((3,)),
            pltpu.SemaphoreType.DMA((2,)),
            pltpu.SemaphoreType.DMA,
        ],
        compiler_params=pltpu.CompilerParams(collective_id=0, has_side_effects=True, vmem_limit_bytes=12 << 20),
        name="render",
    )(
        *[pltpu.with_memory_space_constraint(t, pltpu.HBM) for t in (*tables, pressure)]
    )
    return image[:, :, None]


def fits(mesh, shape):
    bz, rows, cols = shape
    return (
        mesh.shape["gz"] == 2
        and cols == LANES
        and rows % 64 == 0
        and 2 * HALO <= rows <= LANES
        and bz * (HALO - SUB) == LANES
        and bz * (rows // SUB) <= LANES
    )


def on_device(mesh, pressure, *rest):
    if fits(mesh, pressure.shape):
        return two_bricks(mesh, pressure, *rest)
    return many_bricks(pressure, *rest)


def solution(mesh):
    return jax.shard_map(
        functools.partial(on_device, mesh),
        mesh=mesh,
        in_specs=(P("gz", "gy", "gx"), P(), P(), P(), P(), P(), P()),
        out_specs=P(None, None, "gz", "gy", "gx"),
        check_vma=False,
    )
```
